32 devices in a mesh: trial: 16 (over z, y, x), factor: 2 (over core).
Axes of the slice: x: 2, y: 2, z: 4, core: 2. Of those that a mesh axis runs over, the one named last changes fastest.
Arguments:
- observed: float32 [64, 32, 128], P('trial'), may hold values from -6 to 6
- trial_mean: float32 [64], P('trial'), may hold values from -4 to 4
- correlations: float32 [64, 2], P('trial'), may hold values from 0.1 to 0.7
- noise_var: float32 [64], P('trial'), may hold values from 2 to 8
- plot_slot: int32 [64, 32, 128], P('trial'), may hold values from 0 to 2047
- row_count: int32 [64], P('trial'), may hold values from 8 to 32, as said below
- col_count: int32 [64], P('trial'), may hold values from 64 to 128, as said below
- panel_list: int32 [64, 16], P('trial'), may hold values from 0 to 191, as said below
- scores: bfloat16 [128, 24576], P('factor', 'trial'), may hold values from -0.5 to 0.5
- loadings: float32 [64, 128], P('trial', 'factor'), may hold values from -5 to 5
- score_precision: float32 [128], P('factor'), may hold values from 20 to 80
Outputs:
- score_gradient: float32 [128, 24576], P('factor', 'trial')
- loading_gradient: float32 [64, 128], P('trial', 'factor')
The draws below stay inside these ranges and needn't reach their ends.
Inputs may be any that keep to these rules, and one draw needn't show every extreme that they name: `panel_list`: panel p is owned by index p // 12 of trial. Among the 64 entries of each aligned block of 4 trials, no owner holds more than 8 of them, and in every block some owner holds exactly that many. Entries may repeat. `row_count`: the first trial uses all 32 rows. `col_count`: the first trial uses all 128 columns.
All inputs are finite; a program needn't handle non-finite values.
Results may differ from the reference program's by a relative error of at most 0.0023.
Values may be sent and summed in bfloat16 or wider, within the bound.
A program may use at most 64 MiB of HBM per device.

```python
import math
import jax
import jax.numpy as jnp
from jax import lax

K = 128
PANEL = 128
PT = 16
ROWS = 32
COLS = 128
TRIALS_DEV = 4
PANELS_DEV = 12
TRIALS = 64
PANELS = 192
GENOTYPES = 24576


def draw_row_count(key, part):
    lowest = max(2, ROWS // 4)
    values = jax.random.randint(jax.random.fold_in(key, 11), (TRIALS,), lowest, ROWS + 1)
    return values.at[0].set(ROWS).astype(jnp.int32)


def draw_col_count(key, part):
    lowest = max(2, COLS // 2)
    values = jax.random.randint(jax.random.fold_in(key, 12), (TRIALS,), lowest, COLS + 1)
    return values.at[0].set(COLS).astype(jnp.int32)


def draw_panel_list(key, part):
    owners_total = PANELS // PANELS_DEV
    required_count = TRIALS_DEV * PT
    most_count = 2 * required_count // owners_total
    quarter = owners_total // 4
    half_count = required_count // 2
    blocks = TRIALS // TRIALS_DEV

    def one_block(block_key):
        key_owner, key_sorted_order, key_local = jax.random.split(block_key, 3)
        shuffled = jax.random.permutation(key_owner, owners_total)
        places = jnp.arange(required_count)
        first_half = shuffled[jnp.minimum(places // most_count, owners_total - 1)]
        second_half = shuffled[quarter + (places - half_count) % (owners_total - quarter)]
        owner_ids = jnp.where(places < half_count, first_half, second_half)
        owner_ids = owner_ids[jax.random.permutation(key_sorted_order, required_count)]
        local_ids = jax.random.randint(key_local, (required_count,), 0, PANELS_DEV)
        return (owner_ids * PANELS_DEV + local_ids).reshape(TRIALS_DEV, PT)
    block_keys = jax.random.split(jax.random.fold_in(key, 7), blocks)
    return jax.vmap(one_block)(block_keys).reshape(TRIALS, PT).astype(jnp.int32)


def with_ends(values, own_key, low, largest):
    extent = values.shape
    index_at = [jax.random.randint(jax.random.fold_in(own_key, axis), (), 0, extent[axis]) for axis in range(len(extent))]
    values = values.at[tuple(index_at)].set(low)
    longest = extent.index(max(extent))
    index_at[longest] = (index_at[longest] + 1) % extent[longest]
    return values.at[tuple(index_at)].set(largest)


def levels(rng, dims, shards, least, largest):
    factor_of, own = 1.0, jax.random.fold_in(rng, 6)
    for dim, parts in shards:
        steps = jnp.exp(jax.random.uniform(jax.random.fold_in(own, dim), (parts,), jnp.float32, least / len(shards), largest / len(shards)))
        factor_of = factor_of * jnp.repeat(steps, dims[dim] // parts).reshape([-1 if axis == dim else 1 for axis in range(len(dims))])
    return factor_of


def scatter_about(stream_key, shape, spread, most, cuts=(), held_as=jnp.bfloat16):
    values = jax.random.normal(stream_key, shape, jnp.float32) * spread
    if len(cuts) > 0:
        values = levels(stream_key, shape, cuts, -0.22, 0.18) * values
    return jnp.clip(values, min=-most, max=most).astype(held_as)


def setup_inputs(seed: int = 0) -> dict:
    arg_keys = jax.random.split(jax.random.key(seed), 12)
    observed = scatter_about(arg_keys[0], (TRIALS, ROWS, COLS), 1.0, 6.0, ((0, 16),), jnp.float32)
    trial_mean = scatter_about(arg_keys[1], (TRIALS,), 1.0, 4.0, ((0, 16),), jnp.float32)
    correlations = jnp.clip(0.1 + 0.59999999 * jax.random.uniform(arg_keys[2], (TRIALS, 2), jnp.float32) ** levels(arg_keys[2], (TRIALS, 2), ((0, 16),), -0.2, 0.2), 0.1, 0.7)
    noise_var = jnp.clip(jnp.exp(math.log(8.0) - 1.3862944 * jax.random.uniform(arg_keys[3], (TRIALS,), jnp.float32) ** levels(arg_keys[3], (TRIALS,), ((0, 16),), -0.2, 0.2)), 2.0, 8.0)
    plot_slot = with_ends(jax.random.randint(arg_keys[4], (TRIALS, ROWS, COLS), 0, PT * PANEL), jax.random.fold_in(arg_keys[4], 1), 0, (PT * PANEL) - 1).astype(jnp.int32)
    row_count = draw_row_count(jax.random.fold_in(arg_keys[11], 71), 0)
    col_count = draw_col_count(jax.random.fold_in(arg_keys[11], 71), 0)
    panel_list = draw_panel_list(jax.random.fold_in(arg_keys[11], 71), 0)
    scores = scatter_about(arg_keys[8], (K, GENOTYPES), K ** -0.5, 0.5, ((0, 2), (1, 16)))
    loadings = scatter_about(arg_keys[9], (TRIALS, K), 1.0, 5.0, ((0, 16), (1, 2)), jnp.float32)
    score_precision = jnp.clip(jnp.exp(math.log(80.0) - 1.3862944 * jax.random.uniform(arg_keys[10], (K,), jnp.float32) ** levels(arg_keys[10], (K,), ((0, 2),), -0.2, 0.2)), 20.0, 80.0)
    return dict(observed=observed, trial_mean=trial_mean, correlations=correlations, noise_var=noise_var, plot_slot=plot_slot, row_count=row_count, col_count=col_count, panel_list=panel_list, scores=scores, loadings=loadings, score_precision=score_precision)


def sweep_axis(values_in, corr_value, position, limit_count, axis_number):
    factor_scale = 1.0 / (1.0 - corr_value * corr_value)
    interior = ((position > 0) & (position < limit_count - 1)).astype(values_in.dtype)
    padding = [(0, 0)] * values_in.ndim
    padding[axis_number] = (1, 1)
    padded = jnp.pad(values_in, padding)
    length = values_in.shape[axis_number]
    lower_side = lax.slice_in_dim(padded, 0, length, axis=axis_number)
    upper_side = lax.slice_in_dim(padded, 2, length + 2, axis=axis_number)
    result = factor_scale * ((1.0 + corr_value * corr_value * interior) * values_in - corr_value * (lower_side + upper_side))
    return jnp.where(position < limit_count, result, 0.0)


def evaluate(current, loads_all, observed, trial_mean, correlations, noise_var, plot_slot, row_count, col_count, panel_list, score_precision):
    grouped = current.reshape(K, PANELS, PANEL)
    row_index = lax.broadcasted_iota(jnp.int32, (ROWS, COLS), 0)
    col_index = lax.broadcasted_iota(jnp.int32, (ROWS, COLS), 1)

    def per_trial(accum, inputs):
        ids, loads_now, obs_grid, mean_value, corr_pair, noise_value, slot_grid, row_upper_limit, col_limit = inputs
        table = jnp.take(grouped, ids, axis=1).reshape(K, PT * PANEL).astype(jnp.float32)
        effect = jnp.dot(loads_now, table, precision=lax.Precision.HIGHEST)
        fitted = effect[slot_grid]
        active = (row_index < row_upper_limit) & (col_index < col_limit)
        residual = jnp.where(active, obs_grid - mean_value - fitted, 0.0)
        across = sweep_axis(residual, corr_pair[1], col_index, col_limit, 1)
        weighted = sweep_axis(across, corr_pair[0], row_index, row_upper_limit, 0) / noise_value
        slot_weight = jax.ops.segment_sum(weighted.reshape(-1), slot_grid.reshape(-1), num_segments=PT * PANEL)
        load_grad = -jnp.dot(table, slot_weight, precision=lax.Precision.HIGHEST)
        returned = -(loads_now[:, None] * slot_weight[None, :]).reshape(K, PT, PANEL)
        accum = accum.at[:, ids, :].add(returned)
        return accum, load_grad

    accum, load_grads = lax.scan(per_trial, jnp.zeros((K, PANELS, PANEL), jnp.float32),
                                 (panel_list, loads_all, observed, trial_mean, correlations, noise_var, plot_slot, row_count, col_count))
    score_grad = score_precision[:, None] * current.astype(jnp.float32) + accum.reshape(K, PANELS * PANEL)
    return score_grad, load_grads


def reference(observed, trial_mean, correlations, noise_var, plot_slot, row_count, col_count, panel_list, scores, loadings, score_precision):
    first_scores, first_loads = evaluate(scores, loadings, observed, trial_mean, correlations, noise_var, plot_slot, row_count, col_count, panel_list, score_precision)
    new_scores = (scores.astype(jnp.float32) - 0.005 * first_scores).astype(jnp.bfloat16)
    new_loads = loadings - 0.02 * first_loads
    return evaluate(new_scores, new_loads, observed, trial_mean, correlations, noise_var, plot_slot, row_count, col_count, panel_list, score_precision)
```

```python
import functools

import jax
import jax.numpy as jnp
from jax import lax
from jax.experimental import pallas as pl
from jax.experimental.pallas import tpu as pltpu
from jax.sharding import PartitionSpec as P

PANEL = 128
TILE = 8

score_step = 0.005
load_step = 0.02

MESH = pl.DeviceIdType.MESH
F32 = jnp.float32
BF16 = jnp.bfloat16
LEVELS = 32000.0


def halves(x):
    high = x.astype(BF16).astype(F32)
    return high, x - high


def dot(a, b):
    return lax.dot_general(a, b, (((1,), (0,)), ((), ())), preferred_element_type=F32)


def dot_nt(a, b):
    return lax.dot_general(a, b, (((1,), (1,)), ((), ())), preferred_element_type=F32)


def kernel(
    n_trial,
    n_factor,
    rank_tile,
    mean_hbm,
    corr_hbm,
    noise_hbm,
    rows_hbm,
    cols_hbm,
    list_hbm,
    precision_hbm,
    loads_hbm,
    scores_hbm,
    slot_hbm,
    observed_hbm,
    score_out,
    load_out,
    mean_ref,
    corr_ref,
    noise_ref,
    rows_ref,
    cols_ref,
    list_ref,
    precision_ref,
    loads_ref,
    scores_ref,
    slot_ref,
    observed_ref,
    sent,
    got,
    share,
    shares,
    scale,
    scales,
    fac_sent,
    fac_got,
    spread,
    cells,
    fresh,
    copy_sem,
    send_sem,
    recv_sem,
    fac_send_sem,
    fac_recv_sem,
):
    per_dev, grid_rows, grid_cols = observed_ref.shape
    factors = scores_ref.shape[0]
    owned = scores_ref.shape[1] // PANEL
    per_trial = list_ref.shape[1]
    required = per_dev * per_trial
    rows = n_trial * rank_tile
    trials = n_trial * per_dev
    me = lax.axis_index("trial")
    mine = lax.axis_index("factor")

    barrier = pltpu.get_barrier_semaphore()
    for step in range(1, n_trial):
        pl.semaphore_signal(
            barrier,
            inc=1,
            device_id={"trial": lax.rem(me + step, n_trial)},
            device_id_type=MESH,
        )
    for step in range(1, n_factor):
        pl.semaphore_signal(
            barrier,
            inc=1,
            device_id={"factor": lax.rem(mine + step, n_factor)},
            device_id_type=MESH,
        )

    pairs = (
        (list_hbm, list_ref),
        (loads_hbm, loads_ref),
        (slot_hbm, slot_ref),
        (scores_hbm, scores_ref),
        (observed_hbm, observed_ref),
        (precision_hbm, precision_ref),
        (mean_hbm, mean_ref),
        (corr_hbm, corr_ref),
        (noise_hbm, noise_ref),
        (rows_hbm, rows_ref),
        (cols_hbm, cols_ref),
    )
    copies = [
        pltpu.make_async_copy(source, target, copy_sem.at[index])
        for index, (source, target) in enumerate(pairs)
    ]
    for copy in copies:
        copy.start()

    def tile_at(index):
        return pl.ds(pl.multiple_of(index * rank_tile, rank_tile), rank_tile)

    def send(number):
        for step in sorted(range(1, n_trial), key=lambda at: -abs(2 * at - n_trial)):
            target = lax.rem(me + step, n_trial)
            pltpu.make_async_remote_copy(
                src_ref=sent.at[number, tile_at(target)],
                dst_ref=got.at[number, tile_at(me)],
                send_sem=send_sem.at[number],
                recv_sem=recv_sem.at[number],
                device_id={"trial": target},
                device_id_type=MESH,
            ).start()
        got[number, tile_at(me), :] = sent[number, tile_at(me), :]

    def others(number, ref, sem):
        part = ref.at[number, pl.ds(0, (n_trial - 1) * rank_tile)]
        return pltpu.make_async_copy(part, part, sem.at[number])

    def receive(number):
        others(number, got, recv_sem).wait()
        return got[number]

    def send_share():
        for step in range(1, n_trial):
            pltpu.make_async_remote_copy(
                src_ref=share,
                dst_ref=shares.at[me],
                send_sem=send_sem.at[6],
                recv_sem=recv_sem.at[6],
                device_id={"trial": lax.rem(me + step, n_trial)},
                device_id_type=MESH,
            ).start()
            pltpu.make_async_remote_copy(
                src_ref=scale.at[pl.ds(0, 1)],
                dst_ref=scales.at[pl.ds(me, 1)],
                send_sem=send_sem.at[7],
                recv_sem=recv_sem.at[7],
                device_id={"trial": lax.rem(me + step, n_trial)},
                device_id_type=MESH,
            ).start()
        shares[pl.ds(me, 1)] = share[...][None]
        scales[pl.ds(me, 1), :] = scale[0:1, :]

    def other_shares(sem):
        part = shares.at[pl.ds(0, n_trial - 1)]
        return pltpu.make_async_copy(part, part, sem.at[6])

    def other_scales(sem):
        part = scales.at[pl.ds(0, n_trial - 1)]
        return pltpu.make_async_copy(part, part, sem.at[7])

    def factor_sum(number, part):
        fac_sent[number] = part
        for step in range(1, n_factor):
            pltpu.make_async_remote_copy(
                src_ref=fac_sent.at[number],
                dst_ref=fac_got.at[number, mine],
                send_sem=fac_send_sem.at[number, step - 1],
                recv_sem=fac_recv_sem.at[number, step - 1],
                device_id={"factor": lax.rem(mine + step, n_factor)},
                device_id_type=MESH,
            ).start()
        fac_got[number, pl.ds(mine, 1)] = part[None]
        for step in range(1, n_factor):
            origin = lax.rem(mine + n_factor - step, n_factor)
            pltpu.make_async_copy(
                fac_sent.at[number], fac_got.at[number, origin], fac_recv_sem.at[number, step - 1]
            ).wait()
        total = fac_got[number, 0]
        for index in range(1, n_factor):
            total = total + fac_got[number, index]
        return total

    def column(line):
        size = line.shape[1]
        eye = lax.broadcasted_iota(jnp.int32, (size, size), 0) == lax.broadcasted_iota(
            jnp.int32, (size, size), 1
        )
        return jnp.sum(jnp.where(eye, line, 0.0), axis=1, keepdims=True)

    copies[0].wait()
    wanted = jnp.concatenate(
        [list_ref[trial : trial + 1, :] for trial in range(per_dev)], axis=1
    )
    owner = wanted // owned
    local = wanted - owner * owned
    owner_line = owner.astype(F32)
    before = lax.broadcasted_iota(jnp.int32, (required, required), 0)
    after = lax.broadcasted_iota(jnp.int32, (required, required), 1)
    earlier = (column(owner_line) == owner_line) & (before < after)
    rank = jnp.sum(jnp.where(earlier, 1.0, 0.0), axis=0, keepdims=True)
    place = owner_line * rank_tile + rank
    row_of = lax.broadcasted_iota(jnp.int32, (rows, required), 0).astype(F32)
    placed = place == row_of
    slot_trial = lax.broadcasted_iota(jnp.int32, (rows, required), 1) // per_trial
    trial_of = jnp.max(jnp.where(placed, slot_trial.astype(F32), -1.0), axis=1, keepdims=True)
    local_of = jnp.max(jnp.where(placed, local.astype(F32), -1.0), axis=1, keepdims=True)
    pack = jnp.where(placed, 1.0, 0.0)
    pack = jnp.concatenate([pack, pack], axis=1).astype(BF16)

    copies[1].wait()
    loads = loads_ref[...]
    load_rows = jnp.zeros((rows, factors), F32)
    for trial in range(per_dev):
        load_rows = jnp.where(trial_of == trial, loads[trial : trial + 1, :], load_rows)
    sent[0] = jnp.concatenate(
        [
            load_rows,
            jnp.broadcast_to(local_of, (rows, 8)),
            jnp.broadcast_to(trial_of, (rows, PANEL - factors - 8)),
        ],
        axis=1,
    )
    pl.semaphore_wait(barrier, n_trial - 1 + n_factor - 1)
    send(0)

    lane_rows = lax.broadcasted_iota(jnp.int32, (required, rows), 1).astype(F32)
    unpack = jnp.where(column(place) == lane_rows, 1.0, 0.0).astype(BF16)
    unpack = jnp.concatenate([unpack, unpack], axis=1)
    cell_iota = lax.broadcasted_iota(jnp.int32, (PANEL, grid_cols), 0)
    panel_iota = lax.broadcasted_iota(jnp.int32, (per_trial, grid_cols), 0)
    for copy in copies[2:]:
        copy.wait()
    precision = column(precision_ref[...])
    for trial in range(per_dev):
        cell = slot_ref[trial] & (PANEL - 1)
        for row in range(grid_rows):
            cells[trial, :, row * grid_cols : (row + 1) * grid_cols] = jnp.where(
                cell[row : row + 1, :] == cell_iota, 1.0, 0.0
            ).astype(BF16)

    row_index = lax.broadcasted_iota(jnp.int32, (grid_rows, grid_cols), 0)
    col_index = lax.broadcasted_iota(jnp.int32, (grid_rows, grid_cols), 1)

    def sweep(values, corr, position, limit, axis):
        length = values.shape[axis]
        scale = 1.0 / (1.0 - corr * corr)
        inner = jnp.where((position > 0) & (position < limit - 1), corr * corr, 0.0)
        lower = jnp.where(position == 0, 0.0, pltpu.roll(values, 1, axis))
        upper = jnp.where(position == length - 1, 0.0, pltpu.roll(values, length - 1, axis))
        result = scale * ((1.0 + inner) * values - corr * (lower + upper))
        return jnp.where(position < limit, result, 0.0)

    def over_grid(ref, row, lane):
        return jnp.broadcast_to(ref[row : row + 1, lane : lane + 1], (grid_rows, grid_cols))

    def plots(effect):
        totals = []
        for trial in range(per_dev):
            slot = slot_ref[trial]
            panel = slot // PANEL
            cell = slot & (PANEL - 1)
            fitted = jnp.zeros((grid_rows, grid_cols), F32)
            for index in range(per_trial):
                at = trial * per_trial + index
                line = jnp.broadcast_to(effect[at : at + 1, :], (grid_rows, PANEL))
                taken = jnp.take_along_axis(line, cell, axis=1)
                fitted = jnp.where(panel == index, taken, fitted)
            row_limit = over_grid(rows_ref, 0, trial)
            col_limit = over_grid(cols_ref, 0, trial)
            active = (row_index < row_limit) & (col_index < col_limit)
            residual = jnp.where(
                active, observed_ref[trial] - over_grid(mean_ref, 0, trial) - fitted, 0.0
            )
            across = sweep(residual, over_grid(corr_ref, 1, trial), col_index, col_limit, 1)
            weighted = sweep(across, over_grid(corr_ref, 0, trial), row_index, row_limit, 0)
            weighted = weighted / over_grid(noise_ref, 0, trial)
            high, low = halves(weighted)
            for row in range(grid_rows):
                match = panel[row : row + 1, :] == panel_iota
                where_to = slice(row * grid_cols, (row + 1) * grid_cols)
                spread[trial, 0:per_trial, where_to] = jnp.where(
                    match, high[row : row + 1, :], 0.0
                ).astype(BF16)
                spread[trial, per_trial : 2 * per_trial, where_to] = jnp.where(
                    match, low[row : row + 1, :], 0.0
                ).astype(BF16)
            both = dot_nt(spread[trial], cells[trial])
            totals.append(both[0:per_trial] + both[per_trial : 2 * per_trial])
        return jnp.concatenate(totals, axis=0)

    message = receive(0)
    first_loads = message[:, 0:factors]
    panel_of = message[:, factors : factors + 1]
    turned = message.T
    panel_lane = turned[factors : factors + 1, :]
    block_at = lax.broadcasted_iota(jnp.int32, (rows, 1), 0) // rank_tile * per_dev
    block_lane = lax.broadcasted_iota(jnp.int32, (1, rows), 1) // rank_tile * per_dev
    within = message[:, factors + 8 : factors + 9]
    within_lane = turned[factors + 8 : factors + 9, :]
    whose = jnp.where(within >= 0.0, within + block_at.astype(F32), -1.0)
    whose_lane = jnp.where(within_lane >= 0.0, within_lane + block_lane.astype(F32), -1.0)
    gather = whose == lax.broadcasted_iota(jnp.int32, (rows, trials), 1).astype(F32)
    gather = jnp.where(gather, 1.0, 0.0)
    gather = jnp.concatenate([gather, gather], axis=1).astype(BF16)
    collect = whose_lane == lax.broadcasted_iota(jnp.int32, (trials, rows), 0).astype(F32)
    collect = jnp.where(collect, 1.0, 0.0).astype(BF16)
    collect = jnp.concatenate([collect, collect], axis=1)

    def stacked(values):
        high, low = halves(values)
        return jnp.concatenate([high, low], axis=0).astype(BF16)

    def weigh(number, load_part, current_ref):
        load_high, load_low = halves(load_part)
        load_both = jnp.concatenate([load_high, load_low], axis=1).astype(BF16)
        effect = jnp.zeros((rows, PANEL), F32)
        for panel in range(owned):
            block = current_ref[:, panel * PANEL : (panel + 1) * PANEL]
            product = dot(load_both, jnp.concatenate([block, block], axis=0))
            effect = jnp.where(panel_of == panel, product, effect)
        sent[number] = effect
        send(number)
        table = dot(unpack, stacked(receive(number)))
        slot_weight = plots(factor_sum(0 if number == 1 else 1, table))
        sent[number + 1] = dot(pack, stacked(slot_weight))
        send(number + 1)
        return halves(receive(number + 1))

    def load_terms(high, low, current_ref):
        wide = jnp.concatenate([high, low], axis=1).astype(BF16)
        terms = jnp.zeros((rows, factors), F32)
        for panel in range(owned):
            block = current_ref[:, panel * PANEL : (panel + 1) * PANEL]
            product = dot_nt(wide, jnp.concatenate([block, block], axis=1))
            terms = jnp.where(panel_of == panel, product, terms)
        return terms

    def score_grads(high, low, load_lanes, current_ref):
        tall = jnp.concatenate([high, low, high], axis=0).astype(BF16)
        lane_high, lane_low = halves(load_lanes)
        for panel in range(owned):
            where_to = slice(panel * PANEL, (panel + 1) * PANEL)
            match = panel_lane == panel
            masked_high = jnp.where(match, lane_high, 0.0)
            masked_low = jnp.where(match, lane_low, 0.0)
            left = jnp.concatenate([masked_high, masked_high, masked_low], axis=1).astype(BF16)
            current = current_ref[:, where_to].astype(F32)
            yield where_to, current, precision * current - dot(left, tall)

    padding = jnp.zeros((rows, PANEL - factors), F32)
    high, low = weigh(1, first_loads, scores_ref)
    partial = dot(collect, stacked(load_terms(high, low, scores_ref)))
    groups = PANEL // factors
    depth = trials // groups
    packed = jnp.concatenate(
        [partial[index * depth : (index + 1) * depth] for index in range(groups)], axis=1
    )
    unit = jnp.max(jnp.abs(packed), axis=1, keepdims=True) * (1.0 / LEVELS) + 1e-30
    share[...] = jnp.floor(packed / unit + 0.5).astype(jnp.int32).astype(jnp.int16)
    square = jnp.concatenate(
        [jnp.broadcast_to(unit, (depth, PANEL)), jnp.zeros((PANEL - depth, PANEL), F32)], axis=0
    )
    scale[...] = square.T[0:TILE, :]
    send_share()
    for where_to, current, grad in score_grads(high, low, turned[0:factors, :], scores_ref):
        fresh[:, where_to] = (current - score_step * grad).astype(BF16)
    other_shares(recv_sem).wait()
    other_scales(recv_sem).wait()
    tall_scales = scales[...]
    if n_trial < PANEL:
        tall_scales = jnp.concatenate(
            [tall_scales, jnp.zeros((PANEL - n_trial, PANEL), F32)], axis=0
        )
    units = tall_scales.T[0:depth, :]
    summed = jnp.zeros((depth, PANEL), F32)
    for index in range(n_trial):
        whole = shares[index].astype(jnp.int32).astype(F32)
        summed = summed + whole * units[:, index : index + 1]
    gained = jnp.concatenate(
        [summed[:, index * factors : (index + 1) * factors] for index in range(groups)], axis=0
    )
    second_loads = first_loads + load_step * dot(gather, stacked(gained))
    high, low = weigh(3, second_loads, fresh)
    sent[5] = jnp.concatenate([load_terms(high, low, fresh), padding], axis=1)
    send(5)
    turned_loads = jnp.concatenate([second_loads, padding], axis=1).T[0:factors, :]
    for where_to, current, grad in score_grads(high, low, turned_loads, fresh):
        score_out[:, where_to] = grad
    back = receive(5)[:, 0:factors]
    for trial in range(per_dev):
        load_out[trial : trial + 1, :] = -jnp.sum(
            jnp.where(trial_of == trial, back, 0.0), axis=0, keepdims=True
        )

    for number in range(6):
        others(number, sent, send_sem).wait()
    other_shares(send_sem).wait()
    other_scales(send_sem).wait()
    for number in range(2):
        for step in range(1, n_factor):
            pltpu.make_async_copy(
                fac_sent.at[number], fac_sent.at[number], fac_send_sem.at[number, step - 1]
            ).wait()


def body(
    observed,
    trial_mean,
    correlations,
    noise_var,
    plot_slot,
    row_count,
    col_count,
    panel_list,
    scores,
    loadings,
    score_precision,
):
    n_trial = lax.axis_size("trial")
    n_factor = lax.axis_size("factor")
    per_dev, per_trial = panel_list.shape
    required = per_dev * per_trial
    most = 2 * required // n_trial
    rank_tile = -(-most // TILE) * TILE
    rows = n_trial * rank_tile
    factors = scores.shape[0]
    depth = n_trial * per_dev * factors // PANEL
    grid_size = plot_slot.shape[1] * plot_slot.shape[2]
    operands = (
        trial_mean[None],
        correlations.T,
        noise_var[None],
        row_count[None],
        col_count[None],
        panel_list,
        score_precision[None],
        loadings,
        scores,
        plot_slot,
        observed,
    )
    operands = tuple(pltpu.with_memory_space_constraint(x, pltpu.HBM) for x in operands)
    vmem = pl.BlockSpec(memory_space=pltpu.VMEM)
    hbm = pl.BlockSpec(memory_space=pltpu.HBM)
    return pl.pallas_call(
        functools.partial(kernel, n_trial, n_factor, rank_tile),
        out_shape=(
            jax.ShapeDtypeStruct(scores.shape, F32),
            jax.ShapeDtypeStruct(loadings.shape, F32),
        ),
        in_specs=[hbm] * len(operands),
        out_specs=(vmem, vmem),
        scratch_shapes=[pltpu.VMEM(operand.shape, operand.dtype) for operand in operands]
        + [
            pltpu.VMEM((6, rows, PANEL), F32),
            pltpu.VMEM((6, rows, PANEL), F32),
            pltpu.VMEM((depth, PANEL), jnp.int16),
            pltpu.VMEM((n_trial, depth, PANEL), jnp.int16),
            pltpu.VMEM((TILE, PANEL), F32),
            pltpu.VMEM((n_trial, PANEL), F32),
            pltpu.VMEM((2, required, PANEL), F32),
            pltpu.VMEM((2, n_factor, required, PANEL), F32),
            pltpu.VMEM((per_dev, 2 * per_trial, grid_size), BF16),
            pltpu.VMEM((per_dev, PANEL, grid_size), BF16),
            pltpu.VMEM(scores.shape, BF16),
            pltpu.SemaphoreType.DMA((len(operands),)),
            pltpu.SemaphoreType.DMA((8,)),
            pltpu.SemaphoreType.DMA((8,)),
            pltpu.SemaphoreType.DMA((2, max(n_factor - 1, 1))),
            pltpu.SemaphoreType.DMA((2, max(n_factor - 1, 1))),
        ],
        compiler_params=pltpu.CompilerParams(
            collective_id=0, has_side_effects=True, vmem_limit_bytes=48 * 1024 * 1024
        ),
    )(*operands)


def solution(mesh):
    in_specs = (
        P("trial", None, None),
        P("trial"),
        P("trial", None),
        P("trial"),
        P("trial", None, None),
        P("trial"),
        P("trial"),
        P("trial", None),
        P("factor", "trial"),
        P("trial", "factor"),
        P("factor"),
    )
    out_specs = (P("factor", "trial"), P("trial", "factor"))
    return jax.shard_map(body, mesh=mesh, in_specs=in_specs, out_specs=out_specs, check_vma=False)
```

```python
import functools

import jax
import jax.numpy as jnp
from jax import lax
from jax.experimental import pallas as pl
from jax.experimental.pallas import tpu as pltpu
from jax.sharding import PartitionSpec as P

PANEL = 128
TILE = 8

score_step = 0.005
load_step = 0.02

MESH = pl.DeviceIdType.MESH
F32 = jnp.float32
BF16 = jnp.bfloat16
LEVELS = 32000.0


def halves(x):
    high = x.astype(BF16).astype(F32)
    return high, x - high


def dot(a, b):
    return lax.dot_general(a, b, (((1,), (0,)), ((), ())), preferred_element_type=F32)


def dot_nt(a, b):
    return lax.dot_general(a, b, (((1,), (1,)), ((), ())), preferred_element_type=F32)


def split_kernel(
    n_trial,
    rank_tile,
    mean_hbm,
    corr_hbm,
    noise_hbm,
    rows_hbm,
    cols_hbm,
    list_hbm,
    precision_hbm,
    loads_hbm,
    scores_hbm,
    slot_hbm,
    observed_hbm,
    score_out,
    load_out,
    mean_ref,
    corr_ref,
    noise_ref,
    rows_ref,
    cols_ref,
    list_ref,
    precision_ref,
    loads_ref,
    scores_ref,
    slot_ref,
    observed_ref,
    sent,
    got,
    small_sent,
    small_got,
    share,
    shares,
    scale,
    scales,
    back_sent,
    back_got,
    turned_mine,
    turned_other,
    weights_other,
    spread,
    cells,
    coef,
    fresh,
    copy_sem,
    send_sem,
    recv_sem,
    pair_send_sem,
    pair_recv_sem,
):
    per_dev, per_trial = list_ref.shape
    half, grid_rows, grid_cols = observed_ref.shape
    factors = loads_ref.shape[1]
    owned = scores_ref.shape[2] // PANEL
    required = half * per_trial
    rows = n_trial * rank_tile
    trials = n_trial * half
    me = lax.axis_index("trial")
    mine = lax.axis_index("factor")
    other = 1 - mine

    def flip(steps):
        target = me
        for bit in range(n_trial.bit_length() - 1):
            if steps >> bit & 1:
                target = target + (1 << bit) * (1 - 2 * lax.rem(lax.div(me, 1 << bit), 2))
        return target

    if n_trial & (n_trial - 1) == 0:
        order = sorted(
            range(1, n_trial), key=lambda at: -((at >> 2) + (at & 1) + (at >> 1 & 1))
        )
        targets = [flip(at) for at in order]
    else:
        order = sorted(range(1, n_trial), key=lambda at: -abs(2 * at - n_trial))
        targets = [lax.rem(me + at, n_trial) for at in order]

    barrier = pltpu.get_barrier_semaphore()
    for target in targets:
        for core in (mine, other):
            pl.semaphore_signal(
                barrier,
                inc=1,
                device_id={"trial": target, "factor": core},
                device_id_type=MESH,
            )
    pl.semaphore_signal(
        barrier, inc=1, device_id={"trial": me, "factor": other}, device_id_type=MESH
    )

    own_trials = pl.ds(mine * half, half)
    pairs = (
        (list_hbm, list_ref),
        (loads_hbm, loads_ref),
        (slot_hbm.at[own_trials], slot_ref),
        (scores_hbm, scores_ref.at[0]),
        (observed_hbm.at[own_trials], observed_ref),
        (precision_hbm, precision_ref.at[0]),
        (mean_hbm, mean_ref),
        (corr_hbm, corr_ref),
        (noise_hbm, noise_ref),
        (rows_hbm, rows_ref),
        (cols_hbm, cols_ref),
    )
    copies = [
        pltpu.make_async_copy(source, target, copy_sem.at[index])
        for index, (source, target) in enumerate(pairs)
    ]
    for copy in copies:
        copy.start()

    def remote(source, target, send, recv, trial, core):
        pltpu.make_async_remote_copy(
            src_ref=source,
            dst_ref=target,
            send_sem=send,
            recv_sem=recv,
            device_id={"trial": trial, "factor": core},
            device_id_type=MESH,
        ).start()

    def tile_at(index):
        return pl.ds(pl.multiple_of(index * rank_tile, rank_tile), rank_tile)

    def send(number):
        for target in targets:
            remote(
                sent.at[number, tile_at(target)],
                got.at[number, tile_at(me)],
                send_sem.at[number],
                recv_sem.at[number],
                target,
                mine,
            )
        got[number, tile_at(me), :] = sent[number, tile_at(me), :]

    def wait_bytes(part, sem):
        pltpu.make_async_copy(part, part, sem).wait()

    def others(number, ref, sem):
        wait_bytes(ref.at[number, pl.ds(0, (n_trial - 1) * rank_tile)], sem.at[number])

    def receive(number):
        others(number, got, recv_sem)
        return got[number]

    def swap(number, source, target):
        remote(
            source, target, pair_send_sem.at[number], pair_recv_sem.at[number], me, other
        )

    def pick(first, second):
        return jnp.where(mine == 0, first, second)

    def column(line):
        size = line.shape[1]
        eye = lax.broadcasted_iota(jnp.int32, (size, size), 0) == lax.broadcasted_iota(
            jnp.int32, (size, size), 1
        )
        return jnp.sum(jnp.where(eye, line, 0.0), axis=1, keepdims=True)

    copies[0].wait()
    wanted = jnp.concatenate(
        [
            pick(list_ref[at : at + 1, :], list_ref[half + at : half + at + 1, :])
            for at in range(half)
        ],
        axis=1,
    )
    owner = wanted // owned
    local = wanted - owner * owned
    owner_line = owner.astype(F32)
    before = lax.broadcasted_iota(jnp.int32, (required, required), 0)
    after = lax.broadcasted_iota(jnp.int32, (required, required), 1)
    earlier = (column(owner_line) == owner_line) & (before < after)
    rank = jnp.sum(jnp.where(earlier, 1.0, 0.0), axis=0, keepdims=True)
    place = owner_line * rank_tile + rank
    row_of = lax.broadcasted_iota(jnp.int32, (rows, required), 0).astype(F32)
    placed = place == row_of
    slot_trial = lax.broadcasted_iota(jnp.int32, (rows, required), 1) // per_trial
    trial_of = jnp.max(jnp.where(placed, slot_trial.astype(F32), -1.0), axis=1, keepdims=True)
    local_of = jnp.max(jnp.where(placed, local.astype(F32), -1.0), axis=1, keepdims=True)

    copies[1].wait()
    loads = loads_ref[...]
    load_rows = jnp.zeros((rows, factors), F32)
    nothing = jnp.zeros((1, factors), F32)
    for at in range(half):
        low_line, high_line = loads[at : at + 1, :], loads[half + at : half + at + 1, :]
        load_rows = jnp.where(trial_of == at, pick(low_line, high_line), load_rows)
        small_sent[at : at + 1, :] = jnp.concatenate(
            [nothing, pick(high_line, low_line)], axis=1
        )
    sent[0] = jnp.concatenate(
        [
            load_rows,
            jnp.broadcast_to(local_of, (rows, 8)),
            jnp.broadcast_to(trial_of, (rows, PANEL - factors - 8)),
        ],
        axis=1,
    )
    pl.semaphore_wait(barrier, 2 * n_trial - 1)
    send(0)
    for target in targets + [me]:
        remote(
            small_sent.at[pl.ds(0, half)],
            small_got.at[me, pl.ds(0, half)],
            send_sem.at[6],
            recv_sem.at[6],
            target,
            other,
        )
    copies[3].wait()
    swap(0, scores_ref.at[0], scores_ref.at[1])
    copies[5].wait()
    swap(1, precision_ref.at[0], precision_ref.at[1])

    pack = jnp.where(placed, 1.0, 0.0)
    pack = jnp.concatenate([pack, pack], axis=1).astype(BF16)
    lane_rows = lax.broadcasted_iota(jnp.int32, (required, rows), 1).astype(F32)
    unpack = jnp.where(column(place) == lane_rows, 1.0, 0.0).astype(BF16)
    unpack = jnp.concatenate([unpack, unpack], axis=1)
    cell_iota = lax.broadcasted_iota(jnp.int32, (PANEL, grid_cols), 0)
    panel_iota = lax.broadcasted_iota(jnp.int32, (per_trial, grid_cols), 0)
    copies[2].wait()
    copies[4].wait()
    for copy in copies[6:]:
        copy.wait()
    for trial in range(half):
        cell = slot_ref[trial] & (PANEL - 1)
        for row in range(grid_rows):
            cells[trial, :, row * grid_cols : (row + 1) * grid_cols] = jnp.where(
                cell[row : row + 1, :] == cell_iota, 1.0, 0.0
            ).astype(BF16)

    row_index = lax.broadcasted_iota(jnp.int32, (grid_rows, grid_cols), 0)
    col_index = lax.broadcasted_iota(jnp.int32, (grid_rows, grid_cols), 1)

    def over_grid(ref, row, trial):
        value = pick(
            ref[row : row + 1, trial : trial + 1],
            ref[row : row + 1, half + trial : half + trial + 1],
        )
        return jnp.broadcast_to(value, (grid_rows, grid_cols))

    def stencil(corr, position, limit, length, weight):
        scale = weight / (1.0 - corr * corr)
        inner = jnp.where((position > 0) & (position < limit - 1), corr * corr, 0.0)
        inside = position < limit
        middle = jnp.where(inside, scale * (1.0 + inner), 0.0)
        side = jnp.where(inside, scale * corr, 0.0)
        lower = jnp.where(position == 0, 0.0, side)
        upper = jnp.where(position == length - 1, 0.0, side)
        return middle, lower, upper

    for trial in range(half):
        row_limit = over_grid(rows_ref, 0, trial)
        col_limit = over_grid(cols_ref, 0, trial)
        active = (row_index < row_limit) & (col_index < col_limit)
        base = jnp.where(active, observed_ref[trial] - over_grid(mean_ref, 0, trial), 0.0)
        across = stencil(over_grid(corr_ref, 1, trial), col_index, col_limit, grid_cols, 1.0)
        down = stencil(
            over_grid(corr_ref, 0, trial),
            row_index,
            row_limit,
            grid_rows,
            1.0 / over_grid(noise_ref, 0, trial),
        )
        for index, value in enumerate(
            (jnp.where(active, 1.0, 0.0), base) + across + down
        ):
            coef[trial, index] = value

    def plots(effect):
        totals = []
        for trial in range(half):
            slot = slot_ref[trial]
            panel = slot // PANEL
            cell = slot & (PANEL - 1)
            fitted = jnp.zeros((grid_rows, grid_cols), F32)
            for index in range(per_trial):
                at = trial * per_trial + index
                line = jnp.broadcast_to(effect[at : at + 1, :], (grid_rows, PANEL))
                taken = jnp.take_along_axis(line, cell, axis=1)
                fitted = jnp.where(panel == index, taken, fitted)
            residual = coef[trial, 1] - coef[trial, 0] * fitted
            across = (
                coef[trial, 2] * residual
                - coef[trial, 3] * pltpu.roll(residual, 1, 1)
                - coef[trial, 4] * pltpu.roll(residual, grid_cols - 1, 1)
            )
            weighted = (
                coef[trial, 5] * across
                - coef[trial, 6] * pltpu.roll(across, 1, 0)
                - coef[trial, 7] * pltpu.roll(across, grid_rows - 1, 0)
            )
            high, low = halves(weighted)
            for row in range(grid_rows):
                match = panel[row : row + 1, :] == panel_iota
                where_to = slice(row * grid_cols, (row + 1) * grid_cols)
                spread[trial, 0:per_trial, where_to] = jnp.where(
                    match, high[row : row + 1, :], 0.0
                ).astype(BF16)
                spread[trial, per_trial : 2 * per_trial, where_to] = jnp.where(
                    match, low[row : row + 1, :], 0.0
                ).astype(BF16)
            both = dot_nt(spread[trial], cells[trial])
            totals.append(both[0:per_trial] + both[per_trial : 2 * per_trial])
        return jnp.concatenate(totals, axis=0)

    def stacked(values):
        high, low = halves(values)
        return jnp.concatenate([high, low], axis=0).astype(BF16)

    def side_by_side(high, low):
        return jnp.concatenate([high, low], axis=1).astype(BF16)

    def effects(load_part, panel_wide, current_ref):
        load_both = side_by_side(*halves(load_part))
        effect = jnp.zeros((rows, PANEL), F32)
        for panel in range(owned):
            where_to = slice(panel * PANEL, (panel + 1) * PANEL)
            block = jnp.concatenate(
                [current_ref[0, :, where_to], current_ref[1, :, where_to]], axis=0
            )
            product = dot(load_both, jnp.concatenate([block, block], axis=0))
            effect = jnp.where(panel_wide == panel, product, effect)
        return effect

    def load_terms(high, low, panel_wide, current_ref):
        wide = side_by_side(high, low)
        terms = jnp.zeros((rows, PANEL), F32)
        for panel in range(owned):
            where_to = slice(panel * PANEL, (panel + 1) * PANEL)
            block = jnp.concatenate(
                [current_ref[0, :, where_to], current_ref[1, :, where_to]], axis=0
            )
            product = dot_nt(wide, jnp.concatenate([block, block], axis=1))
            terms = jnp.where(panel_wide == panel, product, terms)
        return terms

    def masked(panels, load_lanes, panel):
        lane_high, lane_low = load_lanes
        match = panels == panel
        masked_high = jnp.where(match, lane_high, 0.0)
        return [masked_high, masked_high, jnp.where(match, lane_low, 0.0)]

    others(0, got, recv_sem)
    wait_bytes(small_got.at[:, pl.ds(0, half)], recv_sem.at[6])
    message = got[0]
    panel_of = message[:, factors : factors + 1]
    within = message[:, factors + 8 : factors + 9]
    panel_wide = jnp.broadcast_to(panel_of, (rows, PANEL))
    within_wide = jnp.broadcast_to(within, (rows, PANEL))
    first_loads = message
    lane = lax.broadcasted_iota(jnp.int32, (rows, PANEL), 1)
    for at in range(half):
        line = jnp.concatenate(
            [
                jnp.broadcast_to(small_got[source, at : at + 1, :], (rank_tile, PANEL))
                for source in range(n_trial)
            ],
            axis=0,
        )
        use = lane >= factors
        if at > 0:
            use = use & (within_wide == at)
        first_loads = jnp.where(use, line, first_loads)
    wait_bytes(scores_ref.at[1], pair_recv_sem.at[0])
    sent[1] = effects(first_loads, panel_wide, scores_ref)
    send(1)

    panel_lane = message.T[factors : factors + 1, :]
    turned = first_loads.T
    turned_mine[0, 0:PANEL, :] = turned
    turned_mine[0, PANEL : PANEL + TILE, :] = jnp.broadcast_to(panel_lane, (TILE, rows))
    swap(2, turned_mine.at[0], turned_other.at[0])
    block_at = lax.broadcasted_iota(jnp.int32, (rows, 1), 0) // rank_tile * half
    whose = jnp.where(within >= 0.0, within + block_at.astype(F32), -1.0)
    gather = whose == lax.broadcasted_iota(jnp.int32, (rows, trials), 1).astype(F32)
    gather = jnp.where(gather, 1.0, 0.0).astype(BF16)
    gather = jnp.concatenate([gather, gather], axis=1)
    within_lane = message.T[factors + 8 : factors + 9, :]
    source_lane = lax.broadcasted_iota(jnp.int32, (1, rows), 1) // rank_tile

    def collector(count, step):
        held = source_lane.astype(F32) * step + within_lane
        held = jnp.where(within_lane >= 0.0, held, -1.0)
        match = held == lax.broadcasted_iota(jnp.int32, (count, rows), 0).astype(F32)
        match = jnp.where(match, 1.0, 0.0).astype(BF16)
        return jnp.concatenate([match, match], axis=1)

    collect = collector(trials, half)
    collect_back = collector(n_trial * TILE, TILE)

    table = dot(unpack, stacked(receive(1)))
    sent[2] = dot(pack, stacked(plots(table)))
    send(2)

    high, low = halves(receive(2))
    swap(3, got.at[2], weights_other.at[0])
    partial = dot(collect, stacked(load_terms(high, low, panel_wide, scores_ref)))
    unit = jnp.max(jnp.abs(partial), axis=0, keepdims=True) * (1.0 / LEVELS) + 1e-30
    scale[0:1, :] = unit
    share[...] = jnp.floor(partial * (1.0 / unit) + 0.5).astype(jnp.int32).astype(jnp.int16)
    for target in targets:
        remote(share, shares.at[me], send_sem.at[5], recv_sem.at[5], target, mine)
        remote(
            scale.at[pl.ds(0, 1)],
            scales.at[pl.ds(me, 1)],
            send_sem.at[9],
            recv_sem.at[9],
            target,
            mine,
        )
    shares[pl.ds(me, 1)] = share[...][None]
    scales[pl.ds(me, 1), :] = unit

    wait_bytes(precision_ref.at[1], pair_recv_sem.at[1])
    wait_bytes(turned_other.at[0], pair_recv_sem.at[2])
    wait_bytes(weights_other.at[0], pair_recv_sem.at[3])
    precision = [column(precision_ref[0]), column(precision_ref[1])]
    other_panels = turned_other[0, PANEL : PANEL + 1, :]

    def tall(high, low, number):
        high_other, low_other = halves(weights_other[number])
        return jnp.concatenate(
            [high, low, high, high_other, low_other, high_other], axis=0
        ).astype(BF16)

    stack = tall(high, low, 0)
    for part in range(2):
        lanes = halves(turned[part * factors : (part + 1) * factors, :])
        start = (1 - part) * factors
        lanes_other = halves(turned_other[0, start : start + factors, :])
        for panel in range(owned):
            where_to = slice(panel * PANEL, (panel + 1) * PANEL)
            left = masked(panel_lane, lanes, panel) + masked(other_panels, lanes_other, panel)
            left = jnp.concatenate(left, axis=1).astype(BF16)
            current = scores_ref[part, :, where_to].astype(F32)
            grad = precision[part] * current - dot(left, stack)
            fresh[part, :, where_to] = (current - score_step * grad).astype(BF16)

    wait_bytes(shares.at[pl.ds(0, n_trial - 1)], recv_sem.at[5])
    wait_bytes(scales.at[pl.ds(0, n_trial - 1)], recv_sem.at[9])
    summed = jnp.zeros((trials, PANEL), F32)
    for source in range(n_trial):
        whole = shares[source].astype(jnp.int32).astype(F32)
        summed = summed + whole * scales[source : source + 1, :]
    second_loads = first_loads + load_step * dot(gather, stacked(summed))
    sent[3] = effects(second_loads, panel_wide, fresh)
    send(3)
    turned = second_loads.T
    turned_mine[1, 0:PANEL, :] = turned
    swap(4, turned_mine.at[1, pl.ds(0, PANEL)], turned_other.at[1, pl.ds(0, PANEL)])

    table = dot(unpack, stacked(receive(3)))
    sent[4] = dot(pack, stacked(plots(table)))
    send(4)

    high, low = halves(receive(4))
    swap(5, got.at[4], weights_other.at[1])
    back_sent[...] = dot(collect_back, stacked(load_terms(high, low, panel_wide, fresh)))

    def back_at(index):
        return pl.ds(pl.multiple_of(index * TILE, TILE), half)

    for target in targets:
        for side, core in enumerate((mine, other)):
            remote(
                back_sent.at[back_at(target)],
                back_got.at[side, back_at(me)],
                send_sem.at[7 + side],
                recv_sem.at[7 + side],
                target,
                core,
            )
    remote(
        back_sent.at[back_at(me)],
        back_got.at[1, back_at(me)],
        send_sem.at[8],
        recv_sem.at[8],
        me,
        other,
    )
    whole_tile = pl.ds(pl.multiple_of(me * TILE, TILE), TILE)
    back_got[0, whole_tile, :] = back_sent[whole_tile, :]

    wait_bytes(turned_other.at[1, pl.ds(0, PANEL)], pair_recv_sem.at[4])
    wait_bytes(weights_other.at[1], pair_recv_sem.at[5])
    stack = tall(high, low, 1)
    lanes = halves(turned[0:factors, :])
    lanes_other = halves(turned_other[1, factors : 2 * factors, :])
    for panel in range(owned):
        where_to = slice(panel * PANEL, (panel + 1) * PANEL)
        left = masked(panel_lane, lanes, panel) + masked(other_panels, lanes_other, panel)
        left = jnp.concatenate(left, axis=1).astype(BF16)
        current = fresh[0, :, where_to].astype(F32)
        score_out[:, where_to] = precision[0] * current - dot(left, stack)

    sizes = ((n_trial - 1) * half, n_trial * half)
    for side in range(2):
        wait_bytes(back_got.at[side, pl.ds(0, sizes[side])], recv_sem.at[7 + side])
    sums = []
    for side in range(2):
        total = back_got[side, 0:half, :]
        for source in range(1, n_trial):
            total = total + back_got[side, source * TILE : source * TILE + half, :]
        sums.append(total[:, side * factors : (side + 1) * factors])
    load_out[0:half, :] = -pick(sums[0], sums[1])
    load_out[half:per_dev, :] = -pick(sums[1], sums[0])

    for number in range(5):
        others(number, sent, send_sem)
    wait_bytes(shares.at[pl.ds(0, n_trial - 1)], send_sem.at[5])
    wait_bytes(scales.at[pl.ds(0, n_trial - 1)], send_sem.at[9])
    wait_bytes(small_got.at[:, pl.ds(0, half)], send_sem.at[6])
    for side in range(2):
        wait_bytes(back_got.at[side, pl.ds(0, sizes[side])], send_sem.at[7 + side])
    swapped = (
        scores_ref.at[0],
        precision_ref.at[0],
        turned_mine.at[0],
        got.at[2],
        turned_mine.at[1, pl.ds(0, PANEL)],
        got.at[4],
    )
    for number, part in enumerate(swapped):
        wait_bytes(part, pair_send_sem.at[number])


def split_call(n_trial, rank_tile, operands):
    mean, corr, noise, row_limits, col_limits, listed, precision, loads, scores, slots, seen = (
        operands
    )
    per_dev, per_trial = listed.shape
    half = per_dev // 2
    rows = n_trial * rank_tile
    grid = slots.shape[1:]
    grid_size = grid[0] * grid[1]
    vmem = pl.BlockSpec(memory_space=pltpu.VMEM)
    hbm = pl.BlockSpec(memory_space=pltpu.HBM)
    whole = (mean, corr, noise, row_limits, col_limits, listed)
    return pl.pallas_call(
        functools.partial(split_kernel, n_trial, rank_tile),
        out_shape=(
            jax.ShapeDtypeStruct(scores.shape, F32),
            jax.ShapeDtypeStruct(loads.shape, F32),
        ),
        in_specs=[hbm] * len(operands),
        out_specs=(vmem, vmem),
        scratch_shapes=[pltpu.VMEM(operand.shape, operand.dtype) for operand in whole]
        + [
            pltpu.VMEM((2,) + precision.shape, F32),
            pltpu.VMEM(loads.shape, F32),
            pltpu.VMEM((2,) + scores.shape, BF16),
            pltpu.VMEM((half,) + grid, jnp.int32),
            pltpu.VMEM((half,) + grid, F32),
            pltpu.VMEM((5, rows, PANEL), F32),
            pltpu.VMEM((5, rows, PANEL), F32),
            pltpu.VMEM((TILE, PANEL), F32),
            pltpu.VMEM((n_trial, TILE, PANEL), F32),
            pltpu.VMEM((n_trial * half, PANEL), jnp.int16),
            pltpu.VMEM((n_trial, n_trial * half, PANEL), jnp.int16),
            pltpu.VMEM((TILE, PANEL), F32),
            pltpu.VMEM((n_trial, PANEL), F32),
            pltpu.VMEM((n_trial * TILE, PANEL), F32),
            pltpu.VMEM((2, n_trial * TILE, PANEL), F32),
            pltpu.VMEM((2, PANEL + TILE, rows), F32),
            pltpu.VMEM((2, PANEL + TILE, rows), F32),
            pltpu.VMEM((2, rows, PANEL), F32),
            pltpu.VMEM((half, 2 * per_trial, grid_size), BF16),
            pltpu.VMEM((half, PANEL, grid_size), BF16),
            pltpu.VMEM((half, 8) + grid, F32),
            pltpu.VMEM((2,) + scores.shape, BF16),
            pltpu.SemaphoreType.DMA((len(operands),)),
            pltpu.SemaphoreType.DMA((10,)),
            pltpu.SemaphoreType.DMA((10,)),
            pltpu.SemaphoreType.DMA((6,)),
            pltpu.SemaphoreType.DMA((6,)),
        ],
        compiler_params=pltpu.CompilerParams(
            collective_id=0, has_side_effects=True, vmem_limit_bytes=48 * 1024 * 1024
        ),
    )(*operands)


def kernel(
    n_trial,
    n_factor,
    rank_tile,
    mean_hbm,
    corr_hbm,
    noise_hbm,
    rows_hbm,
    cols_hbm,
    list_hbm,
    precision_hbm,
    loads_hbm,
    scores_hbm,
    slot_hbm,
    observed_hbm,
    score_out,
    load_out,
    mean_ref,
    corr_ref,
    noise_ref,
    rows_ref,
    cols_ref,
    list_ref,
    precision_ref,
    loads_ref,
    scores_ref,
    slot_ref,
    observed_ref,
    sent,
    got,
    share,
    shares,
    scale,
    scales,
    fac_sent,
    fac_got,
    spread,
    cells,
    fresh,
    copy_sem,
    send_sem,
    recv_sem,
    fac_send_sem,
    fac_recv_sem,
):
    per_dev, grid_rows, grid_cols = observed_ref.shape
    factors = scores_ref.shape[0]
    owned = scores_ref.shape[1] // PANEL
    per_trial = list_ref.shape[1]
    required = per_dev * per_trial
    rows = n_trial * rank_tile
    trials = n_trial * per_dev
    me = lax.axis_index("trial")
    mine = lax.axis_index("factor")

    barrier = pltpu.get_barrier_semaphore()
    for step in range(1, n_trial):
        pl.semaphore_signal(
            barrier,
            inc=1,
            device_id={"trial": lax.rem(me + step, n_trial)},
            device_id_type=MESH,
        )
    for step in range(1, n_factor):
        pl.semaphore_signal(
            barrier,
            inc=1,
            device_id={"factor": lax.rem(mine + step, n_factor)},
            device_id_type=MESH,
        )

    pairs = (
        (list_hbm, list_ref),
        (loads_hbm, loads_ref),
        (slot_hbm, slot_ref),
        (scores_hbm, scores_ref),
        (observed_hbm, observed_ref),
        (precision_hbm, precision_ref),
        (mean_hbm, mean_ref),
        (corr_hbm, corr_ref),
        (noise_hbm, noise_ref),
        (rows_hbm, rows_ref),
        (cols_hbm, cols_ref),
    )
    copies = [
        pltpu.make_async_copy(source, target, copy_sem.at[index])
        for index, (source, target) in enumerate(pairs)
    ]
    for copy in copies:
        copy.start()

    def tile_at(index):
        return pl.ds(pl.multiple_of(index * rank_tile, rank_tile), rank_tile)

    def send(number):
        for step in sorted(range(1, n_trial), key=lambda at: -abs(2 * at - n_trial)):
            target = lax.rem(me + step, n_trial)
            pltpu.make_async_remote_copy(
                src_ref=sent.at[number, tile_at(target)],
                dst_ref=got.at[number, tile_at(me)],
                send_sem=send_sem.at[number],
                recv_sem=recv_sem.at[number],
                device_id={"trial": target},
                device_id_type=MESH,
            ).start()
        got[number, tile_at(me), :] = sent[number, tile_at(me), :]

    def others(number, ref, sem):
        part = ref.at[number, pl.ds(0, (n_trial - 1) * rank_tile)]
        return pltpu.make_async_copy(part, part, sem.at[number])

    def receive(number):
        others(number, got, recv_sem).wait()
        return got[number]

    def send_share():
        for step in range(1, n_trial):
            pltpu.make_async_remote_copy(
                src_ref=share,
                dst_ref=shares.at[me],
                send_sem=send_sem.at[6],
                recv_sem=recv_sem.at[6],
                device_id={"trial": lax.rem(me + step, n_trial)},
                device_id_type=MESH,
            ).start()
            pltpu.make_async_remote_copy(
                src_ref=scale.at[pl.ds(0, 1)],
                dst_ref=scales.at[pl.ds(me, 1)],
                send_sem=send_sem.at[7],
                recv_sem=recv_sem.at[7],
                device_id={"trial": lax.rem(me + step, n_trial)},
                device_id_type=MESH,
            ).start()
        shares[pl.ds(me, 1)] = share[...][None]
        scales[pl.ds(me, 1), :] = scale[0:1, :]

    def other_shares(sem):
        part = shares.at[pl.ds(0, n_trial - 1)]
        return pltpu.make_async_copy(part, part, sem.at[6])

    def other_scales(sem):
        part = scales.at[pl.ds(0, n_trial - 1)]
        return pltpu.make_async_copy(part, part, sem.at[7])

    def factor_sum(number, part):
        fac_sent[number] = part
        for step in range(1, n_factor):
            pltpu.make_async_remote_copy(
                src_ref=fac_sent.at[number],
                dst_ref=fac_got.at[number, mine],
                send_sem=fac_send_sem.at[number, step - 1],
                recv_sem=fac_recv_sem.at[number, step - 1],
                device_id={"factor": lax.rem(mine + step, n_factor)},
                device_id_type=MESH,
            ).start()
        fac_got[number, pl.ds(mine, 1)] = part[None]
        for step in range(1, n_factor):
            origin = lax.rem(mine + n_factor - step, n_factor)
            pltpu.make_async_copy(
                fac_sent.at[number], fac_got.at[number, origin], fac_recv_sem.at[number, step - 1]
            ).wait()
        total = fac_got[number, 0]
        for index in range(1, n_factor):
            total = total + fac_got[number, index]
        return total

    def column(line):
        size = line.shape[1]
        eye = lax.broadcasted_iota(jnp.int32, (size, size), 0) == lax.broadcasted_iota(
            jnp.int32, (size, size), 1
        )
        return jnp.sum(jnp.where(eye, line, 0.0), axis=1, keepdims=True)

    copies[0].wait()
    wanted = jnp.concatenate(
        [list_ref[trial : trial + 1, :] for trial in range(per_dev)], axis=1
    )
    owner = wanted // owned
    local = wanted - owner * owned
    owner_line = owner.astype(F32)
    before = lax.broadcasted_iota(jnp.int32, (required, required), 0)
    after = lax.broadcasted_iota(jnp.int32, (required, required), 1)
    earlier = (column(owner_line) == owner_line) & (before < after)
    rank = jnp.sum(jnp.where(earlier, 1.0, 0.0), axis=0, keepdims=True)
    place = owner_line * rank_tile + rank
    row_of = lax.broadcasted_iota(jnp.int32, (rows, required), 0).astype(F32)
    placed = place == row_of
    slot_trial = lax.broadcasted_iota(jnp.int32, (rows, required), 1) // per_trial
    trial_of = jnp.max(jnp.where(placed, slot_trial.astype(F32), -1.0), axis=1, keepdims=True)
    local_of = jnp.max(jnp.where(placed, local.astype(F32), -1.0), axis=1, keepdims=True)
    pack = jnp.where(placed, 1.0, 0.0)
    pack = jnp.concatenate([pack, pack], axis=1).astype(BF16)

    copies[1].wait()
    loads = loads_ref[...]
    load_rows = jnp.zeros((rows, factors), F32)
    for trial in range(per_dev):
        load_rows = jnp.where(trial_of == trial, loads[trial : trial + 1, :], load_rows)
    sent[0] = jnp.concatenate(
        [
            load_rows,
            jnp.broadcast_to(local_of, (rows, 8)),
            jnp.broadcast_to(trial_of, (rows, PANEL - factors - 8)),
        ],
        axis=1,
    )
    pl.semaphore_wait(barrier, n_trial - 1 + n_factor - 1)
    send(0)

    lane_rows = lax.broadcasted_iota(jnp.int32, (required, rows), 1).astype(F32)
    unpack = jnp.where(column(place) == lane_rows, 1.0, 0.0).astype(BF16)
    unpack = jnp.concatenate([unpack, unpack], axis=1)
    cell_iota = lax.broadcasted_iota(jnp.int32, (PANEL, grid_cols), 0)
    panel_iota = lax.broadcasted_iota(jnp.int32, (per_trial, grid_cols), 0)
    for copy in copies[2:]:
        copy.wait()
    precision = column(precision_ref[...])
    for trial in range(per_dev):
        cell = slot_ref[trial] & (PANEL - 1)
        for row in range(grid_rows):
            cells[trial, :, row * grid_cols : (row + 1) * grid_cols] = jnp.where(
                cell[row : row + 1, :] == cell_iota, 1.0, 0.0
            ).astype(BF16)

    row_index = lax.broadcasted_iota(jnp.int32, (grid_rows, grid_cols), 0)
    col_index = lax.broadcasted_iota(jnp.int32, (grid_rows, grid_cols), 1)

    def sweep(values, corr, position, limit, axis):
        length = values.shape[axis]
        scale = 1.0 / (1.0 - corr * corr)
        inner = jnp.where((position > 0) & (position < limit - 1), corr * corr, 0.0)
        lower = jnp.where(position == 0, 0.0, pltpu.roll(values, 1, axis))
        upper = jnp.where(position == length - 1, 0.0, pltpu.roll(values, length - 1, axis))
        result = scale * ((1.0 + inner) * values - corr * (lower + upper))
        return jnp.where(position < limit, result, 0.0)

    def over_grid(ref, row, lane):
        return jnp.broadcast_to(ref[row : row + 1, lane : lane + 1], (grid_rows, grid_cols))

    def plots(effect):
        totals = []
        for trial in range(per_dev):
            slot = slot_ref[trial]
            panel = slot // PANEL
            cell = slot & (PANEL - 1)
            fitted = jnp.zeros((grid_rows, grid_cols), F32)
            for index in range(per_trial):
                at = trial * per_trial + index
                line = jnp.broadcast_to(effect[at : at + 1, :], (grid_rows, PANEL))
                taken = jnp.take_along_axis(line, cell, axis=1)
                fitted = jnp.where(panel == index, taken, fitted)
            row_limit = over_grid(rows_ref, 0, trial)
            col_limit = over_grid(cols_ref, 0, trial)
            active = (row_index < row_limit) & (col_index < col_limit)
            residual = jnp.where(
                active, observed_ref[trial] - over_grid(mean_ref, 0, trial) - fitted, 0.0
            )
            across = sweep(residual, over_grid(corr_ref, 1, trial), col_index, col_limit, 1)
            weighted = sweep(across, over_grid(corr_ref, 0, trial), row_index, row_limit, 0)
            weighted = weighted / over_grid(noise_ref, 0, trial)
            high, low = halves(weighted)
            for row in range(grid_rows):
                match = panel[row : row + 1, :] == panel_iota
                where_to = slice(row * grid_cols, (row + 1) * grid_cols)
                spread[trial, 0:per_trial, where_to] = jnp.where(
                    match, high[row : row + 1, :], 0.0
                ).astype(BF16)
                spread[trial, per_trial : 2 * per_trial, where_to] = jnp.where(
                    match, low[row : row + 1, :], 0.0
                ).astype(BF16)
            both = dot_nt(spread[trial], cells[trial])
            totals.append(both[0:per_trial] + both[per_trial : 2 * per_trial])
        return jnp.concatenate(totals, axis=0)

    message = receive(0)
    first_loads = message[:, 0:factors]
    panel_of = message[:, factors : factors + 1]
    turned = message.T
    panel_lane = turned[factors : factors + 1, :]
    block_at = lax.broadcasted_iota(jnp.int32, (rows, 1), 0) // rank_tile * per_dev
    block_lane = lax.broadcasted_iota(jnp.int32, (1, rows), 1) // rank_tile * per_dev
    within = message[:, factors + 8 : factors + 9]
    within_lane = turned[factors + 8 : factors + 9, :]
    whose = jnp.where(within >= 0.0, within + block_at.astype(F32), -1.0)
    whose_lane = jnp.where(within_lane >= 0.0, within_lane + block_lane.astype(F32), -1.0)
    gather = whose == lax.broadcasted_iota(jnp.int32, (rows, trials), 1).astype(F32)
    gather = jnp.where(gather, 1.0, 0.0)
    gather = jnp.concatenate([gather, gather], axis=1).astype(BF16)
    collect = whose_lane == lax.broadcasted_iota(jnp.int32, (trials, rows), 0).astype(F32)
    collect = jnp.where(collect, 1.0, 0.0).astype(BF16)
    collect = jnp.concatenate([collect, collect], axis=1)

    def stacked(values):
        high, low = halves(values)
        return jnp.concatenate([high, low], axis=0).astype(BF16)

    def weigh(number, load_part, current_ref):
        load_high, load_low = halves(load_part)
        load_both = jnp.concatenate([load_high, load_low], axis=1).astype(BF16)
        effect = jnp.zeros((rows, PANEL), F32)
        for panel in range(owned):
            block = current_ref[:, panel * PANEL : (panel + 1) * PANEL]
            product = dot(load_both, jnp.concatenate([block, block], axis=0))
            effect = jnp.where(panel_of == panel, product, effect)
        sent[number] = effect
        send(number)
        table = dot(unpack, stacked(receive(number)))
        slot_weight = plots(factor_sum(0 if number == 1 else 1, table))
        sent[number + 1] = dot(pack, stacked(slot_weight))
        send(number + 1)
        return halves(receive(number + 1))

    def load_terms(high, low, current_ref):
        wide = jnp.concatenate([high, low], axis=1).astype(BF16)
        terms = jnp.zeros((rows, factors), F32)
        for panel in range(owned):
            block = current_ref[:, panel * PANEL : (panel + 1) * PANEL]
            product = dot_nt(wide, jnp.concatenate([block, block], axis=1))
            terms = jnp.where(panel_of == panel, product, terms)
        return terms

    def score_grads(high, low, load_lanes, current_ref):
        tall = jnp.concatenate([high, low, high], axis=0).astype(BF16)
        lane_high, lane_low = halves(load_lanes)
        for panel in range(owned):
            where_to = slice(panel * PANEL, (panel + 1) * PANEL)
            match = panel_lane == panel
            masked_high = jnp.where(match, lane_high, 0.0)
            masked_low = jnp.where(match, lane_low, 0.0)
            left = jnp.concatenate([masked_high, masked_high, masked_low], axis=1).astype(BF16)
            current = current_ref[:, where_to].astype(F32)
            yield where_to, current, precision * current - dot(left, tall)

    padding = jnp.zeros((rows, PANEL - factors), F32)
    high, low = weigh(1, first_loads, scores_ref)
    partial = dot(collect, stacked(load_terms(high, low, scores_ref)))
    groups = PANEL // factors
    depth = trials // groups
    packed = jnp.concatenate(
        [partial[index * depth : (index + 1) * depth] for index in range(groups)], axis=1
    )
    unit = jnp.max(jnp.abs(packed), axis=1, keepdims=True) * (1.0 / LEVELS) + 1e-30
    share[...] = jnp.floor(packed / unit + 0.5).astype(jnp.int32).astype(jnp.int16)
    square = jnp.concatenate(
        [jnp.broadcast_to(unit, (depth, PANEL)), jnp.zeros((PANEL - depth, PANEL), F32)], axis=0
    )
    scale[...] = square.T[0:TILE, :]
    send_share()
    for where_to, current, grad in score_grads(high, low, turned[0:factors, :], scores_ref):
        fresh[:, where_to] = (current - score_step * grad).astype(BF16)
    other_shares(recv_sem).wait()
    other_scales(recv_sem).wait()
    tall_scales = scales[...]
    if n_trial < PANEL:
        tall_scales = jnp.concatenate(
            [tall_scales, jnp.zeros((PANEL - n_trial, PANEL), F32)], axis=0
        )
    units = tall_scales.T[0:depth, :]
    summed = jnp.zeros((depth, PANEL), F32)
    for index in range(n_trial):
        whole = shares[index].astype(jnp.int32).astype(F32)
        summed = summed + whole * units[:, index : index + 1]
    gained = jnp.concatenate(
        [summed[:, index * factors : (index + 1) * factors] for index in range(groups)], axis=0
    )
    second_loads = first_loads + load_step * dot(gather, stacked(gained))
    high, low = weigh(3, second_loads, fresh)
    sent[5] = jnp.concatenate([load_terms(high, low, fresh), padding], axis=1)
    send(5)
    turned_loads = jnp.concatenate([second_loads, padding], axis=1).T[0:factors, :]
    for where_to, current, grad in score_grads(high, low, turned_loads, fresh):
        score_out[:, where_to] = grad
    back = receive(5)[:, 0:factors]
    for trial in range(per_dev):
        load_out[trial : trial + 1, :] = -jnp.sum(
            jnp.where(trial_of == trial, back, 0.0), axis=0, keepdims=True
        )

    for number in range(6):
        others(number, sent, send_sem).wait()
    other_shares(send_sem).wait()
    other_scales(send_sem).wait()
    for number in range(2):
        for step in range(1, n_factor):
            pltpu.make_async_copy(
                fac_sent.at[number], fac_sent.at[number], fac_send_sem.at[number, step - 1]
            ).wait()


def body(
    observed,
    trial_mean,
    correlations,
    noise_var,
    plot_slot,
    row_count,
    col_count,
    panel_list,
    scores,
    loadings,
    score_precision,
):
    n_trial = lax.axis_size("trial")
    n_factor = lax.axis_size("factor")
    per_dev, per_trial = panel_list.shape
    required = per_dev * per_trial
    most = 2 * required // n_trial
    rank_tile = -(-most // TILE) * TILE
    rows = n_trial * rank_tile
    factors = scores.shape[0]
    depth = n_trial * per_dev * factors // PANEL
    split = n_factor == 2 and per_dev % 2 == 0 and 2 * factors == PANEL
    grid_size = plot_slot.shape[1] * plot_slot.shape[2]
    operands = (
        trial_mean[None],
        correlations.T,
        noise_var[None],
        row_count[None],
        col_count[None],
        panel_list,
        score_precision[None],
        loadings,
        scores,
        plot_slot,
        observed,
    )
    operands = tuple(pltpu.with_memory_space_constraint(x, pltpu.HBM) for x in operands)
    vmem = pl.BlockSpec(memory_space=pltpu.VMEM)
    hbm = pl.BlockSpec(memory_space=pltpu.HBM)
    if split:
        return split_call(n_trial, rank_tile, operands)
    return pl.pallas_call(
        functools.partial(kernel, n_trial, n_factor, rank_tile),
        out_shape=(
            jax.ShapeDtypeStruct(scores.shape, F32),
            jax.ShapeDtypeStruct(loadings.shape, F32),
        ),
        in_specs=[hbm] * len(operands),
        out_specs=(vmem, vmem),
        scratch_shapes=[pltpu.VMEM(operand.shape, operand.dtype) for operand in operands]
        + [
            pltpu.VMEM((6, rows, PANEL), F32),
            pltpu.VMEM((6, rows, PANEL), F32),
            pltpu.VMEM((depth, PANEL), jnp.int16),
            pltpu.VMEM((n_trial, depth, PANEL), jnp.int16),
            pltpu.VMEM((TILE, PANEL), F32),
            pltpu.VMEM((n_trial, PANEL), F32),
            pltpu.VMEM((2, required, PANEL), F32),
            pltpu.VMEM((2, n_factor, required, PANEL), F32),
            pltpu.VMEM((per_dev, 2 * per_trial, grid_size), BF16),
            pltpu.VMEM((per_dev, PANEL, grid_size), BF16),
            pltpu.VMEM(scores.shape, BF16),
            pltpu.SemaphoreType.DMA((len(operands),)),
            pltpu.SemaphoreType.DMA((8,)),
            pltpu.SemaphoreType.DMA((8,)),
            pltpu.SemaphoreType.DMA((2, max(n_factor - 1, 1))),
            pltpu.SemaphoreType.DMA((2, max(n_factor - 1, 1))),
        ],
        compiler_params=pltpu.CompilerParams(
            collective_id=0, has_side_effects=True, vmem_limit_bytes=48 * 1024 * 1024
        ),
    )(*operands)


def solution(mesh):
    in_specs = (
        P("trial", None, None),
        P("trial"),
        P("trial", None),
        P("trial"),
        P("trial", None, None),
        P("trial"),
        P("trial"),
        P("trial", None),
        P("factor", "trial"),
        P("trial", "factor"),
        P("factor"),
    )
    out_specs = (P("factor", "trial"), P("trial", "factor"))
    return jax.shard_map(body, mesh=mesh, in_specs=in_specs, out_specs=out_specs, check_vma=False)
```

```python
import functools

import jax
import jax.numpy as jnp
from jax import lax
from jax.experimental import pallas as pl
from jax.experimental.pallas import tpu as pltpu
from jax.sharding import PartitionSpec as P

PANEL = 128
TILE = 8

score_step = 0.005
load_step = 0.02

MESH = pl.DeviceIdType.MESH
F32 = jnp.float32
BF16 = jnp.bfloat16
LEVELS = 32000.0


def halves(x):
    high = x.astype(BF16).astype(F32)
    return high, x - high


def dot(a, b):
    return lax.dot_general(a, b, (((1,), (0,)), ((), ())), preferred_element_type=F32)


def dot_nt(a, b):
    return lax.dot_general(a, b, (((1,), (1,)), ((), ())), preferred_element_type=F32)


def split_kernel(
    n_trial,
    rank_tile,
    mean_hbm,
    corr_hbm,
    noise_hbm,
    rows_hbm,
    cols_hbm,
    list_hbm,
    precision_hbm,
    loads_hbm,
    scores_hbm,
    slot_hbm,
    observed_hbm,
    score_out,
    load_out,
    mean_ref,
    corr_ref,
    noise_ref,
    rows_ref,
    cols_ref,
    list_ref,
    precision_ref,
    loads_ref,
    scores_ref,
    slot_ref,
    observed_ref,
    sent,
    got,
    small_sent,
    small_got,
    share,
    shares,
    scale,
    scales,
    back_sent,
    back_got,
    turned_mine,
    turned_other,
    weights_other,
    spread,
    cells,
    coef,
    fresh,
    copy_sem,
    send_sem,
    recv_sem,
    pair_send_sem,
    pair_recv_sem,
):
    per_dev, per_trial = list_ref.shape
    half, grid_rows, grid_cols = observed_ref.shape
    factors = loads_ref.shape[1]
    owned = scores_ref.shape[2] // PANEL
    required = half * per_trial
    rows = n_trial * rank_tile
    trials = n_trial * half
    me = lax.axis_index("trial")
    mine = lax.axis_index("factor")
    other = 1 - mine

    def flip(steps):
        target = me
        for bit in range(n_trial.bit_length() - 1):
            if steps >> bit & 1:
                target = target + (1 << bit) * (1 - 2 * lax.rem(lax.div(me, 1 << bit), 2))
        return target

    if n_trial & (n_trial - 1) == 0:
        order = sorted(
            range(1, n_trial), key=lambda at: -((at >> 2) + (at & 1) + (at >> 1 & 1))
        )
        targets = [flip(at) for at in order]
    else:
        order = sorted(range(1, n_trial), key=lambda at: -abs(2 * at - n_trial))
        targets = [lax.rem(me + at, n_trial) for at in order]

    barrier = pltpu.get_barrier_semaphore()
    for target in targets:
        for core in (mine, other):
            pl.semaphore_signal(
                barrier,
                inc=1,
                device_id={"trial": target, "factor": core},
                device_id_type=MESH,
            )
    pl.semaphore_signal(
        barrier, inc=1, device_id={"trial": me, "factor": other}, device_id_type=MESH
    )

    own_trials = pl.ds(mine * half, half)
    pairs = (
        (list_hbm, list_ref),
        (loads_hbm, loads_ref),
        (slot_hbm.at[own_trials], slot_ref),
        (scores_hbm, scores_ref.at[0]),
        (observed_hbm.at[own_trials], observed_ref),
        (precision_hbm, precision_ref.at[0]),
        (mean_hbm, mean_ref),
        (corr_hbm, corr_ref),
        (noise_hbm, noise_ref),
        (rows_hbm, rows_ref),
        (cols_hbm, cols_ref),
    )
    copies = [
        pltpu.make_async_copy(source, target, copy_sem.at[index])
        for index, (source, target) in enumerate(pairs)
    ]
    for copy in copies:
        copy.start()

    def remote(source, target, send, recv, trial, core):
        pltpu.make_async_remote_copy(
            src_ref=source,
            dst_ref=target,
            send_sem=send,
            recv_sem=recv,
            device_id={"trial": trial, "factor": core},
            device_id_type=MESH,
        ).start()

    def tile_at(index):
        return pl.ds(pl.multiple_of(index * rank_tile, rank_tile), rank_tile)

    def send(number):
        for target in targets:
            remote(
                sent.at[number, tile_at(target)],
                got.at[number, tile_at(me)],
                send_sem.at[number],
                recv_sem.at[number],
                target,
                mine,
            )
        got[number, tile_at(me), :] = sent[number, tile_at(me), :]

    def wait_bytes(part, sem):
        pltpu.make_async_copy(part, part, sem).wait()

    def others(number, ref, sem):
        wait_bytes(ref.at[number, pl.ds(0, (n_trial - 1) * rank_tile)], sem.at[number])

    def receive(number):
        others(number, got, recv_sem)
        return got[number]

    def swap(number, source, target):
        remote(
            source, target, pair_send_sem.at[number], pair_recv_sem.at[number], me, other
        )

    def pick(first, second):
        return jnp.where(mine == 0, first, second)

    def column(line):
        size = line.shape[1]
        eye = lax.broadcasted_iota(jnp.int32, (size, size), 0) == lax.broadcasted_iota(
            jnp.int32, (size, size), 1
        )
        return jnp.sum(jnp.where(eye, line, 0.0), axis=1, keepdims=True)

    copies[0].wait()
    wanted = jnp.concatenate(
        [
            pick(list_ref[at : at + 1, :], list_ref[half + at : half + at + 1, :])
            for at in range(half)
        ],
        axis=1,
    )
    owner = wanted // owned
    local = wanted - owner * owned
    owner_line = owner.astype(F32)
    before = lax.broadcasted_iota(jnp.int32, (required, required), 0)
    after = lax.broadcasted_iota(jnp.int32, (required, required), 1)
    earlier = (column(owner_line) == owner_line) & (before < after)
    rank = jnp.sum(jnp.where(earlier, 1.0, 0.0), axis=0, keepdims=True)
    place = owner_line * rank_tile + rank
    row_of = lax.broadcasted_iota(jnp.int32, (rows, required), 0).astype(F32)
    placed = place == row_of
    slot_trial = lax.broadcasted_iota(jnp.int32, (rows, required), 1) // per_trial
    trial_of = jnp.max(jnp.where(placed, slot_trial.astype(F32), -1.0), axis=1, keepdims=True)
    local_of = jnp.max(jnp.where(placed, local.astype(F32), -1.0), axis=1, keepdims=True)

    copies[1].wait()
    loads = loads_ref[...]
    load_rows = jnp.zeros((rows, factors), F32)
    nothing = jnp.zeros((1, factors), F32)
    for at in range(half):
        low_line, high_line = loads[at : at + 1, :], loads[half + at : half + at + 1, :]
        load_rows = jnp.where(trial_of == at, pick(low_line, high_line), load_rows)
        small_sent[at : at + 1, :] = jnp.concatenate(
            [nothing, pick(high_line, low_line)], axis=1
        )
    sent[0] = jnp.concatenate(
        [
            load_rows,
            jnp.broadcast_to(local_of, (rows, 8)),
            jnp.broadcast_to(trial_of, (rows, PANEL - factors - 8)),
        ],
        axis=1,
    )
    pl.semaphore_wait(barrier, 2 * n_trial - 1)
    send(0)
    for target in targets + [me]:
        remote(
            small_sent.at[pl.ds(0, half)],
            small_got.at[me, pl.ds(0, half)],
            send_sem.at[6],
            recv_sem.at[6],
            target,
            other,
        )
    copies[3].wait()
    swap(0, scores_ref.at[0], scores_ref.at[1])
    copies[5].wait()
    swap(1, precision_ref.at[0], precision_ref.at[1])

    pack = jnp.where(placed, 1.0, 0.0)
    pack = jnp.concatenate([pack, pack], axis=1).astype(BF16)
    lane_rows = lax.broadcasted_iota(jnp.int32, (required, rows), 1).astype(F32)
    unpack = jnp.where(column(place) == lane_rows, 1.0, 0.0).astype(BF16)
    unpack = jnp.concatenate([unpack, unpack], axis=1)
    cell_iota = lax.broadcasted_iota(jnp.int32, (PANEL, grid_cols), 0)
    panel_iota = lax.broadcasted_iota(jnp.int32, (per_trial, grid_cols), 0)
    copies[2].wait()
    copies[4].wait()
    for copy in copies[6:]:
        copy.wait()
    for trial in range(half):
        cell = slot_ref[trial] & (PANEL - 1)
        for row in range(grid_rows):
            match = jnp.where(cell[row : row + 1, :] == cell_iota, 1.0, 0.0)
            cells[trial, row * grid_cols : (row + 1) * grid_cols, :] = match.T.astype(BF16)

    row_index = lax.broadcasted_iota(jnp.int32, (grid_rows, grid_cols), 0)
    col_index = lax.broadcasted_iota(jnp.int32, (grid_rows, grid_cols), 1)

    def over_grid(ref, row, trial):
        value = pick(
            ref[row : row + 1, trial : trial + 1],
            ref[row : row + 1, half + trial : half + trial + 1],
        )
        return jnp.broadcast_to(value, (grid_rows, grid_cols))

    def stencil(corr, position, limit, length, weight):
        scale = weight / (1.0 - corr * corr)
        inner = jnp.where((position > 0) & (position < limit - 1), corr * corr, 0.0)
        inside = position < limit
        middle = jnp.where(inside, scale * (1.0 + inner), 0.0)
        side = jnp.where(inside, scale * corr, 0.0)
        lower = jnp.where(position == 0, 0.0, side)
        upper = jnp.where(position == length - 1, 0.0, side)
        return middle, lower, upper

    for trial in range(half):
        row_limit = over_grid(rows_ref, 0, trial)
        col_limit = over_grid(cols_ref, 0, trial)
        active = (row_index < row_limit) & (col_index < col_limit)
        base = jnp.where(active, observed_ref[trial] - over_grid(mean_ref, 0, trial), 0.0)
        across = stencil(over_grid(corr_ref, 1, trial), col_index, col_limit, grid_cols, 1.0)
        down = stencil(
            over_grid(corr_ref, 0, trial),
            row_index,
            row_limit,
            grid_rows,
            1.0 / over_grid(noise_ref, 0, trial),
        )
        for index, value in enumerate(
            (jnp.where(active, 1.0, 0.0), base) + across + down
        ):
            coef[trial, index] = value

    def plots(effect):
        totals = []
        for trial in range(half):
            slot = slot_ref[trial]
            panel = slot // PANEL
            cell = slot & (PANEL - 1)
            fitted = jnp.zeros((grid_rows, grid_cols), F32)
            for index in range(per_trial):
                at = trial * per_trial + index
                line = jnp.broadcast_to(effect[at : at + 1, :], (grid_rows, PANEL))
                taken = jnp.take_along_axis(line, cell, axis=1)
                fitted = jnp.where(panel == index, taken, fitted)
            residual = coef[trial, 1] - coef[trial, 0] * fitted
            across = (
                coef[trial, 2] * residual
                - coef[trial, 3] * pltpu.roll(residual, 1, 1)
                - coef[trial, 4] * pltpu.roll(residual, grid_cols - 1, 1)
            )
            weighted = (
                coef[trial, 5] * across
                - coef[trial, 6] * pltpu.roll(across, 1, 0)
                - coef[trial, 7] * pltpu.roll(across, grid_rows - 1, 0)
            )
            high, low = halves(weighted)
            for row in range(grid_rows):
                match = panel[row : row + 1, :] == panel_iota
                where_to = slice(row * grid_cols, (row + 1) * grid_cols)
                spread[trial, 0:per_trial, where_to] = jnp.where(
                    match, high[row : row + 1, :], 0.0
                ).astype(BF16)
                spread[trial, per_trial : 2 * per_trial, where_to] = jnp.where(
                    match, low[row : row + 1, :], 0.0
                ).astype(BF16)
            both = dot(spread[trial], cells[trial])
            totals.append(both[0:per_trial] + both[per_trial : 2 * per_trial])
        return jnp.concatenate(totals, axis=0)

    def stacked(values):
        high, low = halves(values)
        return jnp.concatenate([high, low], axis=0).astype(BF16)

    def side_by_side(high, low):
        return jnp.concatenate([high, low], axis=1).astype(BF16)

    def effects(load_part, panel_wide, current_ref):
        load_both = side_by_side(*halves(load_part))
        effect = jnp.zeros((rows, PANEL), F32)
        for panel in range(owned):
            where_to = slice(panel * PANEL, (panel + 1) * PANEL)
            block = jnp.concatenate(
                [current_ref[0, :, where_to], current_ref[1, :, where_to]], axis=0
            )
            product = dot(load_both, jnp.concatenate([block, block], axis=0))
            effect = jnp.where(panel_wide == panel, product, effect)
        return effect

    def load_terms(high, low, panel_wide, current_ref):
        wide = side_by_side(high, low)
        terms = jnp.zeros((rows, PANEL), F32)
        for panel in range(owned):
            where_to = slice(panel * PANEL, (panel + 1) * PANEL)
            block = jnp.concatenate(
                [current_ref[0, :, where_to], current_ref[1, :, where_to]], axis=0
            )
            product = dot_nt(wide, jnp.concatenate([block, block], axis=1))
            terms = jnp.where(panel_wide == panel, product, terms)
        return terms

    def masked(panels, load_lanes, panel):
        lane_high, lane_low = load_lanes
        match = panels == panel
        masked_high = jnp.where(match, lane_high, 0.0)
        return [masked_high, masked_high, jnp.where(match, lane_low, 0.0)]

    others(0, got, recv_sem)
    wait_bytes(small_got.at[:, pl.ds(0, half)], recv_sem.at[6])
    message = got[0]
    panel_of = message[:, factors : factors + 1]
    within = message[:, factors + 8 : factors + 9]
    panel_wide = jnp.broadcast_to(panel_of, (rows, PANEL))
    within_wide = jnp.broadcast_to(within, (rows, PANEL))
    first_loads = message
    lane = lax.broadcasted_iota(jnp.int32, (rows, PANEL), 1)
    for at in range(half):
        line = jnp.concatenate(
            [
                jnp.broadcast_to(small_got[source, at : at + 1, :], (rank_tile, PANEL))
                for source in range(n_trial)
            ],
            axis=0,
        )
        use = lane >= factors
        if at > 0:
            use = use & (within_wide == at)
        first_loads = jnp.where(use, line, first_loads)
    wait_bytes(scores_ref.at[1], pair_recv_sem.at[0])
    sent[1] = effects(first_loads, panel_wide, scores_ref)
    send(1)

    panel_lane = message.T[factors : factors + 1, :]
    turned = first_loads.T
    turned_mine[0, 0:PANEL, :] = turned
    turned_mine[0, PANEL : PANEL + TILE, :] = jnp.broadcast_to(panel_lane, (TILE, rows))
    swap(2, turned_mine.at[0], turned_other.at[0])
    block_at = lax.broadcasted_iota(jnp.int32, (rows, 1), 0) // rank_tile * half
    whose = jnp.where(within >= 0.0, within + block_at.astype(F32), -1.0)
    gather = whose == lax.broadcasted_iota(jnp.int32, (rows, trials), 1).astype(F32)
    gather = jnp.where(gather, 1.0, 0.0).astype(BF16)
    gather = jnp.concatenate([gather, gather], axis=1)
    within_lane = message.T[factors + 8 : factors + 9, :]
    source_lane = lax.broadcasted_iota(jnp.int32, (1, rows), 1) // rank_tile

    def collector(count, step):
        held = source_lane.astype(F32) * step + within_lane
        held = jnp.where(within_lane >= 0.0, held, -1.0)
        match = held == lax.broadcasted_iota(jnp.int32, (count, rows), 0).astype(F32)
        match = jnp.where(match, 1.0, 0.0).astype(BF16)
        return jnp.concatenate([match, match], axis=1)

    collect = collector(trials, half)
    collect_back = collector(n_trial * TILE, TILE)

    table = dot(unpack, stacked(receive(1)))
    sent[2] = dot(pack, stacked(plots(table)))
    send(2)

    high, low = halves(receive(2))
    swap(3, got.at[2], weights_other.at[0])
    partial = dot(collect, stacked(load_terms(high, low, panel_wide, scores_ref)))
    unit = jnp.max(jnp.abs(partial), axis=0, keepdims=True) * (1.0 / LEVELS) + 1e-30
    scale[0:1, :] = unit
    share[...] = jnp.floor(partial * (1.0 / unit) + 0.5).astype(jnp.int32).astype(jnp.int16)
    for target in targets:
        remote(share, shares.at[me], send_sem.at[5], recv_sem.at[5], target, mine)
        remote(
            scale.at[pl.ds(0, 1)],
            scales.at[pl.ds(me, 1)],
            send_sem.at[9],
            recv_sem.at[9],
            target,
            mine,
        )
    shares[pl.ds(me, 1)] = share[...][None]
    scales[pl.ds(me, 1), :] = unit

    wait_bytes(precision_ref.at[1], pair_recv_sem.at[1])
    wait_bytes(turned_other.at[0], pair_recv_sem.at[2])
    wait_bytes(weights_other.at[0], pair_recv_sem.at[3])
    precision = [column(precision_ref[0]), column(precision_ref[1])]
    other_panels = turned_other[0, PANEL : PANEL + 1, :]

    def tall(high, low, number):
        high_other, low_other = halves(weights_other[number])
        return jnp.concatenate(
            [high, low, high, high_other, low_other, high_other], axis=0
        ).astype(BF16)

    stack = tall(high, low, 0)
    for part in range(2):
        lanes = halves(turned[part * factors : (part + 1) * factors, :])
        start = (1 - part) * factors
        lanes_other = halves(turned_other[0, start : start + factors, :])
        for panel in range(owned):
            where_to = slice(panel * PANEL, (panel + 1) * PANEL)
            left = masked(panel_lane, lanes, panel) + masked(other_panels, lanes_other, panel)
            left = jnp.concatenate(left, axis=1).astype(BF16)
            current = scores_ref[part, :, where_to].astype(F32)
            grad = precision[part] * current - dot(left, stack)
            fresh[part, :, where_to] = (current - score_step * grad).astype(BF16)

    wait_bytes(shares.at[pl.ds(0, n_trial - 1)], recv_sem.at[5])
    wait_bytes(scales.at[pl.ds(0, n_trial - 1)], recv_sem.at[9])
    summed = jnp.zeros((trials, PANEL), F32)
    for source in range(n_trial):
        whole = shares[source].astype(jnp.int32).astype(F32)
        summed = summed + whole * scales[source : source + 1, :]
    second_loads = first_loads + load_step * dot(gather, stacked(summed))
    sent[3] = effects(second_loads, panel_wide, fresh)
    send(3)
    turned = second_loads.T
    turned_mine[1, 0:PANEL, :] = turned
    swap(4, turned_mine.at[1, pl.ds(0, PANEL)], turned_other.at[1, pl.ds(0, PANEL)])

    table = dot(unpack, stacked(receive(3)))
    sent[4] = dot(pack, stacked(plots(table)))
    send(4)

    high, low = halves(receive(4))
    swap(5, got.at[4], weights_other.at[1])
    back_sent[...] = dot(collect_back, stacked(load_terms(high, low, panel_wide, fresh)))

    def back_at(index):
        return pl.ds(pl.multiple_of(index * TILE, TILE), half)

    for target in targets:
        for side, core in enumerate((mine, other)):
            remote(
                back_sent.at[back_at(target)],
                back_got.at[side, back_at(me)],
                send_sem.at[7 + side],
                recv_sem.at[7 + side],
                target,
                core,
            )
    remote(
        back_sent.at[back_at(me)],
        back_got.at[1, back_at(me)],
        send_sem.at[8],
        recv_sem.at[8],
        me,
        other,
    )
    whole_tile = pl.ds(pl.multiple_of(me * TILE, TILE), TILE)
    back_got[0, whole_tile, :] = back_sent[whole_tile, :]

    wait_bytes(turned_other.at[1, pl.ds(0, PANEL)], pair_recv_sem.at[4])
    wait_bytes(weights_other.at[1], pair_recv_sem.at[5])
    stack = tall(high, low, 1)
    lanes = halves(turned[0:factors, :])
    lanes_other = halves(turned_other[1, factors : 2 * factors, :])
    for panel in range(owned):
        where_to = slice(panel * PANEL, (panel + 1) * PANEL)
        left = masked(panel_lane, lanes, panel) + masked(other_panels, lanes_other, panel)
        left = jnp.concatenate(left, axis=1).astype(BF16)
        current = fresh[0, :, where_to].astype(F32)
        score_out[:, where_to] = precision[0] * current - dot(left, stack)

    sizes = ((n_trial - 1) * half, n_trial * half)
    for side in range(2):
        wait_bytes(back_got.at[side, pl.ds(0, sizes[side])], recv_sem.at[7 + side])
    sums = []
    for side in range(2):
        total = back_got[side, 0:half, :]
        for source in range(1, n_trial):
            total = total + back_got[side, source * TILE : source * TILE + half, :]
        sums.append(total[:, side * factors : (side + 1) * factors])
    load_out[0:half, :] = -pick(sums[0], sums[1])
    load_out[half:per_dev, :] = -pick(sums[1], sums[0])

    for number in range(5):
        others(number, sent, send_sem)
    wait_bytes(shares.at[pl.ds(0, n_trial - 1)], send_sem.at[5])
    wait_bytes(scales.at[pl.ds(0, n_trial - 1)], send_sem.at[9])
    wait_bytes(small_got.at[:, pl.ds(0, half)], send_sem.at[6])
    for side in range(2):
        wait_bytes(back_got.at[side, pl.ds(0, sizes[side])], send_sem.at[7 + side])
    swapped = (
        scores_ref.at[0],
        precision_ref.at[0],
        turned_mine.at[0],
        got.at[2],
        turned_mine.at[1, pl.ds(0, PANEL)],
        got.at[4],
    )
    for number, part in enumerate(swapped):
        wait_bytes(part, pair_send_sem.at[number])


def write_out(score_ref, load_ref, score_hbm, load_hbm, sem):
    copies = [
        pltpu.make_async_copy(load_ref, load_hbm, sem.at[0]),
        pltpu.make_async_copy(score_ref, score_hbm, sem.at[1]),
    ]
    for copy in copies:
        copy.start()
    for copy in copies:
        copy.wait()


def split_call(n_trial, rank_tile, operands):
    mean, corr, noise, row_limits, col_limits, listed, precision, loads, scores, slots, seen = (
        operands
    )
    per_dev, per_trial = listed.shape
    half = per_dev // 2
    rows = n_trial * rank_tile
    grid = slots.shape[1:]
    grid_size = grid[0] * grid[1]
    vmem = pl.BlockSpec(memory_space=pltpu.VMEM)
    hbm = pl.BlockSpec(memory_space=pltpu.HBM)
    whole = (mean, corr, noise, row_limits, col_limits, listed)
    results = pl.pallas_call(
        functools.partial(split_kernel, n_trial, rank_tile),
        out_shape=(
            jax.ShapeDtypeStruct(scores.shape, F32),
            jax.ShapeDtypeStruct(loads.shape, F32),
        ),
        in_specs=[hbm] * len(operands),
        out_specs=(vmem, vmem),
        scratch_shapes=[pltpu.VMEM(operand.shape, operand.dtype) for operand in whole]
        + [
            pltpu.VMEM((2,) + precision.shape, F32),
            pltpu.VMEM(loads.shape, F32),
            pltpu.VMEM((2,) + scores.shape, BF16),
            pltpu.VMEM((half,) + grid, jnp.int32),
            pltpu.VMEM((half,) + grid, F32),
            pltpu.VMEM((5, rows, PANEL), F32),
            pltpu.VMEM((5, rows, PANEL), F32),
            pltpu.VMEM((TILE, PANEL), F32),
            pltpu.VMEM((n_trial, TILE, PANEL), F32),
            pltpu.VMEM((n_trial * half, PANEL), jnp.int16),
            pltpu.VMEM((n_trial, n_trial * half, PANEL), jnp.int16),
            pltpu.VMEM((TILE, PANEL), F32),
            pltpu.VMEM((n_trial, PANEL), F32),
            pltpu.VMEM((n_trial * TILE, PANEL), F32),
            pltpu.VMEM((2, n_trial * TILE, PANEL), F32),
            pltpu.VMEM((2, PANEL + TILE, rows), F32),
            pltpu.VMEM((2, PANEL + TILE, rows), F32),
            pltpu.VMEM((2, rows, PANEL), F32),
            pltpu.VMEM((half, 2 * per_trial, grid_size), BF16),
            pltpu.VMEM((half, grid_size, PANEL), BF16),
            pltpu.VMEM((half, 8) + grid, F32),
            pltpu.VMEM((2,) + scores.shape, BF16),
            pltpu.SemaphoreType.DMA((len(operands),)),
            pltpu.SemaphoreType.DMA((10,)),
            pltpu.SemaphoreType.DMA((10,)),
            pltpu.SemaphoreType.DMA((6,)),
            pltpu.SemaphoreType.DMA((6,)),
        ],
        compiler_params=pltpu.CompilerParams(
            collective_id=0, has_side_effects=True, vmem_limit_bytes=48 * 1024 * 1024
        ),
    )(*operands)
    return pl.pallas_call(
        write_out,
        out_shape=tuple(jax.ShapeDtypeStruct(value.shape, value.dtype) for value in results),
        in_specs=[vmem, vmem],
        out_specs=(hbm, hbm),
        scratch_shapes=[pltpu.SemaphoreType.DMA((2,))],
        compiler_params=pltpu.CompilerParams(vmem_limit_bytes=4 * 1024 * 1024),
    )(*results)


def kernel(
    n_trial,
    n_factor,
    rank_tile,
    mean_hbm,
    corr_hbm,
    noise_hbm,
    rows_hbm,
    cols_hbm,
    list_hbm,
    precision_hbm,
    loads_hbm,
    scores_hbm,
    slot_hbm,
    observed_hbm,
    score_out,
    load_out,
    mean_ref,
    corr_ref,
    noise_ref,
    rows_ref,
    cols_ref,
    list_ref,
    precision_ref,
    loads_ref,
    scores_ref,
    slot_ref,
    observed_ref,
    sent,
    got,
    share,
    shares,
    scale,
    scales,
    fac_sent,
    fac_got,
    spread,
    cells,
    fresh,
    copy_sem,
    send_sem,
    recv_sem,
    fac_send_sem,
    fac_recv_sem,
):
    per_dev, grid_rows, grid_cols = observed_ref.shape
    factors = scores_ref.shape[0]
    owned = scores_ref.shape[1] // PANEL
    per_trial = list_ref.shape[1]
    required = per_dev * per_trial
    rows = n_trial * rank_tile
    trials = n_trial * per_dev
    me = lax.axis_index("trial")
    mine = lax.axis_index("factor")

    barrier = pltpu.get_barrier_semaphore()
    for step in range(1, n_trial):
        pl.semaphore_signal(
            barrier,
            inc=1,
            device_id={"trial": lax.rem(me + step, n_trial)},
            device_id_type=MESH,
        )
    for step in range(1, n_factor):
        pl.semaphore_signal(
            barrier,
            inc=1,
            device_id={"factor": lax.rem(mine + step, n_factor)},
            device_id_type=MESH,
        )

    pairs = (
        (list_hbm, list_ref),
        (loads_hbm, loads_ref),
        (slot_hbm, slot_ref),
        (scores_hbm, scores_ref),
        (observed_hbm, observed_ref),
        (precision_hbm, precision_ref),
        (mean_hbm, mean_ref),
        (corr_hbm, corr_ref),
        (noise_hbm, noise_ref),
        (rows_hbm, rows_ref),
        (cols_hbm, cols_ref),
    )
    copies = [
        pltpu.make_async_copy(source, target, copy_sem.at[index])
        for index, (source, target) in enumerate(pairs)
    ]
    for copy in copies:
        copy.start()

    def tile_at(index):
        return pl.ds(pl.multiple_of(index * rank_tile, rank_tile), rank_tile)

    def send(number):
        for step in sorted(range(1, n_trial), key=lambda at: -abs(2 * at - n_trial)):
            target = lax.rem(me + step, n_trial)
            pltpu.make_async_remote_copy(
                src_ref=sent.at[number, tile_at(target)],
                dst_ref=got.at[number, tile_at(me)],
                send_sem=send_sem.at[number],
                recv_sem=recv_sem.at[number],
                device_id={"trial": target},
                device_id_type=MESH,
            ).start()
        got[number, tile_at(me), :] = sent[number, tile_at(me), :]

    def others(number, ref, sem):
        part = ref.at[number, pl.ds(0, (n_trial - 1) * rank_tile)]
        return pltpu.make_async_copy(part, part, sem.at[number])

    def receive(number):
        others(number, got, recv_sem).wait()
        return got[number]

    def send_share():
        for step in range(1, n_trial):
            pltpu.make_async_remote_copy(
                src_ref=share,
                dst_ref=shares.at[me],
                send_sem=send_sem.at[6],
                recv_sem=recv_sem.at[6],
                device_id={"trial": lax.rem(me + step, n_trial)},
                device_id_type=MESH,
            ).start()
            pltpu.make_async_remote_copy(
                src_ref=scale.at[pl.ds(0, 1)],
                dst_ref=scales.at[pl.ds(me, 1)],
                send_sem=send_sem.at[7],
                recv_sem=recv_sem.at[7],
                device_id={"trial": lax.rem(me + step, n_trial)},
                device_id_type=MESH,
            ).start()
        shares[pl.ds(me, 1)] = share[...][None]
        scales[pl.ds(me, 1), :] = scale[0:1, :]

    def other_shares(sem):
        part = shares.at[pl.ds(0, n_trial - 1)]
        return pltpu.make_async_copy(part, part, sem.at[6])

    def other_scales(sem):
        part = scales.at[pl.ds(0, n_trial - 1)]
        return pltpu.make_async_copy(part, part, sem.at[7])

    def factor_sum(number, part):
        fac_sent[number] = part
        for step in range(1, n_factor):
            pltpu.make_async_remote_copy(
                src_ref=fac_sent.at[number],
                dst_ref=fac_got.at[number, mine],
                send_sem=fac_send_sem.at[number, step - 1],
                recv_sem=fac_recv_sem.at[number, step - 1],
                device_id={"factor": lax.rem(mine + step, n_factor)},
                device_id_type=MESH,
            ).start()
        fac_got[number, pl.ds(mine, 1)] = part[None]
        for step in range(1, n_factor):
            origin = lax.rem(mine + n_factor - step, n_factor)
            pltpu.make_async_copy(
                fac_sent.at[number], fac_got.at[number, origin], fac_recv_sem.at[number, step - 1]
            ).wait()
        total = fac_got[number, 0]
        for index in range(1, n_factor):
            total = total + fac_got[number, index]
        return total

    def column(line):
        size = line.shape[1]
        eye = lax.broadcasted_iota(jnp.int32, (size, size), 0) == lax.broadcasted_iota(
            jnp.int32, (size, size), 1
        )
        return jnp.sum(jnp.where(eye, line, 0.0), axis=1, keepdims=True)

    copies[0].wait()
    wanted = jnp.concatenate(
        [list_ref[trial : trial + 1, :] for trial in range(per_dev)], axis=1
    )
    owner = wanted // owned
    local = wanted - owner * owned
    owner_line = owner.astype(F32)
    before = lax.broadcasted_iota(jnp.int32, (required, required), 0)
    after = lax.broadcasted_iota(jnp.int32, (required, required), 1)
    earlier = (column(owner_line) == owner_line) & (before < after)
    rank = jnp.sum(jnp.where(earlier, 1.0, 0.0), axis=0, keepdims=True)
    place = owner_line * rank_tile + rank
    row_of = lax.broadcasted_iota(jnp.int32, (rows, required), 0).astype(F32)
    placed = place == row_of
    slot_trial = lax.broadcasted_iota(jnp.int32, (rows, required), 1) // per_trial
    trial_of = jnp.max(jnp.where(placed, slot_trial.astype(F32), -1.0), axis=1, keepdims=True)
    local_of = jnp.max(jnp.where(placed, local.astype(F32), -1.0), axis=1, keepdims=True)
    pack = jnp.where(placed, 1.0, 0.0)
    pack = jnp.concatenate([pack, pack], axis=1).astype(BF16)

    copies[1].wait()
    loads = loads_ref[...]
    load_rows = jnp.zeros((rows, factors), F32)
    for trial in range(per_dev):
        load_rows = jnp.where(trial_of == trial, loads[trial : trial + 1, :], load_rows)
    sent[0] = jnp.concatenate(
        [
            load_rows,
            jnp.broadcast_to(local_of, (rows, 8)),
            jnp.broadcast_to(trial_of, (rows, PANEL - factors - 8)),
        ],
        axis=1,
    )
    pl.semaphore_wait(barrier, n_trial - 1 + n_factor - 1)
    send(0)

    lane_rows = lax.broadcasted_iota(jnp.int32, (required, rows), 1).astype(F32)
    unpack = jnp.where(column(place) == lane_rows, 1.0, 0.0).astype(BF16)
    unpack = jnp.concatenate([unpack, unpack], axis=1)
    cell_iota = lax.broadcasted_iota(jnp.int32, (PANEL, grid_cols), 0)
    panel_iota = lax.broadcasted_iota(jnp.int32, (per_trial, grid_cols), 0)
    for copy in copies[2:]:
        copy.wait()
    precision = column(precision_ref[...])
    for trial in range(per_dev):
        cell = slot_ref[trial] & (PANEL - 1)
        for row in range(grid_rows):
            cells[trial, :, row * grid_cols : (row + 1) * grid_cols] = jnp.where(
                cell[row : row + 1, :] == cell_iota, 1.0, 0.0
            ).astype(BF16)

    row_index = lax.broadcasted_iota(jnp.int32, (grid_rows, grid_cols), 0)
    col_index = lax.broadcasted_iota(jnp.int32, (grid_rows, grid_cols), 1)

    def sweep(values, corr, position, limit, axis):
        length = values.shape[axis]
        scale = 1.0 / (1.0 - corr * corr)
        inner = jnp.where((position > 0) & (position < limit - 1), corr * corr, 0.0)
        lower = jnp.where(position == 0, 0.0, pltpu.roll(values, 1, axis))
        upper = jnp.where(position == length - 1, 0.0, pltpu.roll(values, length - 1, axis))
        result = scale * ((1.0 + inner) * values - corr * (lower + upper))
        return jnp.where(position < limit, result, 0.0)

    def over_grid(ref, row, lane):
        return jnp.broadcast_to(ref[row : row + 1, lane : lane + 1], (grid_rows, grid_cols))

    def plots(effect):
        totals = []
        for trial in range(per_dev):
            slot = slot_ref[trial]
            panel = slot // PANEL
            cell = slot & (PANEL - 1)
            fitted = jnp.zeros((grid_rows, grid_cols), F32)
            for index in range(per_trial):
                at = trial * per_trial + index
                line = jnp.broadcast_to(effect[at : at + 1, :], (grid_rows, PANEL))
                taken = jnp.take_along_axis(line, cell, axis=1)
                fitted = jnp.where(panel == index, taken, fitted)
            row_limit = over_grid(rows_ref, 0, trial)
            col_limit = over_grid(cols_ref, 0, trial)
            active = (row_index < row_limit) & (col_index < col_limit)
            residual = jnp.where(
                active, observed_ref[trial] - over_grid(mean_ref, 0, trial) - fitted, 0.0
            )
            across = sweep(residual, over_grid(corr_ref, 1, trial), col_index, col_limit, 1)
            weighted = sweep(across, over_grid(corr_ref, 0, trial), row_index, row_limit, 0)
            weighted = weighted / over_grid(noise_ref, 0, trial)
            high, low = halves(weighted)
            for row in range(grid_rows):
                match = panel[row : row + 1, :] == panel_iota
                where_to = slice(row * grid_cols, (row + 1) * grid_cols)
                spread[trial, 0:per_trial, where_to] = jnp.where(
                    match, high[row : row + 1, :], 0.0
                ).astype(BF16)
                spread[trial, per_trial : 2 * per_trial, where_to] = jnp.where(
                    match, low[row : row + 1, :], 0.0
                ).astype(BF16)
            both = dot_nt(spread[trial], cells[trial])
            totals.append(both[0:per_trial] + both[per_trial : 2 * per_trial])
        return jnp.concatenate(totals, axis=0)

    message = receive(0)
    first_loads = message[:, 0:factors]
    panel_of = message[:, factors : factors + 1]
    turned = message.T
    panel_lane = turned[factors : factors + 1, :]
    block_at = lax.broadcasted_iota(jnp.int32, (rows, 1), 0) // rank_tile * per_dev
    block_lane = lax.broadcasted_iota(jnp.int32, (1, rows), 1) // rank_tile * per_dev
    within = message[:, factors + 8 : factors + 9]
    within_lane = turned[factors + 8 : factors + 9, :]
    whose = jnp.where(within >= 0.0, within + block_at.astype(F32), -1.0)
    whose_lane = jnp.where(within_lane >= 0.0, within_lane + block_lane.astype(F32), -1.0)
    gather = whose == lax.broadcasted_iota(jnp.int32, (rows, trials), 1).astype(F32)
    gather = jnp.where(gather, 1.0, 0.0)
    gather = jnp.concatenate([gather, gather], axis=1).astype(BF16)
    collect = whose_lane == lax.broadcasted_iota(jnp.int32, (trials, rows), 0).astype(F32)
    collect = jnp.where(collect, 1.0, 0.0).astype(BF16)
    collect = jnp.concatenate([collect, collect], axis=1)

    def stacked(values):
        high, low = halves(values)
        return jnp.concatenate([high, low], axis=0).astype(BF16)

    def weigh(number, load_part, current_ref):
        load_high, load_low = halves(load_part)
        load_both = jnp.concatenate([load_high, load_low], axis=1).astype(BF16)
        effect = jnp.zeros((rows, PANEL), F32)
        for panel in range(owned):
            block = current_ref[:, panel * PANEL : (panel + 1) * PANEL]
            product = dot(load_both, jnp.concatenate([block, block], axis=0))
            effect = jnp.where(panel_of == panel, product, effect)
        sent[number] = effect
        send(number)
        table = dot(unpack, stacked(receive(number)))
        slot_weight = plots(factor_sum(0 if number == 1 else 1, table))
        sent[number + 1] = dot(pack, stacked(slot_weight))
        send(number + 1)
        return halves(receive(number + 1))

    def load_terms(high, low, current_ref):
        wide = jnp.concatenate([high, low], axis=1).astype(BF16)
        terms = jnp.zeros((rows, factors), F32)
        for panel in range(owned):
            block = current_ref[:, panel * PANEL : (panel + 1) * PANEL]
            product = dot_nt(wide, jnp.concatenate([block, block], axis=1))
            terms = jnp.where(panel_of == panel, product, terms)
        return terms

    def score_grads(high, low, load_lanes, current_ref):
        tall = jnp.concatenate([high, low, high], axis=0).astype(BF16)
        lane_high, lane_low = halves(load_lanes)
        for panel in range(owned):
            where_to = slice(panel * PANEL, (panel + 1) * PANEL)
            match = panel_lane == panel
            masked_high = jnp.where(match, lane_high, 0.0)
            masked_low = jnp.where(match, lane_low, 0.0)
            left = jnp.concatenate([masked_high, masked_high, masked_low], axis=1).astype(BF16)
            current = current_ref[:, where_to].astype(F32)
            yield where_to, current, precision * current - dot(left, tall)

    padding = jnp.zeros((rows, PANEL - factors), F32)
    high, low = weigh(1, first_loads, scores_ref)
    partial = dot(collect, stacked(load_terms(high, low, scores_ref)))
    groups = PANEL // factors
    depth = trials // groups
    packed = jnp.concatenate(
        [partial[index * depth : (index + 1) * depth] for index in range(groups)], axis=1
    )
    unit = jnp.max(jnp.abs(packed), axis=1, keepdims=True) * (1.0 / LEVELS) + 1e-30
    share[...] = jnp.floor(packed / unit + 0.5).astype(jnp.int32).astype(jnp.int16)
    square = jnp.concatenate(
        [jnp.broadcast_to(unit, (depth, PANEL)), jnp.zeros((PANEL - depth, PANEL), F32)], axis=0
    )
    scale[...] = square.T[0:TILE, :]
    send_share()
    for where_to, current, grad in score_grads(high, low, turned[0:factors, :], scores_ref):
        fresh[:, where_to] = (current - score_step * grad).astype(BF16)
    other_shares(recv_sem).wait()
    other_scales(recv_sem).wait()
    tall_scales = scales[...]
    if n_trial < PANEL:
        tall_scales = jnp.concatenate(
            [tall_scales, jnp.zeros((PANEL - n_trial, PANEL), F32)], axis=0
        )
    units = tall_scales.T[0:depth, :]
    summed = jnp.zeros((depth, PANEL), F32)
    for index in range(n_trial):
        whole = shares[index].astype(jnp.int32).astype(F32)
        summed = summed + whole * units[:, index : index + 1]
    gained = jnp.concatenate(
        [summed[:, index * factors : (index + 1) * factors] for index in range(groups)], axis=0
    )
    second_loads = first_loads + load_step * dot(gather, stacked(gained))
    high, low = weigh(3, second_loads, fresh)
    sent[5] = jnp.concatenate([load_terms(high, low, fresh), padding], axis=1)
    send(5)
    turned_loads = jnp.concatenate([second_loads, padding], axis=1).T[0:factors, :]
    for where_to, current, grad in score_grads(high, low, turned_loads, fresh):
        score_out[:, where_to] = grad
    back = receive(5)[:, 0:factors]
    for trial in range(per_dev):
        load_out[trial : trial + 1, :] = -jnp.sum(
            jnp.where(trial_of == trial, back, 0.0), axis=0, keepdims=True
        )

    for number in range(6):
        others(number, sent, send_sem).wait()
    other_shares(send_sem).wait()
    other_scales(send_sem).wait()
    for number in range(2):
        for step in range(1, n_factor):
            pltpu.make_async_copy(
                fac_sent.at[number], fac_sent.at[number], fac_send_sem.at[number, step - 1]
            ).wait()


def body(
    observed,
    trial_mean,
    correlations,
    noise_var,
    plot_slot,
    row_count,
    col_count,
    panel_list,
    scores,
    loadings,
    score_precision,
):
    n_trial = lax.axis_size("trial")
    n_factor = lax.axis_size("factor")
    per_dev, per_trial = panel_list.shape
    required = per_dev * per_trial
    most = 2 * required // n_trial
    rank_tile = -(-most // TILE) * TILE
    rows = n_trial * rank_tile
    factors = scores.shape[0]
    depth = n_trial * per_dev * factors // PANEL
    split = n_factor == 2 and per_dev % 2 == 0 and 2 * factors == PANEL
    grid_size = plot_slot.shape[1] * plot_slot.shape[2]
    operands = (
        trial_mean[None],
        correlations.T,
        noise_var[None],
        row_count[None],
        col_count[None],
        panel_list,
        score_precision[None],
        loadings,
        scores,
        plot_slot,
        observed,
    )
    operands = tuple(pltpu.with_memory_space_constraint(x, pltpu.HBM) for x in operands)
    vmem = pl.BlockSpec(memory_space=pltpu.VMEM)
    hbm = pl.BlockSpec(memory_space=pltpu.HBM)
    if split:
        return split_call(n_trial, rank_tile, operands)
    return pl.pallas_call(
        functools.partial(kernel, n_trial, n_factor, rank_tile),
        out_shape=(
            jax.ShapeDtypeStruct(scores.shape, F32),
            jax.ShapeDtypeStruct(loadings.shape, F32),
        ),
        in_specs=[hbm] * len(operands),
        out_specs=(vmem, vmem),
        scratch_shapes=[pltpu.VMEM(operand.shape, operand.dtype) for operand in operands]
        + [
            pltpu.VMEM((6, rows, PANEL), F32),
            pltpu.VMEM((6, rows, PANEL), F32),
            pltpu.VMEM((depth, PANEL), jnp.int16),
            pltpu.VMEM((n_trial, depth, PANEL), jnp.int16),
            pltpu.VMEM((TILE, PANEL), F32),
            pltpu.VMEM((n_trial, PANEL), F32),
            pltpu.VMEM((2, required, PANEL), F32),
            pltpu.VMEM((2, n_factor, required, PANEL), F32),
            pltpu.VMEM((per_dev, 2 * per_trial, grid_size), BF16),
            pltpu.VMEM((per_dev, PANEL, grid_size), BF16),
            pltpu.VMEM(scores.shape, BF16),
            pltpu.SemaphoreType.DMA((len(operands),)),
            pltpu.SemaphoreType.DMA((8,)),
            pltpu.SemaphoreType.DMA((8,)),
            pltpu.SemaphoreType.DMA((2, max(n_factor - 1, 1))),
            pltpu.SemaphoreType.DMA((2, max(n_factor - 1, 1))),
        ],
        compiler_params=pltpu.CompilerParams(
            collective_id=0, has_side_effects=True, vmem_limit_bytes=48 * 1024 * 1024
        ),
    )(*operands)


def solution(mesh):
    in_specs = (
        P("trial", None, None),
        P("trial"),
        P("trial", None),
        P("trial"),
        P("trial", None, None),
        P("trial"),
        P("trial"),
        P("trial", None),
        P("factor", "trial"),
        P("trial", "factor"),
        P("factor"),
    )
    out_specs = (P("factor", "trial"), P("trial", "factor"))
    return jax.shard_map(body, mesh=mesh, in_specs=in_specs, out_specs=out_specs, check_vma=False)
```

```python
import functools

import jax
import jax.numpy as jnp
from jax import lax
from jax.experimental import pallas as pl
from jax.experimental.pallas import tpu as pltpu
from jax.sharding import PartitionSpec as P

PANEL = 128
TILE = 8

score_step = 0.005
load_step = 0.02

MESH = pl.DeviceIdType.MESH
F32 = jnp.float32
BF16 = jnp.bfloat16
LEVELS = 32000.0


def halves(x):
    high = x.astype(BF16).astype(F32)
    return high, x - high


def dot(a, b):
    return lax.dot_general(a, b, (((1,), (0,)), ((), ())), preferred_element_type=F32)


def dot_nt(a, b):
    return lax.dot_general(a, b, (((1,), (1,)), ((), ())), preferred_element_type=F32)


def split_kernel(
    n_trial,
    rank_tile,
    mean_hbm,
    corr_hbm,
    noise_hbm,
    rows_hbm,
    cols_hbm,
    list_hbm,
    precision_hbm,
    loads_hbm,
    scores_hbm,
    slot_hbm,
    observed_hbm,
    score_out,
    load_out,
    mean_ref,
    corr_ref,
    noise_ref,
    rows_ref,
    cols_ref,
    list_ref,
    precision_ref,
    loads_ref,
    scores_ref,
    slot_ref,
    observed_ref,
    sent,
    got,
    first_effects,
    second_effects,
    small_sent,
    small_got,
    share,
    shares,
    scale,
    scales,
    back_sent,
    back_got,
    turned_mine,
    turned_other,
    weights_other,
    spread,
    cells,
    coef,
    fresh,
    place_line,
    places,
    copy_sem,
    send_sem,
    recv_sem,
    pair_send_sem,
    pair_recv_sem,
):
    per_dev, per_trial = list_ref.shape
    half, grid_rows, grid_cols = observed_ref.shape
    factors = loads_ref.shape[1]
    owned = scores_ref.shape[2] // PANEL
    required = half * per_trial
    rows = n_trial * rank_tile
    trials = n_trial * half
    me = lax.axis_index("trial")
    mine = lax.axis_index("factor")
    other = 1 - mine

    def flip(steps):
        target = me
        for bit in range(n_trial.bit_length() - 1):
            if steps >> bit & 1:
                target = target + (1 << bit) * (1 - 2 * lax.rem(lax.div(me, 1 << bit), 2))
        return target

    if n_trial & (n_trial - 1) == 0:
        order = sorted(
            range(1, n_trial), key=lambda at: -((at >> 2) + (at & 1) + (at >> 1 & 1))
        )
        targets = [flip(at) for at in order]
    else:
        order = sorted(range(1, n_trial), key=lambda at: -abs(2 * at - n_trial))
        targets = [lax.rem(me + at, n_trial) for at in order]

    barrier = pltpu.get_barrier_semaphore()
    for target in targets:
        for core in (mine, other):
            pl.semaphore_signal(
                barrier,
                inc=1,
                device_id={"trial": target, "factor": core},
                device_id_type=MESH,
            )
    pl.semaphore_signal(
        barrier, inc=1, device_id={"trial": me, "factor": other}, device_id_type=MESH
    )

    own_trials = pl.ds(mine * half, half)
    pairs = (
        (list_hbm, list_ref),
        (loads_hbm, loads_ref),
        (slot_hbm.at[own_trials], slot_ref),
        (scores_hbm, scores_ref.at[0]),
        (observed_hbm.at[own_trials], observed_ref),
        (precision_hbm, precision_ref.at[0]),
        (mean_hbm, mean_ref),
        (corr_hbm, corr_ref),
        (noise_hbm, noise_ref),
        (rows_hbm, rows_ref),
        (cols_hbm, cols_ref),
    )
    copies = [
        pltpu.make_async_copy(source, target, copy_sem.at[index])
        for index, (source, target) in enumerate(pairs)
    ]
    for copy in copies:
        copy.start()

    def remote(source, target, send, recv, trial, core):
        pltpu.make_async_remote_copy(
            src_ref=source,
            dst_ref=target,
            send_sem=send,
            recv_sem=recv,
            device_id={"trial": trial, "factor": core},
            device_id_type=MESH,
        ).start()

    def tile_at(index):
        return pl.ds(pl.multiple_of(index * rank_tile, rank_tile), rank_tile)

    def landing(number):
        return {1: first_effects, 3: second_effects}.get(number, got.at[number])

    def send_tile(number, target):
        remote(
            sent.at[number, tile_at(target)],
            landing(number).at[tile_at(me)],
            send_sem.at[number],
            recv_sem.at[number],
            target,
            mine,
        )

    def send(number):
        for target in targets:
            send_tile(number, target)
        landing(number)[tile_at(me), :] = sent[number, tile_at(me), :]

    def wait_bytes(part, sem):
        pltpu.make_async_copy(part, part, sem).wait()

    def others(number, sem):
        wait_bytes(landing(number).at[pl.ds(0, (n_trial - 1) * rank_tile)], sem.at[number])

    def receive(number):
        others(number, recv_sem)
        return landing(number)[...]

    def swap(number, source, target):
        remote(
            source, target, pair_send_sem.at[number], pair_recv_sem.at[number], me, other
        )

    def pick(first, second):
        return jnp.where(mine == 0, first, second)

    def column(line):
        size = line.shape[1]
        eye = lax.broadcasted_iota(jnp.int32, (size, size), 0) == lax.broadcasted_iota(
            jnp.int32, (size, size), 1
        )
        return jnp.sum(jnp.where(eye, line, 0.0), axis=1, keepdims=True)

    copies[0].wait()
    wanted = jnp.concatenate(
        [
            pick(list_ref[at : at + 1, :], list_ref[half + at : half + at + 1, :])
            for at in range(half)
        ],
        axis=1,
    )
    owner = wanted // owned
    local = wanted - owner * owned
    owner_line = owner.astype(F32)
    before = lax.broadcasted_iota(jnp.int32, (required, required), 0)
    after = lax.broadcasted_iota(jnp.int32, (required, required), 1)
    earlier = (column(owner_line) == owner_line) & (before < after)
    rank = jnp.sum(jnp.where(earlier, 1.0, 0.0), axis=0, keepdims=True)
    place = owner_line * rank_tile + rank
    row_of = lax.broadcasted_iota(jnp.int32, (rows, required), 0).astype(F32)
    placed = place == row_of
    slot_trial = lax.broadcasted_iota(jnp.int32, (rows, required), 1) // per_trial
    trial_of = jnp.max(jnp.where(placed, slot_trial.astype(F32), -1.0), axis=1, keepdims=True)
    local_of = jnp.max(jnp.where(placed, local.astype(F32), -1.0), axis=1, keepdims=True)

    copies[1].wait()
    loads = loads_ref[...]
    load_rows = jnp.zeros((rows, factors), F32)
    nothing = jnp.zeros((1, factors), F32)
    for at in range(half):
        low_line, high_line = loads[at : at + 1, :], loads[half + at : half + at + 1, :]
        load_rows = jnp.where(trial_of == at, pick(low_line, high_line), load_rows)
        small_sent[at : at + 1, :] = jnp.concatenate(
            [nothing, pick(high_line, low_line)], axis=1
        )
    sent[0] = jnp.concatenate(
        [
            load_rows,
            jnp.broadcast_to(local_of, (rows, 8)),
            jnp.broadcast_to(trial_of, (rows, PANEL - factors - 8)),
        ],
        axis=1,
    )
    pl.semaphore_wait(barrier, 2 * n_trial - 1)
    for target in targets + [me]:
        remote(
            small_sent.at[pl.ds(0, half)],
            small_got.at[me, pl.ds(0, half)],
            send_sem.at[6],
            recv_sem.at[6],
            target,
            other,
        )
        if target is not me:
            send_tile(0, target)
    landing(0)[tile_at(me), :] = sent[0, tile_at(me), :]
    copies[3].wait()
    swap(0, scores_ref.at[0], scores_ref.at[1])
    copies[5].wait()
    swap(1, precision_ref.at[0], precision_ref.at[1])

    pack = jnp.where(placed, 1.0, 0.0)
    pack = jnp.concatenate([pack, pack], axis=1).astype(BF16)
    place_line[...] = jnp.clip(place.astype(jnp.int32), 0, rows - 1)
    to_scalars = pltpu.make_async_copy(place_line, places, copy_sem.at[len(pairs)])
    to_scalars.start()
    to_scalars.wait()
    cell_iota = lax.broadcasted_iota(jnp.int32, (PANEL, grid_cols), 0)
    panel_iota = lax.broadcasted_iota(jnp.int32, (per_trial, grid_cols), 0)
    copies[2].wait()
    copies[4].wait()
    for copy in copies[6:]:
        copy.wait()
    for trial in range(half):
        cell = slot_ref[trial] & (PANEL - 1)
        for row in range(grid_rows):
            match = jnp.where(cell[row : row + 1, :] == cell_iota, 1.0, 0.0)
            cells[trial, row * grid_cols : (row + 1) * grid_cols, :] = match.T.astype(BF16)

    row_index = lax.broadcasted_iota(jnp.int32, (grid_rows, grid_cols), 0)
    col_index = lax.broadcasted_iota(jnp.int32, (grid_rows, grid_cols), 1)

    def over_grid(ref, row, trial):
        value = pick(
            ref[row : row + 1, trial : trial + 1],
            ref[row : row + 1, half + trial : half + trial + 1],
        )
        return jnp.broadcast_to(value, (grid_rows, grid_cols))

    def stencil(corr, position, limit, length, weight):
        scale = weight / (1.0 - corr * corr)
        inner = jnp.where((position > 0) & (position < limit - 1), corr * corr, 0.0)
        inside = position < limit
        middle = jnp.where(inside, scale * (1.0 + inner), 0.0)
        side = jnp.where(inside, scale * corr, 0.0)
        lower = jnp.where(position == 0, 0.0, side)
        upper = jnp.where(position == length - 1, 0.0, side)
        return middle, lower, upper

    for trial in range(half):
        row_limit = over_grid(rows_ref, 0, trial)
        col_limit = over_grid(cols_ref, 0, trial)
        active = (row_index < row_limit) & (col_index < col_limit)
        base = jnp.where(active, observed_ref[trial] - over_grid(mean_ref, 0, trial), 0.0)
        across = stencil(over_grid(corr_ref, 1, trial), col_index, col_limit, grid_cols, 1.0)
        down = stencil(
            over_grid(corr_ref, 0, trial),
            row_index,
            row_limit,
            grid_rows,
            1.0 / over_grid(noise_ref, 0, trial),
        )
        for index, value in enumerate(
            (jnp.where(active, 1.0, 0.0), base) + across + down
        ):
            coef[trial, index] = value

    def plots(number):
        others(number, recv_sem)
        totals = []
        for trial in range(half):
            slot = slot_ref[trial]
            panel = slot // PANEL
            cell = slot & (PANEL - 1)
            fitted = jnp.zeros((grid_rows, grid_cols), F32)
            for index in range(per_trial):
                at = trial * per_trial + index
                row = jnp.minimum(jnp.maximum(places[0, at], 0), rows - 1)
                line = landing(number)[pl.ds(row, 1), :]
                line = jnp.broadcast_to(line, (grid_rows, PANEL))
                taken = jnp.take_along_axis(line, cell, axis=1)
                fitted = jnp.where(panel == index, taken, fitted)
            residual = coef[trial, 1] - coef[trial, 0] * fitted
            across = (
                coef[trial, 2] * residual
                - coef[trial, 3] * pltpu.roll(residual, 1, 1)
                - coef[trial, 4] * pltpu.roll(residual, grid_cols - 1, 1)
            )
            weighted = (
                coef[trial, 5] * across
                - coef[trial, 6] * pltpu.roll(across, 1, 0)
                - coef[trial, 7] * pltpu.roll(across, grid_rows - 1, 0)
            )
            high, low = halves(weighted)
            for row in range(grid_rows):
                match = panel[row : row + 1, :] == panel_iota
                where_to = slice(row * grid_cols, (row + 1) * grid_cols)
                spread[trial, 0:per_trial, where_to] = jnp.where(
                    match, high[row : row + 1, :], 0.0
                ).astype(BF16)
                spread[trial, per_trial : 2 * per_trial, where_to] = jnp.where(
                    match, low[row : row + 1, :], 0.0
                ).astype(BF16)
            both = dot(spread[trial], cells[trial])
            totals.append(both[0:per_trial] + both[per_trial : 2 * per_trial])
        return jnp.concatenate(totals, axis=0)

    def stacked(values):
        high, low = halves(values)
        return jnp.concatenate([high, low], axis=0).astype(BF16)

    def side_by_side(high, low):
        return jnp.concatenate([high, low], axis=1).astype(BF16)

    def effects(load_part, panel_wide, current_ref):
        load_both = side_by_side(*halves(load_part))
        effect = jnp.zeros((rows, PANEL), F32)
        for panel in range(owned):
            where_to = slice(panel * PANEL, (panel + 1) * PANEL)
            block = jnp.concatenate(
                [current_ref[0, :, where_to], current_ref[1, :, where_to]], axis=0
            )
            product = dot(load_both, jnp.concatenate([block, block], axis=0))
            effect = jnp.where(panel_wide == panel, product, effect)
        return effect

    def load_terms(high, low, panel_wide, current_ref):
        wide = side_by_side(high, low)
        terms = jnp.zeros((rows, PANEL), F32)
        for panel in range(owned):
            where_to = slice(panel * PANEL, (panel + 1) * PANEL)
            block = jnp.concatenate(
                [current_ref[0, :, where_to], current_ref[1, :, where_to]], axis=0
            )
            product = dot_nt(wide, jnp.concatenate([block, block], axis=1))
            terms = jnp.where(panel_wide == panel, product, terms)
        return terms

    def masked(panels, load_lanes, panel):
        lane_high, lane_low = load_lanes
        match = panels == panel
        masked_high = jnp.where(match, lane_high, 0.0)
        return [masked_high, masked_high, jnp.where(match, lane_low, 0.0)]

    others(0, recv_sem)
    wait_bytes(small_got.at[:, pl.ds(0, half)], recv_sem.at[6])
    message = got[0]
    panel_of = message[:, factors : factors + 1]
    within = message[:, factors + 8 : factors + 9]
    panel_wide = jnp.broadcast_to(panel_of, (rows, PANEL))
    within_wide = jnp.broadcast_to(within, (rows, PANEL))
    first_loads = message
    lane = lax.broadcasted_iota(jnp.int32, (rows, PANEL), 1)
    for at in range(half):
        line = jnp.concatenate(
            [
                jnp.broadcast_to(small_got[source, at : at + 1, :], (rank_tile, PANEL))
                for source in range(n_trial)
            ],
            axis=0,
        )
        use = lane >= factors
        if at > 0:
            use = use & (within_wide == at)
        first_loads = jnp.where(use, line, first_loads)
    wait_bytes(scores_ref.at[1], pair_recv_sem.at[0])
    sent[1] = effects(first_loads, panel_wide, scores_ref)
    send(1)

    panel_lane = message.T[factors : factors + 1, :]
    turned = first_loads.T
    turned_mine[0, 0:PANEL, :] = turned
    turned_mine[0, PANEL : PANEL + TILE, :] = jnp.broadcast_to(panel_lane, (TILE, rows))
    swap(2, turned_mine.at[0], turned_other.at[0])
    block_at = lax.broadcasted_iota(jnp.int32, (rows, 1), 0) // rank_tile * half
    whose = jnp.where(within >= 0.0, within + block_at.astype(F32), -1.0)
    gather = whose == lax.broadcasted_iota(jnp.int32, (rows, trials), 1).astype(F32)
    gather = jnp.where(gather, 1.0, 0.0).astype(BF16)
    gather = jnp.concatenate([gather, gather], axis=1)
    within_lane = message.T[factors + 8 : factors + 9, :]
    source_lane = lax.broadcasted_iota(jnp.int32, (1, rows), 1) // rank_tile

    def collector(count, step):
        held = source_lane.astype(F32) * step + within_lane
        held = jnp.where(within_lane >= 0.0, held, -1.0)
        match = held == lax.broadcasted_iota(jnp.int32, (count, rows), 0).astype(F32)
        match = jnp.where(match, 1.0, 0.0).astype(BF16)
        return jnp.concatenate([match, match], axis=1)

    collect = collector(trials, half)
    collect_back = collector(n_trial * TILE, TILE)

    sent[2] = dot(pack, stacked(plots(1)))
    send(2)

    high, low = halves(receive(2))
    partial = dot(collect, stacked(load_terms(high, low, panel_wide, scores_ref)))
    unit = jnp.max(jnp.abs(partial), axis=0, keepdims=True) * (1.0 / LEVELS) + 1e-30
    scale[0:1, :] = unit
    for target in targets:
        remote(
            scale.at[pl.ds(0, 1)],
            scales.at[pl.ds(me, 1)],
            send_sem.at[9],
            recv_sem.at[9],
            target,
            mine,
        )
    share[...] = jnp.floor(partial * (1.0 / unit) + 0.5).astype(jnp.int32).astype(jnp.int16)
    for target in targets:
        remote(share, shares.at[me], send_sem.at[5], recv_sem.at[5], target, mine)
    swap(3, got.at[2], weights_other.at[0])
    shares[pl.ds(me, 1)] = share[...][None]
    scales[pl.ds(me, 1), :] = unit

    wait_bytes(precision_ref.at[1], pair_recv_sem.at[1])
    wait_bytes(turned_other.at[0], pair_recv_sem.at[2])
    wait_bytes(weights_other.at[0], pair_recv_sem.at[3])
    precision = [column(precision_ref[0]), column(precision_ref[1])]
    other_panels = turned_other[0, PANEL : PANEL + 1, :]

    def tall(high, low, number):
        high_other, low_other = halves(weights_other[number])
        return jnp.concatenate(
            [high, low, high, high_other, low_other, high_other], axis=0
        ).astype(BF16)

    stack = tall(high, low, 0)
    for part in range(2):
        lanes = halves(turned[part * factors : (part + 1) * factors, :])
        start = (1 - part) * factors
        lanes_other = halves(turned_other[0, start : start + factors, :])
        for panel in range(owned):
            where_to = slice(panel * PANEL, (panel + 1) * PANEL)
            left = masked(panel_lane, lanes, panel) + masked(other_panels, lanes_other, panel)
            left = jnp.concatenate(left, axis=1).astype(BF16)
            current = scores_ref[part, :, where_to].astype(F32)
            grad = precision[part] * current - dot(left, stack)
            fresh[part, :, where_to] = (current - score_step * grad).astype(BF16)

    wait_bytes(shares.at[pl.ds(0, n_trial - 1)], recv_sem.at[5])
    wait_bytes(scales.at[pl.ds(0, n_trial - 1)], recv_sem.at[9])
    summed = jnp.zeros((trials, PANEL), F32)
    for source in range(n_trial):
        whole = shares[source].astype(jnp.int32).astype(F32)
        summed = summed + whole * scales[source : source + 1, :]
    second_loads = first_loads + load_step * dot(gather, stacked(summed))
    sent[3] = effects(second_loads, panel_wide, fresh)
    send(3)
    turned = second_loads.T
    turned_mine[1, 0:PANEL, :] = turned
    swap(4, turned_mine.at[1, pl.ds(0, PANEL)], turned_other.at[1, pl.ds(0, PANEL)])

    sent[4] = dot(pack, stacked(plots(3)))
    send(4)

    high, low = halves(receive(4))
    back_sent[...] = dot(collect_back, stacked(load_terms(high, low, panel_wide, fresh)))

    def back_at(index):
        return pl.ds(pl.multiple_of(index * TILE, TILE), half)

    for target in targets:
        for side, core in enumerate((mine, other)):
            remote(
                back_sent.at[back_at(target)],
                back_got.at[side, back_at(me)],
                send_sem.at[7 + side],
                recv_sem.at[7 + side],
                target,
                core,
            )
    remote(
        back_sent.at[back_at(me)],
        back_got.at[1, back_at(me)],
        send_sem.at[8],
        recv_sem.at[8],
        me,
        other,
    )
    swap(5, got.at[4], weights_other.at[1])
    whole_tile = pl.ds(pl.multiple_of(me * TILE, TILE), TILE)
    back_got[0, whole_tile, :] = back_sent[whole_tile, :]

    wait_bytes(turned_other.at[1, pl.ds(0, PANEL)], pair_recv_sem.at[4])
    wait_bytes(weights_other.at[1], pair_recv_sem.at[5])
    stack = tall(high, low, 1)
    lanes = halves(turned[0:factors, :])
    lanes_other = halves(turned_other[1, factors : 2 * factors, :])
    for panel in range(owned):
        where_to = slice(panel * PANEL, (panel + 1) * PANEL)
        left = masked(panel_lane, lanes, panel) + masked(other_panels, lanes_other, panel)
        left = jnp.concatenate(left, axis=1).astype(BF16)
        current = fresh[0, :, where_to].astype(F32)
        score_out[:, where_to] = precision[0] * current - dot(left, stack)

    sizes = ((n_trial - 1) * half, n_trial * half)
    for side in range(2):
        wait_bytes(back_got.at[side, pl.ds(0, sizes[side])], recv_sem.at[7 + side])
    sums = []
    for side in range(2):
        total = back_got[side, 0:half, :]
        for source in range(1, n_trial):
            total = total + back_got[side, source * TILE : source * TILE + half, :]
        sums.append(total[:, side * factors : (side + 1) * factors])
    load_out[0:half, :] = -pick(sums[0], sums[1])
    load_out[half:per_dev, :] = -pick(sums[1], sums[0])

    for number in range(5):
        others(number, send_sem)
    wait_bytes(shares.at[pl.ds(0, n_trial - 1)], send_sem.at[5])
    wait_bytes(scales.at[pl.ds(0, n_trial - 1)], send_sem.at[9])
    wait_bytes(small_got.at[:, pl.ds(0, half)], send_sem.at[6])
    for side in range(2):
        wait_bytes(back_got.at[side, pl.ds(0, sizes[side])], send_sem.at[7 + side])
    swapped = (
        scores_ref.at[0],
        precision_ref.at[0],
        turned_mine.at[0],
        got.at[2],
        turned_mine.at[1, pl.ds(0, PANEL)],
        got.at[4],
    )
    for number, part in enumerate(swapped):
        wait_bytes(part, pair_send_sem.at[number])


def write_out(score_ref, load_ref, score_hbm, load_hbm, sem):
    copies = [
        pltpu.make_async_copy(load_ref, load_hbm, sem.at[0]),
        pltpu.make_async_copy(score_ref, score_hbm, sem.at[1]),
    ]
    for copy in copies:
        copy.start()
    for copy in copies:
        copy.wait()


def split_call(n_trial, rank_tile, operands):
    mean, corr, noise, row_limits, col_limits, listed, precision, loads, scores, slots, seen = (
        operands
    )
    per_dev, per_trial = listed.shape
    half = per_dev // 2
    rows = n_trial * rank_tile
    grid = slots.shape[1:]
    grid_size = grid[0] * grid[1]
    vmem = pl.BlockSpec(memory_space=pltpu.VMEM)
    hbm = pl.BlockSpec(memory_space=pltpu.HBM)
    whole = (mean, corr, noise, row_limits, col_limits, listed)
    results = pl.pallas_call(
        functools.partial(split_kernel, n_trial, rank_tile),
        out_shape=(
            jax.ShapeDtypeStruct(scores.shape, F32),
            jax.ShapeDtypeStruct(loads.shape, F32),
        ),
        in_specs=[hbm] * len(operands),
        out_specs=(vmem, vmem),
        scratch_shapes=[pltpu.VMEM(operand.shape, operand.dtype) for operand in whole]
        + [
            pltpu.VMEM((2,) + precision.shape, F32),
            pltpu.VMEM(loads.shape, F32),
            pltpu.VMEM((2,) + scores.shape, BF16),
            pltpu.VMEM((half,) + grid, jnp.int32),
            pltpu.VMEM((half,) + grid, F32),
            pltpu.VMEM((5, rows, PANEL), F32),
            pltpu.VMEM((5, rows, PANEL), F32),
            pltpu.VMEM((rows, PANEL), F32),
            pltpu.VMEM((rows, PANEL), F32),
            pltpu.VMEM((TILE, PANEL), F32),
            pltpu.VMEM((n_trial, TILE, PANEL), F32),
            pltpu.VMEM((n_trial * half, PANEL), jnp.int16),
            pltpu.VMEM((n_trial, n_trial * half, PANEL), jnp.int16),
            pltpu.VMEM((TILE, PANEL), F32),
            pltpu.VMEM((n_trial, PANEL), F32),
            pltpu.VMEM((n_trial * TILE, PANEL), F32),
            pltpu.VMEM((2, n_trial * TILE, PANEL), F32),
            pltpu.VMEM((2, PANEL + TILE, rows), F32),
            pltpu.VMEM((2, PANEL + TILE, rows), F32),
            pltpu.VMEM((2, rows, PANEL), F32),
            pltpu.VMEM((half, 2 * per_trial, grid_size), BF16),
            pltpu.VMEM((half, grid_size, PANEL), BF16),
            pltpu.VMEM((half, 8) + grid, F32),
            pltpu.VMEM((2,) + scores.shape, BF16),
            pltpu.VMEM((1, half * per_trial), jnp.int32),
            pltpu.SMEM((1, half * per_trial), jnp.int32),
            pltpu.SemaphoreType.DMA((len(operands) + 1,)),
            pltpu.SemaphoreType.DMA((10,)),
            pltpu.SemaphoreType.DMA((10,)),
            pltpu.SemaphoreType.DMA((6,)),
            pltpu.SemaphoreType.DMA((6,)),
        ],
        compiler_params=pltpu.CompilerParams(
            collective_id=0, has_side_effects=True, vmem_limit_bytes=48 * 1024 * 1024
        ),
    )(*operands)
    return pl.pallas_call(
        write_out,
        out_shape=tuple(jax.ShapeDtypeStruct(value.shape, value.dtype) for value in results),
        in_specs=[vmem, vmem],
        out_specs=(hbm, hbm),
        scratch_shapes=[pltpu.SemaphoreType.DMA((2,))],
        compiler_params=pltpu.CompilerParams(vmem_limit_bytes=4 * 1024 * 1024),
    )(*results)


def kernel(
    n_trial,
    n_factor,
    rank_tile,
    mean_hbm,
    corr_hbm,
    noise_hbm,
    rows_hbm,
    cols_hbm,
    list_hbm,
    precision_hbm,
    loads_hbm,
    scores_hbm,
    slot_hbm,
    observed_hbm,
    score_out,
    load_out,
    mean_ref,
    corr_ref,
    noise_ref,
    rows_ref,
    cols_ref,
    list_ref,
    precision_ref,
    loads_ref,
    scores_ref,
    slot_ref,
    observed_ref,
    sent,
    got,
    share,
    shares,
    scale,
    scales,
    fac_sent,
    fac_got,
    spread,
    cells,
    fresh,
    copy_sem,
    send_sem,
    recv_sem,
    fac_send_sem,
    fac_recv_sem,
):
    per_dev, grid_rows, grid_cols = observed_ref.shape
    factors = scores_ref.shape[0]
    owned = scores_ref.shape[1] // PANEL
    per_trial = list_ref.shape[1]
    required = per_dev * per_trial
    rows = n_trial * rank_tile
    trials = n_trial * per_dev
    me = lax.axis_index("trial")
    mine = lax.axis_index("factor")

    barrier = pltpu.get_barrier_semaphore()
    for step in range(1, n_trial):
        pl.semaphore_signal(
            barrier,
            inc=1,
            device_id={"trial": lax.rem(me + step, n_trial)},
            device_id_type=MESH,
        )
    for step in range(1, n_factor):
        pl.semaphore_signal(
            barrier,
            inc=1,
            device_id={"factor": lax.rem(mine + step, n_factor)},
            device_id_type=MESH,
        )

    pairs = (
        (list_hbm, list_ref),
        (loads_hbm, loads_ref),
        (slot_hbm, slot_ref),
        (scores_hbm, scores_ref),
        (observed_hbm, observed_ref),
        (precision_hbm, precision_ref),
        (mean_hbm, mean_ref),
        (corr_hbm, corr_ref),
        (noise_hbm, noise_ref),
        (rows_hbm, rows_ref),
        (cols_hbm, cols_ref),
    )
    copies = [
        pltpu.make_async_copy(source, target, copy_sem.at[index])
        for index, (source, target) in enumerate(pairs)
    ]
    for copy in copies:
        copy.start()

    def tile_at(index):
        return pl.ds(pl.multiple_of(index * rank_tile, rank_tile), rank_tile)

    def send(number):
        for step in sorted(range(1, n_trial), key=lambda at: -abs(2 * at - n_trial)):
            target = lax.rem(me + step, n_trial)
            pltpu.make_async_remote_copy(
                src_ref=sent.at[number, tile_at(target)],
                dst_ref=got.at[number, tile_at(me)],
                send_sem=send_sem.at[number],
                recv_sem=recv_sem.at[number],
                device_id={"trial": target},
                device_id_type=MESH,
            ).start()
        got[number, tile_at(me), :] = sent[number, tile_at(me), :]

    def others(number, ref, sem):
        part = ref.at[number, pl.ds(0, (n_trial - 1) * rank_tile)]
        return pltpu.make_async_copy(part, part, sem.at[number])

    def receive(number):
        others(number, got, recv_sem).wait()
        return got[number]

    def send_share():
        for step in range(1, n_trial):
            pltpu.make_async_remote_copy(
                src_ref=share,
                dst_ref=shares.at[me],
                send_sem=send_sem.at[6],
                recv_sem=recv_sem.at[6],
                device_id={"trial": lax.rem(me + step, n_trial)},
                device_id_type=MESH,
            ).start()
            pltpu.make_async_remote_copy(
                src_ref=scale.at[pl.ds(0, 1)],
                dst_ref=scales.at[pl.ds(me, 1)],
                send_sem=send_sem.at[7],
                recv_sem=recv_sem.at[7],
                device_id={"trial": lax.rem(me + step, n_trial)},
                device_id_type=MESH,
            ).start()
        shares[pl.ds(me, 1)] = share[...][None]
        scales[pl.ds(me, 1), :] = scale[0:1, :]

    def other_shares(sem):
        part = shares.at[pl.ds(0, n_trial - 1)]
        return pltpu.make_async_copy(part, part, sem.at[6])

    def other_scales(sem):
        part = scales.at[pl.ds(0, n_trial - 1)]
        return pltpu.make_async_copy(part, part, sem.at[7])

    def factor_sum(number, part):
        fac_sent[number] = part
        for step in range(1, n_factor):
            pltpu.make_async_remote_copy(
                src_ref=fac_sent.at[number],
                dst_ref=fac_got.at[number, mine],
                send_sem=fac_send_sem.at[number, step - 1],
                recv_sem=fac_recv_sem.at[number, step - 1],
                device_id={"factor": lax.rem(mine + step, n_factor)},
                device_id_type=MESH,
            ).start()
        fac_got[number, pl.ds(mine, 1)] = part[None]
        for step in range(1, n_factor):
            origin = lax.rem(mine + n_factor - step, n_factor)
            pltpu.make_async_copy(
                fac_sent.at[number], fac_got.at[number, origin], fac_recv_sem.at[number, step - 1]
            ).wait()
        total = fac_got[number, 0]
        for index in range(1, n_factor):
            total = total + fac_got[number, index]
        return total

    def column(line):
        size = line.shape[1]
        eye = lax.broadcasted_iota(jnp.int32, (size, size), 0) == lax.broadcasted_iota(
            jnp.int32, (size, size), 1
        )
        return jnp.sum(jnp.where(eye, line, 0.0), axis=1, keepdims=True)

    copies[0].wait()
    wanted = jnp.concatenate(
        [list_ref[trial : trial + 1, :] for trial in range(per_dev)], axis=1
    )
    owner = wanted // owned
    local = wanted - owner * owned
    owner_line = owner.astype(F32)
    before = lax.broadcasted_iota(jnp.int32, (required, required), 0)
    after = lax.broadcasted_iota(jnp.int32, (required, required), 1)
    earlier = (column(owner_line) == owner_line) & (before < after)
    rank = jnp.sum(jnp.where(earlier, 1.0, 0.0), axis=0, keepdims=True)
    place = owner_line * rank_tile + rank
    row_of = lax.broadcasted_iota(jnp.int32, (rows, required), 0).astype(F32)
    placed = place == row_of
    slot_trial = lax.broadcasted_iota(jnp.int32, (rows, required), 1) // per_trial
    trial_of = jnp.max(jnp.where(placed, slot_trial.astype(F32), -1.0), axis=1, keepdims=True)
    local_of = jnp.max(jnp.where(placed, local.astype(F32), -1.0), axis=1, keepdims=True)
    pack = jnp.where(placed, 1.0, 0.0)
    pack = jnp.concatenate([pack, pack], axis=1).astype(BF16)

    copies[1].wait()
    loads = loads_ref[...]
    load_rows = jnp.zeros((rows, factors), F32)
    for trial in range(per_dev):
        load_rows = jnp.where(trial_of == trial, loads[trial : trial + 1, :], load_rows)
    sent[0] = jnp.concatenate(
        [
            load_rows,
            jnp.broadcast_to(local_of, (rows, 8)),
            jnp.broadcast_to(trial_of, (rows, PANEL - factors - 8)),
        ],
        axis=1,
    )
    pl.semaphore_wait(barrier, n_trial - 1 + n_factor - 1)
    send(0)

    lane_rows = lax.broadcasted_iota(jnp.int32, (required, rows), 1).astype(F32)
    unpack = jnp.where(column(place) == lane_rows, 1.0, 0.0).astype(BF16)
    unpack = jnp.concatenate([unpack, unpack], axis=1)
    cell_iota = lax.broadcasted_iota(jnp.int32, (PANEL, grid_cols), 0)
    panel_iota = lax.broadcasted_iota(jnp.int32, (per_trial, grid_cols), 0)
    for copy in copies[2:]:
        copy.wait()
    precision = column(precision_ref[...])
    for trial in range(per_dev):
        cell = slot_ref[trial] & (PANEL - 1)
        for row in range(grid_rows):
            cells[trial, :, row * grid_cols : (row + 1) * grid_cols] = jnp.where(
                cell[row : row + 1, :] == cell_iota, 1.0, 0.0
            ).astype(BF16)

    row_index = lax.broadcasted_iota(jnp.int32, (grid_rows, grid_cols), 0)
    col_index = lax.broadcasted_iota(jnp.int32, (grid_rows, grid_cols), 1)

    def sweep(values, corr, position, limit, axis):
        length = values.shape[axis]
        scale = 1.0 / (1.0 - corr * corr)
        inner = jnp.where((position > 0) & (position < limit - 1), corr * corr, 0.0)
        lower = jnp.where(position == 0, 0.0, pltpu.roll(values, 1, axis))
        upper = jnp.where(position == length - 1, 0.0, pltpu.roll(values, length - 1, axis))
        result = scale * ((1.0 + inner) * values - corr * (lower + upper))
        return jnp.where(position < limit, result, 0.0)

    def over_grid(ref, row, lane):
        return jnp.broadcast_to(ref[row : row + 1, lane : lane + 1], (grid_rows, grid_cols))

    def plots(effect):
        totals = []
        for trial in range(per_dev):
            slot = slot_ref[trial]
            panel = slot // PANEL
            cell = slot & (PANEL - 1)
            fitted = jnp.zeros((grid_rows, grid_cols), F32)
            for index in range(per_trial):
                at = trial * per_trial + index
                line = jnp.broadcast_to(effect[at : at + 1, :], (grid_rows, PANEL))
                taken = jnp.take_along_axis(line, cell, axis=1)
                fitted = jnp.where(panel == index, taken, fitted)
            row_limit = over_grid(rows_ref, 0, trial)
            col_limit = over_grid(cols_ref, 0, trial)
            active = (row_index < row_limit) & (col_index < col_limit)
            residual = jnp.where(
                active, observed_ref[trial] - over_grid(mean_ref, 0, trial) - fitted, 0.0
            )
            across = sweep(residual, over_grid(corr_ref, 1, trial), col_index, col_limit, 1)
            weighted = sweep(across, over_grid(corr_ref, 0, trial), row_index, row_limit, 0)
            weighted = weighted / over_grid(noise_ref, 0, trial)
            high, low = halves(weighted)
            for row in range(grid_rows):
                match = panel[row : row + 1, :] == panel_iota
                where_to = slice(row * grid_cols, (row + 1) * grid_cols)
                spread[trial, 0:per_trial, where_to] = jnp.where(
                    match, high[row : row + 1, :], 0.0
                ).astype(BF16)
                spread[trial, per_trial : 2 * per_trial, where_to] = jnp.where(
                    match, low[row : row + 1, :], 0.0
                ).astype(BF16)
            both = dot_nt(spread[trial], cells[trial])
            totals.append(both[0:per_trial] + both[per_trial : 2 * per_trial])
        return jnp.concatenate(totals, axis=0)

    message = receive(0)
    first_loads = message[:, 0:factors]
    panel_of = message[:, factors : factors + 1]
    turned = message.T
    panel_lane = turned[factors : factors + 1, :]
    block_at = lax.broadcasted_iota(jnp.int32, (rows, 1), 0) // rank_tile * per_dev
    block_lane = lax.broadcasted_iota(jnp.int32, (1, rows), 1) // rank_tile * per_dev
    within = message[:, factors + 8 : factors + 9]
    within_lane = turned[factors + 8 : factors + 9, :]
    whose = jnp.where(within >= 0.0, within + block_at.astype(F32), -1.0)
    whose_lane = jnp.where(within_lane >= 0.0, within_lane + block_lane.astype(F32), -1.0)
    gather = whose == lax.broadcasted_iota(jnp.int32, (rows, trials), 1).astype(F32)
    gather = jnp.where(gather, 1.0, 0.0)
    gather = jnp.concatenate([gather, gather], axis=1).astype(BF16)
    collect = whose_lane == lax.broadcasted_iota(jnp.int32, (trials, rows), 0).astype(F32)
    collect = jnp.where(collect, 1.0, 0.0).astype(BF16)
    collect = jnp.concatenate([collect, collect], axis=1)

    def stacked(values):
        high, low = halves(values)
        return jnp.concatenate([high, low], axis=0).astype(BF16)

    def weigh(number, load_part, current_ref):
        load_high, load_low = halves(load_part)
        load_both = jnp.concatenate([load_high, load_low], axis=1).astype(BF16)
        effect = jnp.zeros((rows, PANEL), F32)
        for panel in range(owned):
            block = current_ref[:, panel * PANEL : (panel + 1) * PANEL]
            product = dot(load_both, jnp.concatenate([block, block], axis=0))
            effect = jnp.where(panel_of == panel, product, effect)
        sent[number] = effect
        send(number)
        table = dot(unpack, stacked(receive(number)))
        slot_weight = plots(factor_sum(0 if number == 1 else 1, table))
        sent[number + 1] = dot(pack, stacked(slot_weight))
        send(number + 1)
        return halves(receive(number + 1))

    def load_terms(high, low, current_ref):
        wide = jnp.concatenate([high, low], axis=1).astype(BF16)
        terms = jnp.zeros((rows, factors), F32)
        for panel in range(owned):
            block = current_ref[:, panel * PANEL : (panel + 1) * PANEL]
            product = dot_nt(wide, jnp.concatenate([block, block], axis=1))
            terms = jnp.where(panel_of == panel, product, terms)
        return terms

    def score_grads(high, low, load_lanes, current_ref):
        tall = jnp.concatenate([high, low, high], axis=0).astype(BF16)
        lane_high, lane_low = halves(load_lanes)
        for panel in range(owned):
            where_to = slice(panel * PANEL, (panel + 1) * PANEL)
            match = panel_lane == panel
            masked_high = jnp.where(match, lane_high, 0.0)
            masked_low = jnp.where(match, lane_low, 0.0)
            left = jnp.concatenate([masked_high, masked_high, masked_low], axis=1).astype(BF16)
            current = current_ref[:, where_to].astype(F32)
            yield where_to, current, precision * current - dot(left, tall)

    padding = jnp.zeros((rows, PANEL - factors), F32)
    high, low = weigh(1, first_loads, scores_ref)
    partial = dot(collect, stacked(load_terms(high, low, scores_ref)))
    groups = PANEL // factors
    depth = trials // groups
    packed = jnp.concatenate(
        [partial[index * depth : (index + 1) * depth] for index in range(groups)], axis=1
    )
    unit = jnp.max(jnp.abs(packed), axis=1, keepdims=True) * (1.0 / LEVELS) + 1e-30
    share[...] = jnp.floor(packed / unit + 0.5).astype(jnp.int32).astype(jnp.int16)
    square = jnp.concatenate(
        [jnp.broadcast_to(unit, (depth, PANEL)), jnp.zeros((PANEL - depth, PANEL), F32)], axis=0
    )
    scale[...] = square.T[0:TILE, :]
    send_share()
    for where_to, current, grad in score_grads(high, low, turned[0:factors, :], scores_ref):
        fresh[:, where_to] = (current - score_step * grad).astype(BF16)
    other_shares(recv_sem).wait()
    other_scales(recv_sem).wait()
    tall_scales = scales[...]
    if n_trial < PANEL:
        tall_scales = jnp.concatenate(
            [tall_scales, jnp.zeros((PANEL - n_trial, PANEL), F32)], axis=0
        )
    units = tall_scales.T[0:depth, :]
    summed = jnp.zeros((depth, PANEL), F32)
    for index in range(n_trial):
        whole = shares[index].astype(jnp.int32).astype(F32)
        summed = summed + whole * units[:, index : index + 1]
    gained = jnp.concatenate(
        [summed[:, index * factors : (index + 1) * factors] for index in range(groups)], axis=0
    )
    second_loads = first_loads + load_step * dot(gather, stacked(gained))
    high, low = weigh(3, second_loads, fresh)
    sent[5] = jnp.concatenate([load_terms(high, low, fresh), padding], axis=1)
    send(5)
    turned_loads = jnp.concatenate([second_loads, padding], axis=1).T[0:factors, :]
    for where_to, current, grad in score_grads(high, low, turned_loads, fresh):
        score_out[:, where_to] = grad
    back = receive(5)[:, 0:factors]
    for trial in range(per_dev):
        load_out[trial : trial + 1, :] = -jnp.sum(
            jnp.where(trial_of == trial, back, 0.0), axis=0, keepdims=True
        )

    for number in range(6):
        others(number, sent, send_sem).wait()
    other_shares(send_sem).wait()
    other_scales(send_sem).wait()
    for number in range(2):
        for step in range(1, n_factor):
            pltpu.make_async_copy(
                fac_sent.at[number], fac_sent.at[number], fac_send_sem.at[number, step - 1]
            ).wait()


def body(
    observed,
    trial_mean,
    correlations,
    noise_var,
    plot_slot,
    row_count,
    col_count,
    panel_list,
    scores,
    loadings,
    score_precision,
):
    n_trial = lax.axis_size("trial")
    n_factor = lax.axis_size("factor")
    per_dev, per_trial = panel_list.shape
    required = per_dev * per_trial
    most = 2 * required // n_trial
    rank_tile = -(-most // TILE) * TILE
    rows = n_trial * rank_tile
    factors = scores.shape[0]
    depth = n_trial * per_dev * factors // PANEL
    split = n_factor == 2 and per_dev % 2 == 0 and 2 * factors == PANEL
    grid_size = plot_slot.shape[1] * plot_slot.shape[2]
    operands = (
        trial_mean[None],
        correlations.T,
        noise_var[None],
        row_count[None],
        col_count[None],
        panel_list,
        score_precision[None],
        loadings,
        scores,
        plot_slot,
        observed,
    )
    operands = tuple(pltpu.with_memory_space_constraint(x, pltpu.HBM) for x in operands)
    vmem = pl.BlockSpec(memory_space=pltpu.VMEM)
    hbm = pl.BlockSpec(memory_space=pltpu.HBM)
    if split:
        return split_call(n_trial, rank_tile, operands)
    return pl.pallas_call(
        functools.partial(kernel, n_trial, n_factor, rank_tile),
        out_shape=(
            jax.ShapeDtypeStruct(scores.shape, F32),
            jax.ShapeDtypeStruct(loadings.shape, F32),
        ),
        in_specs=[hbm] * len(operands),
        out_specs=(vmem, vmem),
        scratch_shapes=[pltpu.VMEM(operand.shape, operand.dtype) for operand in operands]
        + [
            pltpu.VMEM((6, rows, PANEL), F32),
            pltpu.VMEM((6, rows, PANEL), F32),
            pltpu.VMEM((depth, PANEL), jnp.int16),
            pltpu.VMEM((n_trial, depth, PANEL), jnp.int16),
            pltpu.VMEM((TILE, PANEL), F32),
            pltpu.VMEM((n_trial, PANEL), F32),
            pltpu.VMEM((2, required, PANEL), F32),
            pltpu.VMEM((2, n_factor, required, PANEL), F32),
            pltpu.VMEM((per_dev, 2 * per_trial, grid_size), BF16),
            pltpu.VMEM((per_dev, PANEL, grid_size), BF16),
            pltpu.VMEM(scores.shape, BF16),
            pltpu.SemaphoreType.DMA((len(operands),)),
            pltpu.SemaphoreType.DMA((8,)),
            pltpu.SemaphoreType.DMA((8,)),
            pltpu.SemaphoreType.DMA((2, max(n_factor - 1, 1))),
            pltpu.SemaphoreType.DMA((2, max(n_factor - 1, 1))),
        ],
        compiler_params=pltpu.CompilerParams(
            collective_id=0, has_side_effects=True, vmem_limit_bytes=48 * 1024 * 1024
        ),
    )(*operands)


def solution(mesh):
    in_specs = (
        P("trial", None, None),
        P("trial"),
        P("trial", None),
        P("trial"),
        P("trial", None, None),
        P("trial"),
        P("trial"),
        P("trial", None),
        P("factor", "trial"),
        P("trial", "factor"),
        P("factor"),
    )
    out_specs = (P("factor", "trial"), P("trial", "factor"))
    return jax.shard_map(body, mesh=mesh, in_specs=in_specs, out_specs=out_specs, check_vma=False)
```

```python
import functools

import jax
import jax.numpy as jnp
from jax import lax
from jax.experimental import pallas as pl
from jax.experimental.pallas import tpu as pltpu
from jax.sharding import PartitionSpec as P

PANEL = 128
TILE = 8

score_step = 0.005
load_step = 0.02

MESH = pl.DeviceIdType.MESH
F32 = jnp.float32
BF16 = jnp.bfloat16
LEVELS = 32000.0


def halves(x):
    high = x.astype(BF16).astype(F32)
    return high, x - high


def dot(a, b):
    return lax.dot_general(a, b, (((1,), (0,)), ((), ())), preferred_element_type=F32)


def dot_nt(a, b):
    return lax.dot_general(a, b, (((1,), (1,)), ((), ())), preferred_element_type=F32)


LOG2_E = 1.4426950408889634


def split_kernel(
    n_trial,
    rank_tile,
    mean_hbm,
    corr_hbm,
    noise_hbm,
    rows_hbm,
    cols_hbm,
    list_hbm,
    precision_hbm,
    loads_hbm,
    scores_hbm,
    slot_hbm,
    observed_hbm,
    score_out,
    load_out,
    mean_ref,
    corr_ref,
    noise_ref,
    rows_ref,
    cols_ref,
    list_ref,
    precision_ref,
    loads_ref,
    scores_ref,
    slot_ref,
    observed_ref,
    sent,
    got,
    first_effects,
    second_effects,
    small_sent,
    small_got,
    share,
    shares,
    back_sent,
    back_got,
    turned_mine,
    turned_other,
    weights_other,
    spread,
    cells,
    coef,
    fresh,
    place_line,
    places,
    copy_sem,
    send_sem,
    recv_sem,
    pair_send_sem,
    pair_recv_sem,
):
    per_dev, per_trial = list_ref.shape
    half, grid_rows, grid_cols = observed_ref.shape
    factors = loads_ref.shape[1]
    owned = scores_ref.shape[2] // PANEL
    required = half * per_trial
    rows = n_trial * rank_tile
    trials = n_trial * half
    folded = trials // 2
    me = lax.axis_index("trial")
    mine = lax.axis_index("factor")
    other = 1 - mine

    def flip(steps):
        target = me
        for bit in range(n_trial.bit_length() - 1):
            if steps >> bit & 1:
                target = target + (1 << bit) * (1 - 2 * lax.rem(lax.div(me, 1 << bit), 2))
        return target

    if n_trial & (n_trial - 1) == 0:
        order = sorted(
            range(1, n_trial), key=lambda at: -((at >> 2) + (at & 1) + (at >> 1 & 1))
        )
        targets = [flip(at) for at in order]
    else:
        order = sorted(range(1, n_trial), key=lambda at: -abs(2 * at - n_trial))
        targets = [lax.rem(me + at, n_trial) for at in order]

    barrier = pltpu.get_barrier_semaphore()
    for target in targets:
        for core in (mine, other):
            pl.semaphore_signal(
                barrier,
                inc=1,
                device_id={"trial": target, "factor": core},
                device_id_type=MESH,
            )
    pl.semaphore_signal(
        barrier, inc=1, device_id={"trial": me, "factor": other}, device_id_type=MESH
    )

    own_trials = pl.ds(mine * half, half)
    pairs = (
        (list_hbm, list_ref),
        (loads_hbm, loads_ref),
        (slot_hbm.at[own_trials], slot_ref),
        (scores_hbm, scores_ref.at[0]),
        (observed_hbm.at[own_trials], observed_ref),
        (precision_hbm, precision_ref.at[0]),
        (mean_hbm, mean_ref),
        (corr_hbm, corr_ref),
        (noise_hbm, noise_ref),
        (rows_hbm, rows_ref),
        (cols_hbm, cols_ref),
    )
    copies = [
        pltpu.make_async_copy(source, target, copy_sem.at[index])
        for index, (source, target) in enumerate(pairs)
    ]
    for copy in copies:
        copy.start()

    def remote(source, target, send, recv, trial, core):
        pltpu.make_async_remote_copy(
            src_ref=source,
            dst_ref=target,
            send_sem=send,
            recv_sem=recv,
            device_id={"trial": trial, "factor": core},
            device_id_type=MESH,
        ).start()

    def tile_at(index):
        return pl.ds(pl.multiple_of(index * rank_tile, rank_tile), rank_tile)

    def landing(number):
        return {1: first_effects, 3: second_effects}.get(number, got.at[number])

    def send_tile(number, target):
        remote(
            sent.at[number, tile_at(target)],
            landing(number).at[tile_at(me)],
            send_sem.at[number],
            recv_sem.at[number],
            target,
            mine,
        )

    def send(number):
        for target in targets:
            send_tile(number, target)
        landing(number)[tile_at(me), :] = sent[number, tile_at(me), :]

    def wait_bytes(part, sem):
        pltpu.make_async_copy(part, part, sem).wait()

    def others(number, sem):
        wait_bytes(landing(number).at[pl.ds(0, (n_trial - 1) * rank_tile)], sem.at[number])

    def receive(number):
        others(number, recv_sem)
        return landing(number)[...]

    def swap(number, source, target):
        remote(
            source, target, pair_send_sem.at[number], pair_recv_sem.at[number], me, other
        )

    def pick(first, second):
        return jnp.where(mine == 0, first, second)

    def column(line):
        size = line.shape[1]
        eye = lax.broadcasted_iota(jnp.int32, (size, size), 0) == lax.broadcasted_iota(
            jnp.int32, (size, size), 1
        )
        return jnp.sum(jnp.where(eye, line, 0.0), axis=1, keepdims=True)

    copies[0].wait()
    wanted = jnp.concatenate(
        [
            pick(list_ref[at : at + 1, :], list_ref[half + at : half + at + 1, :])
            for at in range(half)
        ],
        axis=1,
    )
    owner = wanted // owned
    local = wanted - owner * owned
    owner_line = owner.astype(F32)
    before = lax.broadcasted_iota(jnp.int32, (required, required), 0)
    after = lax.broadcasted_iota(jnp.int32, (required, required), 1)
    earlier = (column(owner_line) == owner_line) & (before < after)
    rank = jnp.sum(jnp.where(earlier, 1.0, 0.0), axis=0, keepdims=True)
    place = owner_line * rank_tile + rank
    row_of = lax.broadcasted_iota(jnp.int32, (rows, required), 0).astype(F32)
    placed = place == row_of
    slot_trial = lax.broadcasted_iota(jnp.int32, (rows, required), 1) // per_trial
    trial_of = jnp.max(jnp.where(placed, slot_trial.astype(F32), -1.0), axis=1, keepdims=True)
    local_of = jnp.max(jnp.where(placed, local.astype(F32), -1.0), axis=1, keepdims=True)

    copies[1].wait()
    loads = loads_ref[...]
    load_rows = jnp.zeros((rows, factors), F32)
    nothing = jnp.zeros((1, factors), F32)
    for at in range(half):
        low_line, high_line = loads[at : at + 1, :], loads[half + at : half + at + 1, :]
        load_rows = jnp.where(trial_of == at, pick(low_line, high_line), load_rows)
        small_sent[at : at + 1, :] = jnp.concatenate(
            [nothing, pick(high_line, low_line)], axis=1
        )
    sent[0] = jnp.concatenate(
        [
            load_rows,
            jnp.broadcast_to(local_of, (rows, 8)),
            jnp.broadcast_to(trial_of, (rows, PANEL - factors - 8)),
        ],
        axis=1,
    )
    pl.semaphore_wait(barrier, 2 * n_trial - 1)
    for target in targets + [me]:
        remote(
            small_sent.at[pl.ds(0, half)],
            small_got.at[me, pl.ds(0, half)],
            send_sem.at[6],
            recv_sem.at[6],
            target,
            other,
        )
        if target is not me:
            send_tile(0, target)
    landing(0)[tile_at(me), :] = sent[0, tile_at(me), :]
    copies[3].wait()
    swap(0, scores_ref.at[0], scores_ref.at[1])
    copies[5].wait()
    swap(1, precision_ref.at[0], precision_ref.at[1])

    pack = jnp.where(placed, 1.0, 0.0)
    pack = jnp.concatenate(
        [
            pack[:, at * per_trial : (at + 1) * per_trial]
            for at in range(half)
            for _ in range(2)
        ],
        axis=1,
    )
    pack = jnp.concatenate([pack, pack], axis=1).astype(BF16)
    place_line[...] = jnp.clip(place.astype(jnp.int32), 0, rows - 1)
    to_scalars = pltpu.make_async_copy(place_line, places, copy_sem.at[len(pairs)])
    to_scalars.start()
    to_scalars.wait()
    cell_iota = lax.broadcasted_iota(jnp.int32, (PANEL, grid_cols), 0)
    panel_iota = lax.broadcasted_iota(jnp.int32, (per_trial, grid_cols), 0)
    copies[2].wait()
    copies[4].wait()
    for copy in copies[6:]:
        copy.wait()
    for trial in range(half):
        cell = slot_ref[trial] & (PANEL - 1)
        for row in range(grid_rows):
            match = jnp.where(cell[row : row + 1, :] == cell_iota, 1.0, 0.0)
            cells[trial, row * grid_cols : (row + 1) * grid_cols, :] = match.T.astype(BF16)

    row_index = lax.broadcasted_iota(jnp.int32, (grid_rows, grid_cols), 0)
    col_index = lax.broadcasted_iota(jnp.int32, (grid_rows, grid_cols), 1)

    def over_grid(ref, row, trial):
        value = pick(
            ref[row : row + 1, trial : trial + 1],
            ref[row : row + 1, half + trial : half + trial + 1],
        )
        return jnp.broadcast_to(value, (grid_rows, grid_cols))

    def stencil(corr, position, limit, length, weight):
        scale = weight / (1.0 - corr * corr)
        inner = jnp.where((position > 0) & (position < limit - 1), corr * corr, 0.0)
        inside = position < limit
        middle = jnp.where(inside, scale * (1.0 + inner), 0.0)
        side = jnp.where(inside, scale * corr, 0.0)
        lower = jnp.where(position == 0, 0.0, side)
        upper = jnp.where(position == length - 1, 0.0, side)
        return middle, lower, upper

    for trial in range(half):
        row_limit = over_grid(rows_ref, 0, trial)
        col_limit = over_grid(cols_ref, 0, trial)
        active = (row_index < row_limit) & (col_index < col_limit)
        base = jnp.where(active, observed_ref[trial] - over_grid(mean_ref, 0, trial), 0.0)
        across = stencil(over_grid(corr_ref, 1, trial), col_index, col_limit, grid_cols, 1.0)
        down = stencil(
            over_grid(corr_ref, 0, trial),
            row_index,
            row_limit,
            grid_rows,
            1.0 / over_grid(noise_ref, 0, trial),
        )
        for index, value in enumerate(
            (jnp.where(active, 1.0, 0.0), base) + across + down
        ):
            coef[trial, index] = value

    def plots(number):
        others(number, recv_sem)
        totals = []
        for trial in range(half):
            slot = slot_ref[trial]
            panel = slot // PANEL
            cell = slot & (PANEL - 1)
            fitted = jnp.zeros((grid_rows, grid_cols), F32)
            for index in range(per_trial):
                at = trial * per_trial + index
                row = jnp.minimum(jnp.maximum(places[0, at], 0), rows - 1)
                line = landing(number)[pl.ds(row, 1), :]
                line = jnp.broadcast_to(line, (grid_rows, PANEL))
                taken = jnp.take_along_axis(line, cell, axis=1)
                fitted = jnp.where(panel == index, taken, fitted)
            residual = coef[trial, 1] - coef[trial, 0] * fitted
            across = (
                coef[trial, 2] * residual
                - coef[trial, 3] * pltpu.roll(residual, 1, 1)
                - coef[trial, 4] * pltpu.roll(residual, grid_cols - 1, 1)
            )
            weighted = (
                coef[trial, 5] * across
                - coef[trial, 6] * pltpu.roll(across, 1, 0)
                - coef[trial, 7] * pltpu.roll(across, grid_rows - 1, 0)
            )
            high, low = halves(weighted)
            for row in range(grid_rows):
                match = panel[row : row + 1, :] == panel_iota
                where_to = slice(row * grid_cols, (row + 1) * grid_cols)
                spread[trial, 0:per_trial, where_to] = jnp.where(
                    match, high[row : row + 1, :], 0.0
                ).astype(BF16)
                spread[trial, per_trial : 2 * per_trial, where_to] = jnp.where(
                    match, low[row : row + 1, :], 0.0
                ).astype(BF16)
            both = dot(spread[trial], cells[trial])
            totals.append(both)
        return jnp.concatenate(totals, axis=0)

    def stacked(values):
        high, low = halves(values)
        return jnp.concatenate([high, low], axis=0).astype(BF16)

    def side_by_side(high, low):
        return jnp.concatenate([high, low], axis=1).astype(BF16)

    def effects(load_part, panel_wide, current_ref):
        load_both = side_by_side(*halves(load_part))
        effect = jnp.zeros((rows, PANEL), F32)
        for panel in range(owned):
            where_to = slice(panel * PANEL, (panel + 1) * PANEL)
            block = jnp.concatenate(
                [current_ref[0, :, where_to], current_ref[1, :, where_to]], axis=0
            )
            product = dot(load_both, jnp.concatenate([block, block], axis=0))
            effect = jnp.where(panel_wide == panel, product, effect)
        return effect

    def load_terms(high, low, panel_wide, current_ref):
        wide = side_by_side(high, low)
        terms = jnp.zeros((rows, PANEL), F32)
        for panel in range(owned):
            where_to = slice(panel * PANEL, (panel + 1) * PANEL)
            block = jnp.concatenate(
                [current_ref[0, :, where_to], current_ref[1, :, where_to]], axis=0
            )
            product = dot_nt(wide, jnp.concatenate([block, block], axis=1))
            terms = jnp.where(panel_wide == panel, product, terms)
        return terms

    def masked(panels, load_lanes, panel):
        lane_high, lane_low = load_lanes
        match = panels == panel
        masked_high = jnp.where(match, lane_high, 0.0)
        return [masked_high, masked_high, jnp.where(match, lane_low, 0.0)]

    others(0, recv_sem)
    wait_bytes(small_got.at[:, pl.ds(0, half)], recv_sem.at[6])
    message = got[0]
    panel_of = message[:, factors : factors + 1]
    within = message[:, factors + 8 : factors + 9]
    panel_wide = jnp.broadcast_to(panel_of, (rows, PANEL))
    within_wide = jnp.broadcast_to(within, (rows, PANEL))
    first_loads = message
    lane = lax.broadcasted_iota(jnp.int32, (rows, PANEL), 1)
    for at in range(half):
        line = jnp.concatenate(
            [
                jnp.broadcast_to(small_got[source, at : at + 1, :], (rank_tile, PANEL))
                for source in range(n_trial)
            ],
            axis=0,
        )
        use = lane >= factors
        if at > 0:
            use = use & (within_wide == at)
        first_loads = jnp.where(use, line, first_loads)
    wait_bytes(scores_ref.at[1], pair_recv_sem.at[0])
    sent[1] = effects(first_loads, panel_wide, scores_ref)
    send(1)

    panel_lane = message.T[factors : factors + 1, :]
    turned = first_loads.T
    turned_mine[0, 0:PANEL, :] = turned
    turned_mine[0, PANEL : PANEL + TILE, :] = jnp.broadcast_to(panel_lane, (TILE, rows))
    swap(2, turned_mine.at[0], turned_other.at[0])
    block_at = lax.broadcasted_iota(jnp.int32, (rows, 1), 0) // rank_tile * half
    whose = jnp.where(within >= 0.0, within + block_at.astype(F32), -1.0)
    gather = whose == lax.broadcasted_iota(jnp.int32, (rows, trials), 1).astype(F32)
    gather = jnp.where(gather, 1.0, 0.0).astype(BF16)
    gather = jnp.concatenate([gather, gather], axis=1)
    within_lane = message.T[factors + 8 : factors + 9, :]
    source_lane = lax.broadcasted_iota(jnp.int32, (1, rows), 1) // rank_tile

    def collector(count, step):
        held = source_lane.astype(F32) * step + within_lane
        held = jnp.where(within_lane >= 0.0, held, -1.0)
        match = held == lax.broadcasted_iota(jnp.int32, (count, rows), 0).astype(F32)
        match = jnp.where(match, 1.0, 0.0).astype(BF16)
        return jnp.concatenate([match, match], axis=1)

    collect = collector(trials, half)
    collect_back = collector(n_trial * TILE, TILE)

    sent[2] = dot(pack, stacked(plots(1)))
    send(2)

    high, low = halves(receive(2))
    partial = dot(collect, stacked(load_terms(high, low, panel_wide, scores_ref)))
    peak = jnp.max(jnp.abs(partial), axis=0, keepdims=True)
    power = jnp.ceil(jnp.log(peak * (1.0 / LEVELS) + 1e-30) * LOG2_E)
    steps = jnp.floor(partial * jnp.exp2(-power) + 0.5).astype(jnp.int32)
    share[0:folded, :] = lax.shift_left(steps[0:folded], 16) + steps[folded:trials]
    share[folded : folded + 1, :] = power.astype(jnp.int32)
    filled = pl.ds(0, folded + 1)
    for target in targets:
        remote(
            share.at[filled],
            shares.at[me, filled],
            send_sem.at[5],
            recv_sem.at[5],
            target,
            mine,
        )
    swap(3, got.at[2], weights_other.at[0])
    shares[pl.ds(me, 1), filled, :] = share[filled, :][None]

    wait_bytes(precision_ref.at[1], pair_recv_sem.at[1])
    wait_bytes(turned_other.at[0], pair_recv_sem.at[2])
    wait_bytes(weights_other.at[0], pair_recv_sem.at[3])
    precision = [column(precision_ref[0]), column(precision_ref[1])]
    other_panels = turned_other[0, PANEL : PANEL + 1, :]

    def tall(high, low, number):
        high_other, low_other = halves(weights_other[number])
        return jnp.concatenate(
            [high, low, high, high_other, low_other, high_other], axis=0
        ).astype(BF16)

    stack = tall(high, low, 0)
    for part in range(2):
        lanes = halves(turned[part * factors : (part + 1) * factors, :])
        start = (1 - part) * factors
        lanes_other = halves(turned_other[0, start : start + factors, :])
        for panel in range(owned):
            where_to = slice(panel * PANEL, (panel + 1) * PANEL)
            left = masked(panel_lane, lanes, panel) + masked(other_panels, lanes_other, panel)
            left = jnp.concatenate(left, axis=1).astype(BF16)
            current = scores_ref[part, :, where_to].astype(F32)
            grad = precision[part] * current - dot(left, stack)
            fresh[part, :, where_to] = (current - score_step * grad).astype(BF16)

    wait_bytes(shares.at[pl.ds(0, n_trial - 1), filled], recv_sem.at[5])
    upper = jnp.zeros((folded, PANEL), F32)
    lower = jnp.zeros((folded, PANEL), F32)
    for source in range(n_trial):
        both = shares[source, 0:folded, :]
        unit = jnp.exp2(shares[source, folded : folded + 1, :].astype(F32))
        second = lax.shift_right_arithmetic(lax.shift_left(both, 16), 16)
        first = lax.shift_right_arithmetic(both - second, 16)
        upper = upper + first.astype(F32) * unit
        lower = lower + second.astype(F32) * unit
    summed = jnp.concatenate([upper, lower], axis=0)
    second_loads = first_loads + load_step * dot(gather, stacked(summed))
    sent[3] = effects(second_loads, panel_wide, fresh)
    send(3)
    turned = second_loads.T
    turned_mine[1, 0:PANEL, :] = turned
    swap(4, turned_mine.at[1, pl.ds(0, PANEL)], turned_other.at[1, pl.ds(0, PANEL)])

    sent[4] = dot(pack, stacked(plots(3)))
    send(4)

    high, low = halves(receive(4))
    back_sent[...] = dot(collect_back, stacked(load_terms(high, low, panel_wide, fresh)))

    def back_at(index):
        return pl.ds(pl.multiple_of(index * TILE, TILE), half)

    for target in targets:
        for side, core in enumerate((mine, other)):
            remote(
                back_sent.at[back_at(target)],
                back_got.at[side, back_at(me)],
                send_sem.at[7 + side],
                recv_sem.at[7 + side],
                target,
                core,
            )
    remote(
        back_sent.at[back_at(me)],
        back_got.at[1, back_at(me)],
        send_sem.at[8],
        recv_sem.at[8],
        me,
        other,
    )
    swap(5, got.at[4], weights_other.at[1])
    whole_tile = pl.ds(pl.multiple_of(me * TILE, TILE), TILE)
    back_got[0, whole_tile, :] = back_sent[whole_tile, :]

    wait_bytes(turned_other.at[1, pl.ds(0, PANEL)], pair_recv_sem.at[4])
    wait_bytes(weights_other.at[1], pair_recv_sem.at[5])
    stack = tall(high, low, 1)
    lanes = halves(turned[0:factors, :])
    lanes_other = halves(turned_other[1, factors : 2 * factors, :])
    for panel in range(owned):
        where_to = slice(panel * PANEL, (panel + 1) * PANEL)
        left = masked(panel_lane, lanes, panel) + masked(other_panels, lanes_other, panel)
        left = jnp.concatenate(left, axis=1).astype(BF16)
        current = fresh[0, :, where_to].astype(F32)
        score_out[:, where_to] = precision[0] * current - dot(left, stack)

    sizes = ((n_trial - 1) * half, n_trial * half)
    for side in range(2):
        wait_bytes(back_got.at[side, pl.ds(0, sizes[side])], recv_sem.at[7 + side])
    sums = []
    for side in range(2):
        total = back_got[side, 0:half, :]
        for source in range(1, n_trial):
            total = total + back_got[side, source * TILE : source * TILE + half, :]
        sums.append(total[:, side * factors : (side + 1) * factors])
    load_out[0:half, :] = -pick(sums[0], sums[1])
    load_out[half:per_dev, :] = -pick(sums[1], sums[0])

    for number in range(5):
        others(number, send_sem)
    wait_bytes(shares.at[pl.ds(0, n_trial - 1), filled], send_sem.at[5])
    wait_bytes(small_got.at[:, pl.ds(0, half)], send_sem.at[6])
    for side in range(2):
        wait_bytes(back_got.at[side, pl.ds(0, sizes[side])], send_sem.at[7 + side])
    swapped = (
        scores_ref.at[0],
        precision_ref.at[0],
        turned_mine.at[0],
        got.at[2],
        turned_mine.at[1, pl.ds(0, PANEL)],
        got.at[4],
    )
    for number, part in enumerate(swapped):
        wait_bytes(part, pair_send_sem.at[number])


def write_out(score_ref, load_ref, score_hbm, load_hbm, sem):
    copies = [
        pltpu.make_async_copy(load_ref, load_hbm, sem.at[0]),
        pltpu.make_async_copy(score_ref, score_hbm, sem.at[1]),
    ]
    for copy in copies:
        copy.start()
    for copy in copies:
        copy.wait()


def split_call(n_trial, rank_tile, operands):
    mean, corr, noise, row_limits, col_limits, listed, precision, loads, scores, slots, seen = (
        operands
    )
    per_dev, per_trial = listed.shape
    half = per_dev // 2
    rows = n_trial * rank_tile
    grid = slots.shape[1:]
    grid_size = grid[0] * grid[1]
    share_rows = n_trial * half // 2 + TILE
    vmem = pl.BlockSpec(memory_space=pltpu.VMEM)
    hbm = pl.BlockSpec(memory_space=pltpu.HBM)
    whole = (mean, corr, noise, row_limits, col_limits, listed)
    results = pl.pallas_call(
        functools.partial(split_kernel, n_trial, rank_tile),
        out_shape=(
            jax.ShapeDtypeStruct(scores.shape, F32),
            jax.ShapeDtypeStruct(loads.shape, F32),
        ),
        in_specs=[hbm] * len(operands),
        out_specs=(vmem, vmem),
        scratch_shapes=[pltpu.VMEM(operand.shape, operand.dtype) for operand in whole]
        + [
            pltpu.VMEM((2,) + precision.shape, F32),
            pltpu.VMEM(loads.shape, F32),
            pltpu.VMEM((2,) + scores.shape, BF16),
            pltpu.VMEM((half,) + grid, jnp.int32),
            pltpu.VMEM((half,) + grid, F32),
            pltpu.VMEM((5, rows, PANEL), F32),
            pltpu.VMEM((5, rows, PANEL), F32),
            pltpu.VMEM((rows, PANEL), F32),
            pltpu.VMEM((rows, PANEL), F32),
            pltpu.VMEM((TILE, PANEL), F32),
            pltpu.VMEM((n_trial, TILE, PANEL), F32),
            pltpu.VMEM((share_rows, PANEL), jnp.int32),
            pltpu.VMEM((n_trial, share_rows, PANEL), jnp.int32),
            pltpu.VMEM((n_trial * TILE, PANEL), F32),
            pltpu.VMEM((2, n_trial * TILE, PANEL), F32),
            pltpu.VMEM((2, PANEL + TILE, rows), F32),
            pltpu.VMEM((2, PANEL + TILE, rows), F32),
            pltpu.VMEM((2, rows, PANEL), F32),
            pltpu.VMEM((half, 2 * per_trial, grid_size), BF16),
            pltpu.VMEM((half, grid_size, PANEL), BF16),
            pltpu.VMEM((half, 8) + grid, F32),
            pltpu.VMEM((2,) + scores.shape, BF16),
            pltpu.VMEM((1, half * per_trial), jnp.int32),
            pltpu.SMEM((1, half * per_trial), jnp.int32),
            pltpu.SemaphoreType.DMA((len(operands) + 1,)),
            pltpu.SemaphoreType.DMA((9,)),
            pltpu.SemaphoreType.DMA((9,)),
            pltpu.SemaphoreType.DMA((6,)),
            pltpu.SemaphoreType.DMA((6,)),
        ],
        compiler_params=pltpu.CompilerParams(
            collective_id=0, has_side_effects=True, vmem_limit_bytes=48 * 1024 * 1024
        ),
    )(*operands)
    return pl.pallas_call(
        write_out,
        out_shape=tuple(jax.ShapeDtypeStruct(value.shape, value.dtype) for value in results),
        in_specs=[vmem, vmem],
        out_specs=(hbm, hbm),
        scratch_shapes=[pltpu.SemaphoreType.DMA((2,))],
        compiler_params=pltpu.CompilerParams(vmem_limit_bytes=4 * 1024 * 1024),
    )(*results)


def kernel(
    n_trial,
    n_factor,
    rank_tile,
    mean_hbm,
    corr_hbm,
    noise_hbm,
    rows_hbm,
    cols_hbm,
    list_hbm,
    precision_hbm,
    loads_hbm,
    scores_hbm,
    slot_hbm,
    observed_hbm,
    score_out,
    load_out,
    mean_ref,
    corr_ref,
    noise_ref,
    rows_ref,
    cols_ref,
    list_ref,
    precision_ref,
    loads_ref,
    scores_ref,
    slot_ref,
    observed_ref,
    sent,
    got,
    share,
    shares,
    scale,
    scales,
    fac_sent,
    fac_got,
    spread,
    cells,
    fresh,
    copy_sem,
    send_sem,
    recv_sem,
    fac_send_sem,
    fac_recv_sem,
):
    per_dev, grid_rows, grid_cols = observed_ref.shape
    factors = scores_ref.shape[0]
    owned = scores_ref.shape[1] // PANEL
    per_trial = list_ref.shape[1]
    required = per_dev * per_trial
    rows = n_trial * rank_tile
    trials = n_trial * per_dev
    me = lax.axis_index("trial")
    mine = lax.axis_index("factor")

    barrier = pltpu.get_barrier_semaphore()
    for step in range(1, n_trial):
        pl.semaphore_signal(
            barrier,
            inc=1,
            device_id={"trial": lax.rem(me + step, n_trial)},
            device_id_type=MESH,
        )
    for step in range(1, n_factor):
        pl.semaphore_signal(
            barrier,
            inc=1,
            device_id={"factor": lax.rem(mine + step, n_factor)},
            device_id_type=MESH,
        )

    pairs = (
        (list_hbm, list_ref),
        (loads_hbm, loads_ref),
        (slot_hbm, slot_ref),
        (scores_hbm, scores_ref),
        (observed_hbm, observed_ref),
        (precision_hbm, precision_ref),
        (mean_hbm, mean_ref),
        (corr_hbm, corr_ref),
        (noise_hbm, noise_ref),
        (rows_hbm, rows_ref),
        (cols_hbm, cols_ref),
    )
    copies = [
        pltpu.make_async_copy(source, target, copy_sem.at[index])
        for index, (source, target) in enumerate(pairs)
    ]
    for copy in copies:
        copy.start()

    def tile_at(index):
        return pl.ds(pl.multiple_of(index * rank_tile, rank_tile), rank_tile)

    def send(number):
        for step in sorted(range(1, n_trial), key=lambda at: -abs(2 * at - n_trial)):
            target = lax.rem(me + step, n_trial)
            pltpu.make_async_remote_copy(
                src_ref=sent.at[number, tile_at(target)],
                dst_ref=got.at[number, tile_at(me)],
                send_sem=send_sem.at[number],
                recv_sem=recv_sem.at[number],
                device_id={"trial": target},
                device_id_type=MESH,
            ).start()
        got[number, tile_at(me), :] = sent[number, tile_at(me), :]

    def others(number, ref, sem):
        part = ref.at[number, pl.ds(0, (n_trial - 1) * rank_tile)]
        return pltpu.make_async_copy(part, part, sem.at[number])

    def receive(number):
        others(number, got, recv_sem).wait()
        return got[number]

    def send_share():
        for step in range(1, n_trial):
            pltpu.make_async_remote_copy(
                src_ref=share,
                dst_ref=shares.at[me],
                send_sem=send_sem.at[6],
                recv_sem=recv_sem.at[6],
                device_id={"trial": lax.rem(me + step, n_trial)},
                device_id_type=MESH,
            ).start()
            pltpu.make_async_remote_copy(
                src_ref=scale.at[pl.ds(0, 1)],
                dst_ref=scales.at[pl.ds(me, 1)],
                send_sem=send_sem.at[7],
                recv_sem=recv_sem.at[7],
                device_id={"trial": lax.rem(me + step, n_trial)},
                device_id_type=MESH,
            ).start()
        shares[pl.ds(me, 1)] = share[...][None]
        scales[pl.ds(me, 1), :] = scale[0:1, :]

    def other_shares(sem):
        part = shares.at[pl.ds(0, n_trial - 1)]
        return pltpu.make_async_copy(part, part, sem.at[6])

    def other_scales(sem):
        part = scales.at[pl.ds(0, n_trial - 1)]
        return pltpu.make_async_copy(part, part, sem.at[7])

    def factor_sum(number, part):
        fac_sent[number] = part
        for step in range(1, n_factor):
            pltpu.make_async_remote_copy(
                src_ref=fac_sent.at[number],
                dst_ref=fac_got.at[number, mine],
                send_sem=fac_send_sem.at[number, step - 1],
                recv_sem=fac_recv_sem.at[number, step - 1],
                device_id={"factor": lax.rem(mine + step, n_factor)},
                device_id_type=MESH,
            ).start()
        fac_got[number, pl.ds(mine, 1)] = part[None]
        for step in range(1, n_factor):
            origin = lax.rem(mine + n_factor - step, n_factor)
            pltpu.make_async_copy(
                fac_sent.at[number], fac_got.at[number, origin], fac_recv_sem.at[number, step - 1]
            ).wait()
        total = fac_got[number, 0]
        for index in range(1, n_factor):
            total = total + fac_got[number, index]
        return total

    def column(line):
        size = line.shape[1]
        eye = lax.broadcasted_iota(jnp.int32, (size, size), 0) == lax.broadcasted_iota(
            jnp.int32, (size, size), 1
        )
        return jnp.sum(jnp.where(eye, line, 0.0), axis=1, keepdims=True)

    copies[0].wait()
    wanted = jnp.concatenate(
        [list_ref[trial : trial + 1, :] for trial in range(per_dev)], axis=1
    )
    owner = wanted // owned
    local = wanted - owner * owned
    owner_line = owner.astype(F32)
    before = lax.broadcasted_iota(jnp.int32, (required, required), 0)
    after = lax.broadcasted_iota(jnp.int32, (required, required), 1)
    earlier = (column(owner_line) == owner_line) & (before < after)
    rank = jnp.sum(jnp.where(earlier, 1.0, 0.0), axis=0, keepdims=True)
    place = owner_line * rank_tile + rank
    row_of = lax.broadcasted_iota(jnp.int32, (rows, required), 0).astype(F32)
    placed = place == row_of
    slot_trial = lax.broadcasted_iota(jnp.int32, (rows, required), 1) // per_trial
    trial_of = jnp.max(jnp.where(placed, slot_trial.astype(F32), -1.0), axis=1, keepdims=True)
    local_of = jnp.max(jnp.where(placed, local.astype(F32), -1.0), axis=1, keepdims=True)
    pack = jnp.where(placed, 1.0, 0.0)
    pack = jnp.concatenate([pack, pack], axis=1).astype(BF16)

    copies[1].wait()
    loads = loads_ref[...]
    load_rows = jnp.zeros((rows, factors), F32)
    for trial in range(per_dev):
        load_rows = jnp.where(trial_of == trial, loads[trial : trial + 1, :], load_rows)
    sent[0] = jnp.concatenate(
        [
            load_rows,
            jnp.broadcast_to(local_of, (rows, 8)),
            jnp.broadcast_to(trial_of, (rows, PANEL - factors - 8)),
        ],
        axis=1,
    )
    pl.semaphore_wait(barrier, n_trial - 1 + n_factor - 1)
    send(0)

    lane_rows = lax.broadcasted_iota(jnp.int32, (required, rows), 1).astype(F32)
    unpack = jnp.where(column(place) == lane_rows, 1.0, 0.0).astype(BF16)
    unpack = jnp.concatenate([unpack, unpack], axis=1)
    cell_iota = lax.broadcasted_iota(jnp.int32, (PANEL, grid_cols), 0)
    panel_iota = lax.broadcasted_iota(jnp.int32, (per_trial, grid_cols), 0)
    for copy in copies[2:]:
        copy.wait()
    precision = column(precision_ref[...])
    for trial in range(per_dev):
        cell = slot_ref[trial] & (PANEL - 1)
        for row in range(grid_rows):
            cells[trial, :, row * grid_cols : (row + 1) * grid_cols] = jnp.where(
                cell[row : row + 1, :] == cell_iota, 1.0, 0.0
            ).astype(BF16)

    row_index = lax.broadcasted_iota(jnp.int32, (grid_rows, grid_cols), 0)
    col_index = lax.broadcasted_iota(jnp.int32, (grid_rows, grid_cols), 1)

    def sweep(values, corr, position, limit, axis):
        length = values.shape[axis]
        scale = 1.0 / (1.0 - corr * corr)
        inner = jnp.where((position > 0) & (position < limit - 1), corr * corr, 0.0)
        lower = jnp.where(position == 0, 0.0, pltpu.roll(values, 1, axis))
        upper = jnp.where(position == length - 1, 0.0, pltpu.roll(values, length - 1, axis))
        result = scale * ((1.0 + inner) * values - corr * (lower + upper))
        return jnp.where(position < limit, result, 0.0)

    def over_grid(ref, row, lane):
        return jnp.broadcast_to(ref[row : row + 1, lane : lane + 1], (grid_rows, grid_cols))

    def plots(effect):
        totals = []
        for trial in range(per_dev):
            slot = slot_ref[trial]
            panel = slot // PANEL
            cell = slot & (PANEL - 1)
            fitted = jnp.zeros((grid_rows, grid_cols), F32)
            for index in range(per_trial):
                at = trial * per_trial + index
                line = jnp.broadcast_to(effect[at : at + 1, :], (grid_rows, PANEL))
                taken = jnp.take_along_axis(line, cell, axis=1)
                fitted = jnp.where(panel == index, taken, fitted)
            row_limit = over_grid(rows_ref, 0, trial)
            col_limit = over_grid(cols_ref, 0, trial)
            active = (row_index < row_limit) & (col_index < col_limit)
            residual = jnp.where(
                active, observed_ref[trial] - over_grid(mean_ref, 0, trial) - fitted, 0.0
            )
            across = sweep(residual, over_grid(corr_ref, 1, trial), col_index, col_limit, 1)
            weighted = sweep(across, over_grid(corr_ref, 0, trial), row_index, row_limit, 0)
            weighted = weighted / over_grid(noise_ref, 0, trial)
            high, low = halves(weighted)
            for row in range(grid_rows):
                match = panel[row : row + 1, :] == panel_iota
                where_to = slice(row * grid_cols, (row + 1) * grid_cols)
                spread[trial, 0:per_trial, where_to] = jnp.where(
                    match, high[row : row + 1, :], 0.0
                ).astype(BF16)
                spread[trial, per_trial : 2 * per_trial, where_to] = jnp.where(
                    match, low[row : row + 1, :], 0.0
                ).astype(BF16)
            both = dot_nt(spread[trial], cells[trial])
            totals.append(both[0:per_trial] + both[per_trial : 2 * per_trial])
        return jnp.concatenate(totals, axis=0)

    message = receive(0)
    first_loads = message[:, 0:factors]
    panel_of = message[:, factors : factors + 1]
    turned = message.T
    panel_lane = turned[factors : factors + 1, :]
    block_at = lax.broadcasted_iota(jnp.int32, (rows, 1), 0) // rank_tile * per_dev
    block_lane = lax.broadcasted_iota(jnp.int32, (1, rows), 1) // rank_tile * per_dev
    within = message[:, factors + 8 : factors + 9]
    within_lane = turned[factors + 8 : factors + 9, :]
    whose = jnp.where(within >= 0.0, within + block_at.astype(F32), -1.0)
    whose_lane = jnp.where(within_lane >= 0.0, within_lane + block_lane.astype(F32), -1.0)
    gather = whose == lax.broadcasted_iota(jnp.int32, (rows, trials), 1).astype(F32)
    gather = jnp.where(gather, 1.0, 0.0)
    gather = jnp.concatenate([gather, gather], axis=1).astype(BF16)
    collect = whose_lane == lax.broadcasted_iota(jnp.int32, (trials, rows), 0).astype(F32)
    collect = jnp.where(collect, 1.0, 0.0).astype(BF16)
    collect = jnp.concatenate([collect, collect], axis=1)

    def stacked(values):
        high, low = halves(values)
        return jnp.concatenate([high, low], axis=0).astype(BF16)

    def weigh(number, load_part, current_ref):
        load_high, load_low = halves(load_part)
        load_both = jnp.concatenate([load_high, load_low], axis=1).astype(BF16)
        effect = jnp.zeros((rows, PANEL), F32)
        for panel in range(owned):
            block = current_ref[:, panel * PANEL : (panel + 1) * PANEL]
            product = dot(load_both, jnp.concatenate([block, block], axis=0))
            effect = jnp.where(panel_of == panel, product, effect)
        sent[number] = effect
        send(number)
        table = dot(unpack, stacked(receive(number)))
        slot_weight = plots(factor_sum(0 if number == 1 else 1, table))
        sent[number + 1] = dot(pack, stacked(slot_weight))
        send(number + 1)
        return halves(receive(number + 1))

    def load_terms(high, low, current_ref):
        wide = jnp.concatenate([high, low], axis=1).astype(BF16)
        terms = jnp.zeros((rows, factors), F32)
        for panel in range(owned):
            block = current_ref[:, panel * PANEL : (panel + 1) * PANEL]
            product = dot_nt(wide, jnp.concatenate([block, block], axis=1))
            terms = jnp.where(panel_of == panel, product, terms)
        return terms

    def score_grads(high, low, load_lanes, current_ref):
        tall = jnp.concatenate([high, low, high], axis=0).astype(BF16)
        lane_high, lane_low = halves(load_lanes)
        for panel in range(owned):
            where_to = slice(panel * PANEL, (panel + 1) * PANEL)
            match = panel_lane == panel
            masked_high = jnp.where(match, lane_high, 0.0)
            masked_low = jnp.where(match, lane_low, 0.0)
            left = jnp.concatenate([masked_high, masked_high, masked_low], axis=1).astype(BF16)
            current = current_ref[:, where_to].astype(F32)
            yield where_to, current, precision * current - dot(left, tall)

    padding = jnp.zeros((rows, PANEL - factors), F32)
    high, low = weigh(1, first_loads, scores_ref)
    partial = dot(collect, stacked(load_terms(high, low, scores_ref)))
    groups = PANEL // factors
    depth = trials // groups
    packed = jnp.concatenate(
        [partial[index * depth : (index + 1) * depth] for index in range(groups)], axis=1
    )
    unit = jnp.max(jnp.abs(packed), axis=1, keepdims=True) * (1.0 / LEVELS) + 1e-30
    share[...] = jnp.floor(packed / unit + 0.5).astype(jnp.int32).astype(jnp.int16)
    square = jnp.concatenate(
        [jnp.broadcast_to(unit, (depth, PANEL)), jnp.zeros((PANEL - depth, PANEL), F32)], axis=0
    )
    scale[...] = square.T[0:TILE, :]
    send_share()
    for where_to, current, grad in score_grads(high, low, turned[0:factors, :], scores_ref):
        fresh[:, where_to] = (current - score_step * grad).astype(BF16)
    other_shares(recv_sem).wait()
    other_scales(recv_sem).wait()
    tall_scales = scales[...]
    if n_trial < PANEL:
        tall_scales = jnp.concatenate(
            [tall_scales, jnp.zeros((PANEL - n_trial, PANEL), F32)], axis=0
        )
    units = tall_scales.T[0:depth, :]
    summed = jnp.zeros((depth, PANEL), F32)
    for index in range(n_trial):
        whole = shares[index].astype(jnp.int32).astype(F32)
        summed = summed + whole * units[:, index : index + 1]
    gained = jnp.concatenate(
        [summed[:, index * factors : (index + 1) * factors] for index in range(groups)], axis=0
    )
    second_loads = first_loads + load_step * dot(gather, stacked(gained))
    high, low = weigh(3, second_loads, fresh)
    sent[5] = jnp.concatenate([load_terms(high, low, fresh), padding], axis=1)
    send(5)
    turned_loads = jnp.concatenate([second_loads, padding], axis=1).T[0:factors, :]
    for where_to, current, grad in score_grads(high, low, turned_loads, fresh):
        score_out[:, where_to] = grad
    back = receive(5)[:, 0:factors]
    for trial in range(per_dev):
        load_out[trial : trial + 1, :] = -jnp.sum(
            jnp.where(trial_of == trial, back, 0.0), axis=0, keepdims=True
        )

    for number in range(6):
        others(number, sent, send_sem).wait()
    other_shares(send_sem).wait()
    other_scales(send_sem).wait()
    for number in range(2):
        for step in range(1, n_factor):
            pltpu.make_async_copy(
                fac_sent.at[number], fac_sent.at[number], fac_send_sem.at[number, step - 1]
            ).wait()


def body(
    observed,
    trial_mean,
    correlations,
    noise_var,
    plot_slot,
    row_count,
    col_count,
    panel_list,
    scores,
    loadings,
    score_precision,
):
    n_trial = lax.axis_size("trial")
    n_factor = lax.axis_size("factor")
    per_dev, per_trial = panel_list.shape
    required = per_dev * per_trial
    most = 2 * required // n_trial
    rank_tile = -(-most // TILE) * TILE
    rows = n_trial * rank_tile
    factors = scores.shape[0]
    depth = n_trial * per_dev * factors // PANEL
    split = n_factor == 2 and per_dev % 2 == 0 and 2 * factors == PANEL
    split = split and n_trial * per_dev % 32 == 0
    grid_size = plot_slot.shape[1] * plot_slot.shape[2]
    operands = (
        trial_mean[None],
        correlations.T,
        noise_var[None],
        row_count[None],
        col_count[None],
        panel_list,
        score_precision[None],
        loadings,
        scores,
        plot_slot,
        observed,
    )
    operands = tuple(pltpu.with_memory_space_constraint(x, pltpu.HBM) for x in operands)
    vmem = pl.BlockSpec(memory_space=pltpu.VMEM)
    hbm = pl.BlockSpec(memory_space=pltpu.HBM)
    if split:
        return split_call(n_trial, rank_tile, operands)
    return pl.pallas_call(
        functools.partial(kernel, n_trial, n_factor, rank_tile),
        out_shape=(
            jax.ShapeDtypeStruct(scores.shape, F32),
            jax.ShapeDtypeStruct(loadings.shape, F32),
        ),
        in_specs=[hbm] * len(operands),
        out_specs=(vmem, vmem),
        scratch_shapes=[pltpu.VMEM(operand.shape, operand.dtype) for operand in operands]
        + [
            pltpu.VMEM((6, rows, PANEL), F32),
            pltpu.VMEM((6, rows, PANEL), F32),
            pltpu.VMEM((depth, PANEL), jnp.int16),
            pltpu.VMEM((n_trial, depth, PANEL), jnp.int16),
            pltpu.VMEM((TILE, PANEL), F32),
            pltpu.VMEM((n_trial, PANEL), F32),
            pltpu.VMEM((2, required, PANEL), F32),
            pltpu.VMEM((2, n_factor, required, PANEL), F32),
            pltpu.VMEM((per_dev, 2 * per_trial, grid_size), BF16),
            pltpu.VMEM((per_dev, PANEL, grid_size), BF16),
            pltpu.VMEM(scores.shape, BF16),
            pltpu.SemaphoreType.DMA((len(operands),)),
            pltpu.SemaphoreType.DMA((8,)),
            pltpu.SemaphoreType.DMA((8,)),
            pltpu.SemaphoreType.DMA((2, max(n_factor - 1, 1))),
            pltpu.SemaphoreType.DMA((2, max(n_factor - 1, 1))),
        ],
        compiler_params=pltpu.CompilerParams(
            collective_id=0, has_side_effects=True, vmem_limit_bytes=48 * 1024 * 1024
        ),
    )(*operands)


def solution(mesh):
    in_specs = (
        P("trial", None, None),
        P("trial"),
        P("trial", None),
        P("trial"),
        P("trial", None, None),
        P("trial"),
        P("trial"),
        P("trial", None),
        P("factor", "trial"),
        P("trial", "factor"),
        P("factor"),
    )
    out_specs = (P("factor", "trial"), P("trial", "factor"))
    return jax.shard_map(body, mesh=mesh, in_specs=in_specs, out_specs=out_specs, check_vma=False)
```
